32 devices in a mesh: grp: 2 (over x), lon: 16 (over z, y, core).
Axes of the slice: x: 2, y: 2, z: 4, core: 2. Of those that a mesh axis runs over, the one named last changes fastest.
Arguments:
- state: bfloat16 [256, 256, 300], P(None, ('grp', 'lon')), parts along dimension 1, may hold values from -6 to 6
- ocean_mask: int32 [256, 128], P(None, 'lon'), may hold values from 0 to 1, as said below
- fold_map: int32 [128], replicated, may hold values from 0 to 127, as said below
- w_first: bfloat16 [3, 3, 300, 256], replicated, may hold values from -0.125 to 0.125
- b_first: float32 [256], replicated, may hold values from -3 to 3
- w_second: bfloat16 [3, 3, 256, 256], replicated, may hold values from -0.125 to 0.125
- b_second: float32 [256], replicated, may hold values from -3 to 3
Outputs:
- features: bfloat16 [256, 256, 256], P(None, ('grp', 'lon')), parts along dimension 1
The draws below stay inside these ranges and needn't reach their ends.
There are 2 independent parts, one for each index of `grp`. The reference program is written for one: setup_inputs(seed, part) draws one part's arguments, and reference() takes and returns one part's arrays. A program takes and returns all parts, laid end to end along the dimension named above; an argument that names none is the same for every part. Nothing has to cross between parts.
Inputs may be any that keep to these rules, and one draw needn't show every extreme that they name: `ocean_mask`: 1 marks ocean, 0 land; the ocean share varies from column to column. A reflection: (fold_map[i] + i) mod 128 is the same for every i.
All inputs are finite; a program needn't handle non-finite values.
Results may differ from the reference program's by a relative error of at most 0.004.
Values may be sent and summed in bfloat16 or wider, within the bound.
No kernel may reach another device: no remote copies, remote signals or barrier semaphores. Data moves between devices by JAX's collectives and lax.ppermute only.
A program may use at most 64 MiB of HBM per device.

```python
import jax
import jax.numpy as jnp

C_IN = 300
HID = 256
LAT = 256
NLON = 128


def draw_ocean_mask(key, part):
    key_col, key_cell = jax.random.split(key)
    share = jax.random.randint(key_col, (NLON,), 25, 101)
    cells = jax.random.randint(key_cell, (LAT, NLON), 0, 100)
    return (cells < share[None, :]).astype(jnp.int32)


def draw_fold_map(key, part):
    pivot = jax.random.randint(key, (), 0, NLON)
    return ((pivot - jnp.arange(NLON, dtype=jnp.int32)) % NLON).astype(jnp.int32)


def block_levels(stream_key, extent, cuts, low, high):
    loudness = 1.0
    for dim, shards_of in cuts:
        draws = jax.random.uniform(jax.random.fold_in(jax.random.fold_in(stream_key, 6), dim), (shards_of,), jnp.float32, low / len(cuts), high / len(cuts))
        loudness = loudness * jnp.repeat(jnp.exp(draws), extent[dim] // shards_of).reshape((-1,) + (1,) * (len(extent) - 1 - dim))
    return loudness


def scatter_about(own_key, shape, width, bound, cuts=(), held_as=jnp.bfloat16):
    result = width * jax.random.normal(own_key, shape, jnp.float32)
    if cuts:
        result = result * block_levels(own_key, shape, cuts, -0.22, 0.18)
    return jnp.clip(result, -bound, bound).astype(held_as)


def setup_inputs(seed: int = 0, part: int = 0) -> dict:
    seeds = jax.random.split(jax.random.key(seed), 8)
    part_splits = jax.random.split(jax.random.fold_in(seeds[7], part), 8)
    state = scatter_about(part_splits[0], (LAT, NLON, C_IN), 1.0, 6.0, ((1, 16),))
    ocean_mask = draw_ocean_mask(jax.random.fold_in(seeds[7], 71), part)
    fold_map = draw_fold_map(jax.random.fold_in(seeds[7], 71), part)
    w_first = scatter_about(seeds[3], (3, 3, C_IN, HID), (9 * C_IN) ** -0.5, 0.125)
    b_first = scatter_about(seeds[4], (HID,), 0.5, 3.0, (), jnp.float32)
    w_second = scatter_about(seeds[5], (3, 3, HID, HID), (9 * HID) ** -0.5, 0.125)
    b_second = scatter_about(seeds[6], (HID,), 0.5, 3.0, (), jnp.float32)
    return {"state": state, "ocean_mask": ocean_mask, "fold_map": fold_map, "w_first": w_first, "b_first": b_first, "w_second": w_second, "b_second": b_second}


def gelu(value):
    return 0.5 * value * (1.0 + jnp.tanh(0.7978845608 * (value + 0.044715 * value * value * value)))


def conv_taps(padded, weight, rows, cols):
    chans = padded.shape[-1]
    total = jnp.zeros((rows * cols, weight.shape[-1]), jnp.float32)
    for shift_y in range(3):
        for shift_x in range(3):
            tap = padded[shift_y:shift_y + rows, shift_x:shift_x + cols].reshape(rows * cols, chans)
            total = total + jnp.dot(tap, weight[shift_y, shift_x], preferred_element_type=jnp.float32)
    return total.reshape(rows, cols, weight.shape[-1])


def extend(field, ghost):
    zeros = jnp.zeros((1,) + field.shape[1:], field.dtype)
    tall = jnp.concatenate([zeros, field, ghost[None]], axis=0)
    return jnp.concatenate([tall[:, -1:], tall, tall[:, :1]], axis=1)


def reference(state, ocean_mask, fold_map, w_first, b_first, w_second, b_second):
    rows, cols, chans = state.shape
    masked = state * ocean_mask.astype(jnp.bfloat16)[:, :, None]
    signs = jnp.where(jnp.arange(chans) < chans // 2, -1.0, 1.0).astype(jnp.bfloat16)
    ghost = jnp.take(masked[rows - 1], fold_map.astype(jnp.int32), axis=0) * signs
    first = conv_taps(extend(masked, ghost), w_first, rows, cols)
    mask_f = ocean_mask.astype(jnp.float32)[:, :, None]
    hidden = (gelu(first + b_first) * mask_f).astype(jnp.bfloat16)
    ghost_hidden = jnp.take(hidden[rows - 1], fold_map.astype(jnp.int32), axis=0)
    second = conv_taps(extend(hidden, ghost_hidden), w_second, rows, cols)
    return ((second + b_second) * mask_f).astype(jnp.bfloat16)
```

```python
import functools

import jax
import jax.numpy as jnp
from jax import lax
from jax.experimental import pallas as pl
from jax.experimental.pallas import tpu as pltpu
from jax.sharding import PartitionSpec as P

BF, F32 = jnp.bfloat16, jnp.float32
LANES, MAIN, SLOT = 128, 256, 64
WIDE = MAIN + 2 * SLOT


def gelu(value):
    return 0.5 * value * (1.0 + jnp.tanh(0.7978845608 * (value + 0.044715 * value * value * value)))


def turned(block, chans):
    rows = block.shape[-1]
    tail = block[MAIN : MAIN + SLOT]
    tail = jnp.concatenate([tail, jnp.zeros((SLOT - tail.shape[0], rows), BF)], axis=0)
    full = jnp.concatenate([block[:MAIN], tail, tail], axis=0)
    eye = (
        lax.broadcasted_iota(jnp.int32, (rows, rows), 0) == lax.broadcasted_iota(jnp.int32, (rows, rows), 1)
    ).astype(F32).astype(BF)
    return lax.dot_general(eye, full, (((1,), (1,)), ((), ())), preferred_element_type=F32)


def prepare(me_ref, x_ref, mask_ref, outer_ref, inner_ref, cols_ref, top_ref, field, topf):
    chans, width, rows = x_ref.shape
    held = outer_ref.shape[1]
    odd = lax.rem(me_ref[0], 2) == 1
    mask = mask_ref[...].astype(F32)
    for i in range(rows // LANES):
        at = slice(i * LANES, (i + 1) * LANES)
        field[i, : chans * width, :] = (x_ref[:, :, at].astype(F32) * mask[None, :, at]).reshape(chans * width, LANES)
        field[i, chans * width : (chans + 1) * width, :] = mask[:, at]
        field[i, (chans + 1) * width :, :] = jnp.zeros(((held - chans - 1) * width, LANES), F32)

    def column(c):
        parts = [field[i, pl.ds(c, held, stride=width), :] for i in range(rows // LANES)]
        return jnp.concatenate(parts, axis=1).astype(BF)

    for c in range(2):
        low, high = column(c), column(width - 2 + c)
        outer_ref[c] = jnp.where(odd, high, low)
        inner_ref[c] = jnp.where(odd, low, high)
    for c in range(width):
        out = turned(column(c), chans)
        cols_ref[c] = out.astype(BF)
        for i in range(2):
            topf[i, c : c + 1, :] = out[rows - 2 + i : rows - 1 + i]
    top_ref[...] = topf[...].astype(BF)


def tails(parts):
    lanes = lax.broadcasted_iota(jnp.int32, parts[0].shape, 1)
    return [jnp.where(lanes < SLOT, parts[0], parts[1]), parts[2]]


def conv_block(
    me_ref, fold_ref, cols_ref, outer_ref, inner_ref, top_ref, w1_ref, b1_ref, w2_ref, b2_ref, out_ref,
    xs, wa, wb, hid, gf, m0, m1, r2, gs, hg, ghost1, ghost2, outf,
):
    chans = w1_ref.shape[2]
    width, rows, _ = cols_ref.shape
    hidden = w1_ref.shape[3]
    total = fold_ref.shape[0]
    me = me_ref[0]
    odd = lax.rem(me, 2) == 1
    for dy in range(3):
        for dx in range(3):
            wa[dx * MAIN : (dx + 1) * MAIN, dy * hidden : (dy + 1) * hidden] = w1_ref[dy, dx, :MAIN, :]
            rest = jnp.concatenate(
                [w1_ref[dy, dx, MAIN:, :], jnp.zeros((SLOT - chans + MAIN, hidden), BF)], axis=0
            )
            wa[3 * MAIN + dx * SLOT : 3 * MAIN + (dx + 1) * SLOT, dy * hidden : (dy + 1) * hidden] = rest
            wb[dx * hidden : (dx + 1) * hidden, dy * hidden : (dy + 1) * hidden] = w2_ref[dy, dx]
    wa[3 * MAIN + 3 * SLOT :, :] = jnp.zeros((SLOT, 3 * hidden), BF)

    xs[2 : 2 + width] = cols_ref[...]
    for c in range(2):
        left = jnp.where(odd, inner_ref[c], outer_ref[c])
        right = jnp.where(odd, outer_ref[c], inner_ref[c])
        xs[c] = turned(left, chans).astype(BF)
        xs[2 + width + c] = turned(right, chans).astype(BF)

    bias1, bias2 = b1_ref[...], b2_ref[...]
    mask_lane = chans
    blocks = top_ref.shape[0]
    gf[...] = top_ref[...].astype(F32).reshape(blocks * 2 * width, WIDE)
    for ref in (m0, m1, r2, gs):
        ref[...] = jnp.zeros_like(ref)
    lane = lax.broadcasted_iota(jnp.int32, (1, WIDE), 1)
    sign = jnp.where(lane < chans // 2, -1.0, 1.0).astype(F32)
    for j in range(width + 4):
        col = lax.rem(me * width + (j - 2) + total, total)
        src = fold_ref[col]
        at = (lax.bitwise_xor(src // width, me) * 2) * width + lax.rem(src, width)
        m0[j : j + 1, :] = gf[pl.ds(at, 1), :]
        north = gf[pl.ds(at + width, 1), :]
        m1[j : j + 1, :] = north
        gs[j : j + 1, :] = north * sign
        r2[j : j + 1, :] = xs[j, rows - 16 :, :].astype(F32)[15:16] * sign

    def taps(ref, offsets):
        parts = [ref[o : o + 16, :].astype(BF) for o in offsets]
        return jnp.concatenate([p[:, :MAIN] for p in parts] + tails([p[:, MAIN:] for p in parts]), axis=1)

    def mm(a, b):
        return jnp.dot(a, b, preferred_element_type=F32)

    ghost1[...] = mm(taps(gs, (0, 1, 2)), wa[:, 2 * hidden :])
    pre = mm(taps(m0, (2, 1, 0)), wa[:, :hidden])
    pre += mm(taps(m1, (2, 1, 0)), wa[:, hidden : 2 * hidden])
    pre += mm(taps(r2, (2, 1, 0)), wa[:, 2 * hidden :])
    hg[...] = jnp.zeros_like(hg)
    hg[:16, :] = gelu(pre + bias1) * m1[1:17, mask_lane : mask_lane + 1]
    ghost2[...] = mm(
        jnp.concatenate([hg[o : o + 16, :].astype(BF) for o in range(3)], axis=1), wb[:, 2 * hidden :]
    )

    row = lax.broadcasted_iota(jnp.int32, (rows, hidden), 0)

    def summed(p, ghost):
        south = jnp.where(row == 0, 0.0, pltpu.roll(p[:, :hidden], 1, 0))
        north = jnp.where(row == rows - 1, ghost, pltpu.roll(p[:, 2 * hidden :], rows - 1, 0))
        return p[:, hidden : 2 * hidden] + south + north

    for h in range(width + 2):
        parts = [xs[h + dx, :, MAIN:] for dx in range(3)]
        lhs = jnp.concatenate([xs[h + dx, :, :MAIN] for dx in range(3)] + tails(parts), axis=1)
        value = summed(mm(lhs, wa[...]), ghost1[h : h + 1, :])
        mask = xs[h + 1, :, MAIN:].astype(F32)[:, mask_lane - MAIN : mask_lane - MAIN + 1]
        hid[h] = (gelu(value + bias1) * mask).astype(BF)
    for o in range(width):
        lhs = jnp.concatenate([hid[o + dx] for dx in range(3)], axis=1)
        value = summed(mm(lhs, wb[...]), ghost2[o : o + 1, :])
        mask = xs[o + 2, :, MAIN:].astype(F32)[:, mask_lane - MAIN : mask_lane - MAIN + 1]
        value = (value + bias2) * mask
        for i in range(hidden // LANES):
            outf[i, pl.ds(o, rows, stride=width), :] = value[:, i * LANES : (i + 1) * LANES]
    for i in range(hidden // LANES):
        out_ref[:, :, i * LANES : (i + 1) * LANES] = outf[i].reshape(rows, width, LANES).astype(BF)


def local(state, ocean_mask, fold_map, w_first, b_first, w_second, b_second):
    rows, width, chans = state.shape
    hidden = w_first.shape[-1]
    n = lax.axis_size("lon")
    me = lax.axis_index("lon")
    assert n & (n - 1) == 0 and MAIN <= chans < MAIN + SLOT and chans // 2 <= MAIN
    held = -(-(chans + 1) // 16) * 16
    smem = pl.BlockSpec(memory_space=pltpu.SMEM)
    vmem = pl.BlockSpec(memory_space=pltpu.VMEM)
    place = jnp.full((1,), me, jnp.int32)
    outer, inner, cols, top = pl.pallas_call(
        prepare,
        out_shape=(
            jax.ShapeDtypeStruct((2, held, rows), BF),
            jax.ShapeDtypeStruct((2, held, rows), BF),
            jax.ShapeDtypeStruct((width, rows, WIDE), BF),
            jax.ShapeDtypeStruct((2, width, WIDE), BF),
        ),
        in_specs=[smem, vmem, vmem],
        out_specs=(vmem,) * 4,
        scratch_shapes=[pltpu.VMEM((rows // LANES, held * width, LANES), F32), pltpu.VMEM((2, width, WIDE), F32)],
        name="prepare",
    )(place, state.transpose(2, 1, 0), ocean_mask.T)

    def swap(value, pairs):
        return lax.ppermute(value, "lon", pairs)

    outer = swap(outer, [(i, (i + 1 if i % 2 else i - 1) % n) for i in range(n)])
    inner = swap(inner, [(i, i ^ 1) for i in range(n)])
    tops, step = top[None], 1
    while step < n:
        tops = jnp.concatenate([tops, swap(tops, [(i, i ^ step) for i in range(n)])], axis=0)
        step *= 2
    blocks = width + 2
    return pl.pallas_call(
        conv_block,
        out_shape=jax.ShapeDtypeStruct((rows, width, hidden), BF),
        in_specs=[smem, smem] + [vmem] * 8,
        out_specs=vmem,
        scratch_shapes=[
            pltpu.VMEM((width + 4, rows, WIDE), BF),
            pltpu.VMEM((3 * MAIN + 4 * SLOT, 3 * hidden), BF),
            pltpu.VMEM((3 * hidden, 3 * hidden), BF),
            pltpu.VMEM((blocks, rows, hidden), BF),
            pltpu.VMEM((n * 2 * width, WIDE), F32),
            pltpu.VMEM((24, WIDE), F32),
            pltpu.VMEM((24, WIDE), F32),
            pltpu.VMEM((24, WIDE), F32),
            pltpu.VMEM((24, WIDE), F32),
            pltpu.VMEM((24, hidden), F32),
            pltpu.VMEM((16, hidden), F32),
            pltpu.VMEM((16, hidden), F32),
            pltpu.VMEM((hidden // LANES, rows * width, LANES), F32),
        ],
        compiler_params=pltpu.CompilerParams(vmem_limit_bytes=48 << 20),
        name="conv_block",
    )(place, fold_map, cols, outer, inner, tops, w_first, b_first[None], w_second, b_second[None])


def solution(mesh):
    return jax.shard_map(
        local,
        mesh=mesh,
        in_specs=(P(None, ("grp", "lon"), None), P(None, "lon"), P(), P(), P(), P(), P()),
        out_specs=P(None, ("grp", "lon"), None),
        check_vma=False,
    )
```

```python
import functools

import jax
import jax.numpy as jnp
from jax import lax
from jax.experimental import pallas as pl
from jax.experimental.pallas import tpu as pltpu
from jax.sharding import PartitionSpec as P

BF, F32 = jnp.bfloat16, jnp.float32
LANES, MAIN, SLOT, PIECES = 128, 256, 64, 4
WIDE = MAIN + 2 * SLOT


def gelu(value):
    return 0.5 * value * (1.0 + jnp.tanh(0.7978845608 * (value + 0.044715 * value * value * value)))


def turned(block, chans):
    rows = block.shape[-1]
    tail = block[MAIN : MAIN + SLOT]
    tail = jnp.concatenate([tail, jnp.zeros((SLOT - tail.shape[0], rows), BF)], axis=0)
    full = jnp.concatenate([block[:MAIN], tail, tail], axis=0)
    eye = (
        lax.broadcasted_iota(jnp.int32, (rows, rows), 0) == lax.broadcasted_iota(jnp.int32, (rows, rows), 1)
    ).astype(F32).astype(BF)
    return lax.dot_general(eye, full, (((1,), (1,)), ((), ())), preferred_element_type=F32)


def prepare(
    me_ref, fold_hbm, x_hbm, mask_hbm, b1_hbm, b2_hbm, outer_ref, inner_ref, cols_ref, top_ref, bias_ref, at_ref,
    x_ref, mask_ref, fold_ref, field, sem,
):
    chans, width, rows = x_ref.shape
    held = outer_ref.shape[1]
    me = me_ref[0]
    cuts = [chans * i // PIECES for i in range(PIECES + 1)]
    pairs = [(mask_hbm, mask_ref)]
    pairs += [(x_hbm.at[lo:hi], x_ref.at[lo:hi]) for lo, hi in zip(cuts, cuts[1:])]
    pairs += [(b1_hbm, bias_ref.at[0:1]), (b2_hbm, bias_ref.at[1:2]), (fold_hbm, fold_ref)]
    copies = [pltpu.make_async_copy(src, dst, sem.at[i]) for i, (src, dst) in enumerate(pairs)]
    for copy in copies:
        copy.start()
    odd = lax.rem(me, 2) == 1
    copies[0].wait()
    mask = mask_ref[...].astype(F32)
    halves = [slice(i * LANES, (i + 1) * LANES) for i in range(rows // LANES)]
    for i, at in enumerate(halves):
        field[i, chans * width : (chans + 1) * width, :] = mask[:, at]
        field[i, (chans + 1) * width :, :] = jnp.zeros(((held - chans - 1) * width, LANES), F32)
    for lo, hi, copy in zip(cuts, cuts[1:], copies[1:]):
        copy.wait()
        for i, at in enumerate(halves):
            block = x_ref[lo:hi, :, at].astype(F32) * mask[None, :, at]
            field[i, lo * width : hi * width, :] = block.reshape((hi - lo) * width, LANES)

    def column(c):
        parts = [field[i, pl.ds(c, held, stride=width), :] for i in range(rows // LANES)]
        return jnp.concatenate(parts, axis=1).astype(BF)

    for c in range(2):
        low, high = column(c), column(width - 2 + c)
        outer_ref[c] = jnp.where(odd, high, low)
        inner_ref[c, :held] = jnp.where(odd, low, high)
    last = []
    for c in range(width):
        out = turned(column(c), chans)
        cols_ref[c] = out.astype(BF)
        last.append(out[rows - 2 :])
    top = jnp.concatenate([v[i : i + 1] for i in range(2) for v in last], axis=0).astype(BF)
    top_ref[0] = top
    inner_ref[0, held:] = top[:, :rows]
    pad = jnp.zeros((2 * width, 2 * rows - WIDE), BF)
    inner_ref[1, held:] = jnp.concatenate([top[:, rows:], pad], axis=1)
    for copy in copies[1 + PIECES :]:
        copy.wait()
    total = fold_ref.shape[0]
    for j in range(16):
        src = fold_ref[lax.rem(me * width + (j - 2) + total, total)]
        at_ref[j] = lax.bitwise_xor(src // width, me) * (2 * width) + lax.rem(src, width)


def top_rows(block):
    return jnp.concatenate([block[0], block[1][:, : WIDE - MAIN]], axis=1)


def join(mine_ref, got_ref, after_ref, out_ref):
    count = mine_ref.shape[0]
    out_ref[:count] = mine_ref[...]
    if got_ref.shape == mine_ref.shape:
        out_ref[count:] = got_ref[...]
    else:
        out_ref[count] = top_rows(got_ref[:, got_ref.shape[1] - mine_ref.shape[1] :])


def mm(a, b):
    return jnp.dot(a, b, preferred_element_type=F32)


def mask_of(column, chans):
    return column[:, MAIN:].astype(F32)[:, chans - MAIN : chans - MAIN + 1]


def tail_weights(w1_ref, wt):
    chans, hidden = w1_ref.shape[2:]
    for dy in range(3):
        for dx in range(3):
            rest = jnp.concatenate(
                [w1_ref[dy, dx, MAIN:, :], jnp.zeros((SLOT - chans + MAIN, hidden), BF)], axis=0
            )
            wt[dx * SLOT : (dx + 1) * SLOT, dy * hidden : (dy + 1) * hidden] = rest
    wt[3 * SLOT :, :] = jnp.zeros((SLOT, 3 * hidden), BF)


def first_taps(columns):
    some = next(c for c in columns if c is not None)
    lanes = lax.broadcasted_iota(jnp.int32, (some.shape[0], LANES), 1)
    zero = jnp.zeros((some.shape[0], LANES), BF)
    tail = [zero if c is None else c[:, MAIN:] for c in columns]
    parts = [c[:, :MAIN] for c in columns if c is not None]
    if columns[0] is not None or columns[1] is not None:
        parts.append(jnp.where(lanes < SLOT, tail[0], tail[1]))
    if columns[2] is not None:
        parts.append(tail[2])
    return jnp.concatenate(parts, axis=1)


def first_weights(w1_ref, wt, columns, dys=(0, 1, 2)):
    hidden = w1_ref.shape[3]
    out = []
    for dy in dys:
        at = slice(dy * hidden, (dy + 1) * hidden)
        parts = [w1_ref[dy, dx, :MAIN, :] for dx in range(3) if columns[dx] is not None]
        if columns[0] is not None or columns[1] is not None:
            parts.append(wt[: 2 * SLOT, at])
        if columns[2] is not None:
            parts.append(wt[2 * SLOT :, at])
        out.append(jnp.concatenate(parts, axis=0))
    return jnp.concatenate(out, axis=1)


def second_weights(w2_ref, columns, dys=(0, 1, 2)):
    return jnp.concatenate(
        [
            jnp.concatenate([w2_ref[dy, dx] for dx in range(3) if columns[dx] is not None], axis=0)
            for dy in dys
        ],
        axis=1,
    )


def summed(p):
    rows, hidden = p.shape[0], p.shape[1] // 3
    row = lax.broadcasted_iota(jnp.int32, (rows, hidden), 0)
    south = jnp.where(row == 0, 0.0, pltpu.roll(p[:, :hidden], 1, 0))
    north = jnp.where(row == rows - 1, 0.0, pltpu.roll(p[:, 2 * hidden :], rows - 1, 0))
    return p[:, hidden : 2 * hidden] + south + north


def edges(width):
    return (0, 1, width, width + 1)


def own_column(cols_ref, j):
    return cols_ref[j - 2] if 2 <= j < 2 + cols_ref.shape[0] else None


def hidden_columns(cols_ref, w1_ref, bias_ref, wt, hid_ref, last_ref, first):
    chans, hidden = w1_ref.shape[2:]
    rows = cols_ref.shape[1]
    row = lax.broadcasted_iota(jnp.int32, (rows, hidden), 0)
    last_ref[...] = jnp.zeros_like(last_ref)
    for i in range(hid_ref.shape[0]):
        columns = [own_column(cols_ref, first + i + dx) for dx in range(3)]
        value = summed(mm(first_taps(columns), first_weights(w1_ref, wt, columns)))
        last_ref[i : i + 1, :] = value[rows - 1 :]
        value = gelu(value + bias_ref[0:1]) * mask_of(columns[1], chans)
        hid_ref[i] = jnp.where(row == rows - 1, 0.0, value).astype(BF)


def inside_a(cols_ref, w1_ref, bias_ref, hid_ref, last_ref, wt_ref):
    tail_weights(w1_ref, wt_ref)
    hidden_columns(cols_ref, w1_ref, bias_ref, wt_ref, hid_ref, last_ref, 2)


def inside_b(before, cols_ref, w1_ref, bias_ref, wt_ref, after_ref, hid_ref, last_ref, part_ref):
    hidden_columns(cols_ref, w1_ref, bias_ref, wt_ref, hid_ref, last_ref, 2 + before)
    for i, h in enumerate(edges(cols_ref.shape[0])):
        columns = [own_column(cols_ref, h + dx) for dx in range(3)]
        part_ref[i] = summed(mm(first_taps(columns), first_weights(w1_ref, wt_ref, columns)))


def inside_c(chans, hid_a, hid_b, cols_ref, w2_ref, bias_ref, after_ref, out_ref):
    width, rows, _ = cols_ref.shape
    hidden = w2_ref.shape[3]
    before = hid_a.shape[0]
    for o in range(width):
        columns = []
        for h in range(o, o + 3):
            inside = 2 <= h < width
            columns.append((hid_a[h - 2] if h - 2 < before else hid_b[h - 2 - before]) if inside else None)
        have = [c for c in columns if c is not None]
        if have:
            value = summed(mm(jnp.concatenate(have, axis=1), second_weights(w2_ref, columns)))
        else:
            value = jnp.zeros((rows, hidden), F32)
        value = value + bias_ref[1:2]
        if len(have) == 3:
            value = value * mask_of(cols_ref[o], chans)
        for i in range(hidden // LANES):
            out_ref[i, pl.ds(o, rows, stride=width), :] = value[:, i * LANES : (i + 1) * LANES]


def border(
    me_ref, cols_ref, top_ref, outer_ref, inner_ref, part_ref, last_a, last_b, outp_ref, wt, w1_ref, bias_ref, w2_ref,
    after_ref, out_hbm, slab_ref, sea_ref, line_ref, own_ref, hx, hid, outf, outb, sem,
):
    chans, hidden = w1_ref.shape[2:]
    width, rows, _ = cols_ref.shape
    held = outer_ref.shape[1]
    odd = lax.rem(me_ref[0], 2) == 1
    for c in range(2):
        hx[c] = turned(jnp.where(odd, inner_ref[c, :held], outer_ref[c]), chans).astype(BF)
        hx[2 + c] = turned(jnp.where(odd, outer_ref[c], inner_ref[c, :held]), chans).astype(BF)

    def column(j):
        return hx[j] if j < 2 else cols_ref[j - 2] if j < 2 + width else hx[j - width]

    own_ref[...] = jnp.zeros_like(own_ref)
    for j in range(width + 4):
        own_ref[j : j + 1, :] = column(j)[rows - 16 :].astype(F32)[15:16]
    bias1 = bias_ref[0:1]
    row = lax.broadcasted_iota(jnp.int32, (rows, hidden), 0)
    line_ref[...] = jnp.zeros_like(line_ref)
    line_ref[2:6] = last_a[:4]
    line_ref[6:width] = last_b[: width - 6]
    for i, h in enumerate(edges(width)):
        columns = [column(h + dx) if not 2 <= h + dx < 2 + width else None for dx in range(3)]
        value = part_ref[i] + summed(mm(first_taps(columns), first_weights(w1_ref, wt, columns)))
        line_ref[h : h + 1, :] = value[rows - 1 :]
        value = gelu(value + bias1) * mask_of(column(h + 1), chans)
        hid[i] = jnp.where(row == rows - 1, 0.0, value).astype(BF)
    for o in (0, 1, width - 2, width - 1):
        columns = [hid[edges(width).index(o + dx)] if o + dx in edges(width) else None for dx in range(3)]
        have = [c for c in columns if c is not None]
        value = summed(mm(jnp.concatenate(have, axis=1), second_weights(w2_ref, columns)))
        mask = mask_of(cols_ref[o], chans)
        for i in range(hidden // LANES):
            at = (i, pl.ds(o, rows, stride=width), slice(None))
            outf[at] = (outp_ref[at] + value[:, i * LANES : (i + 1) * LANES]) * mask
    step = rows // PIECES
    place = lax.rem(lax.broadcasted_iota(jnp.int32, (step * width, LANES), 0), width)
    edge = (place < 2) | (place >= width - 2)
    copies = []
    for p in range(PIECES):
        at = slice(p * step * width, (p + 1) * step * width)
        for i in range(hidden // LANES):
            lanes = slice(i * LANES, (i + 1) * LANES)
            value = jnp.where(edge, outf[i, at], outp_ref[i, at])
            outb[p * step : (p + 1) * step, :, lanes] = value.reshape(step, width, LANES).astype(BF)
            if p == PIECES - 1:
                slab_ref[:, lanes] = value[(step - 2) * width :]
        here = slice(p * step, (p + 1) * step)
        copies.append(pltpu.make_async_copy(outb.at[here], out_hbm.at[here], sem.at[p]))
        copies[-1].start()
    sea = mask_of(top_ref[0], chans)
    sea_ref[...] = jnp.broadcast_to(sea, sea_ref.shape)
    for copy in copies:
        copy.wait()


def fold(
    at_ref, tops_ref, slab_ref, sea_ref, line_ref, own_ref, wt, w1_ref, bias_ref, w2_ref, old_hbm,
    out_hbm, gf, m0, m1, r2, gs, hg, hz, outb, sem,
):
    chans, hidden = w1_ref.shape[2:]
    rows, width, _ = out_hbm.shape
    bias1 = bias_ref[0:1]
    gf[...] = tops_ref[...].astype(F32).reshape(gf.shape)
    for ref in (m0, m1, r2, gs):
        ref[...] = jnp.zeros_like(ref)
    lane = lax.broadcasted_iota(jnp.int32, (1, WIDE), 1)
    sign = jnp.where(lane < chans // 2, -1.0, 1.0).astype(F32)
    for j in range(width + 4):
        at = at_ref[j]
        m0[j : j + 1, :] = gf[pl.ds(at, 1), :]
        north = gf[pl.ds(at + width, 1), :]
        m1[j : j + 1, :] = north
        gs[j : j + 1, :] = north * sign
    r2[...] = own_ref[...] * sign

    def taps(ref, offsets):
        return first_taps([ref[o : o + 16, :].astype(BF) for o in offsets])

    every = (0, 0, 0)
    mixed = mm(
        jnp.concatenate([taps(gs, (0, 1, 2)), taps(r2, (2, 1, 0))], axis=0), first_weights(w1_ref, wt, every, (2,))
    )
    pre = mixed[16:]
    pre += mm(taps(m0, (2, 1, 0)), first_weights(w1_ref, wt, every, (0,)))
    pre += mm(taps(m1, (2, 1, 0)), first_weights(w1_ref, wt, every, (1,)))
    hg[...] = jnp.zeros_like(hg)
    hg[:16, :] = gelu(pre + bias1) * m1[1:17, chans : chans + 1]
    hz[...] = jnp.zeros_like(hz)
    hz[:16, :] = gelu(line_ref[...] + mixed[:16] + bias1) * own_ref[1:17, chans : chans + 1]
    wide = [jnp.concatenate([ref[o : o + 16, :].astype(BF) for o in range(3)], axis=1) for ref in (hz, hg)]
    more = mm(jnp.concatenate(wide, axis=0), second_weights(w2_ref, every, (1, 2)))
    below = more[:width, hidden:]
    level = more[:width, :hidden] + more[16 : 16 + width, hidden:]
    value = slab_ref[...] + jnp.concatenate([below, level], axis=0) * sea_ref[...]
    outb[...] = value.reshape(2, width, hidden).astype(BF)
    copy = pltpu.make_async_copy(outb, out_hbm.at[rows - 2 : rows], sem)
    copy.start()
    copy.wait()


def local(state, ocean_mask, fold_map, w_first, b_first, w_second, b_second):
    rows, width, chans = state.shape
    hidden = w_first.shape[-1]
    n = lax.axis_size("lon")
    me = lax.axis_index("lon")
    assert n & (n - 1) == 0 and MAIN <= chans < MAIN + SLOT and chans // 2 <= MAIN and width == 8 and rows == MAIN
    held = -(-(chans + 1) // 16) * 16
    smem = pl.BlockSpec(memory_space=pltpu.SMEM)
    vmem = pl.BlockSpec(memory_space=pltpu.VMEM)
    hbm = pl.BlockSpec(memory_space=pltpu.MemorySpace.HBM)
    shape = jax.ShapeDtypeStruct
    scratch = pltpu.VMEM
    dma = pltpu.SemaphoreType.DMA
    place = jnp.full((1,), me, jnp.int32)

    def limit(mib):
        return pltpu.CompilerParams(vmem_limit_bytes=mib << 20)

    def far(value):
        return pltpu.with_memory_space_constraint(value, pltpu.MemorySpace.HBM)

    sent, inner, cols, top, bias, at = pl.pallas_call(
        prepare,
        out_shape=(
            shape((2, held, rows), BF),
            shape((2, held + 2 * width, rows), BF),
            shape((width, rows, WIDE), BF),
            shape((1, 2 * width, WIDE), BF),
            shape((2, hidden), F32),
            shape((16,), jnp.int32),
        ),
        in_specs=[smem] + [hbm] * 5,
        out_specs=(vmem,) * 5 + (smem,),
        scratch_shapes=[
            scratch((chans, width, rows), BF),
            scratch((width, rows), jnp.int32),
            pltpu.SMEM(fold_map.shape, jnp.int32),
            scratch((rows // LANES, held * width, LANES), F32),
            dma((PIECES + 4,)),
        ],
        compiler_params=limit(14),
        name="prepare",
    )(
        place, far(fold_map), far(state.transpose(2, 1, 0)), far(ocean_mask.T),
        far(b_first[None]), far(b_second[None]),
    )
    outer = lax.ppermute(sent, "lon", [(i, (i + 1 if i % 2 else i - 1) % n) for i in range(n)])
    inner = lax.ppermute(inner, "lon", [(i, i ^ 1) for i in range(n)])

    def joined(mine, got, after):
        return pl.pallas_call(
            join,
            out_shape=shape((2 * mine.shape[0],) + mine.shape[1:], BF),
            in_specs=[vmem] * 3,
            out_specs=vmem,
            compiler_params=limit(4),
            name="join",
        )(mine, got, after)

    before = 4
    hid_a, last_a, wt = pl.pallas_call(
        inside_a,
        out_shape=(
            shape((before, rows, hidden), BF),
            shape((8, hidden), F32),
            shape((4 * SLOT, 3 * hidden), BF),
        ),
        in_specs=[vmem] * 3,
        out_specs=(vmem,) * 3,
        compiler_params=limit(12),
        name="inside_a",
    )(cols, w_first, bias)

    def stage_b(after):
        return pl.pallas_call(
            functools.partial(inside_b, before),
            out_shape=(
                shape((width - 2 - before, rows, hidden), BF),
                shape((8, hidden), F32),
                shape((4, rows, hidden), F32),
            ),
            in_specs=[vmem] * 5,
            out_specs=(vmem,) * 3,
            compiler_params=limit(12),
            name="inside_b",
        )(cols, w_first, bias, wt, after)

    def stage_c(hid_b, after):
        return pl.pallas_call(
            functools.partial(inside_c, chans),
            out_shape=shape((hidden // LANES, rows * width, LANES), F32),
            in_specs=[vmem] * 6,
            out_specs=vmem,
            compiler_params=limit(12),
            name="inside_c",
        )(hid_a, hid_b, cols, w_second, bias, after)

    tops = joined(top, inner, last_a)
    step, stage, after = 2, 0, tops
    while step < n:
        got = lax.ppermute(tops, "lon", [(i, i ^ step) for i in range(n)])
        if stage == 0:
            hid_b, last_b, part = stage_b(tops)
            after = last_b
        elif stage == 1:
            outp = stage_c(hid_b, tops)
            after = outp
        else:
            after = tops
        if stage < 2:
            tops = joined(tops, got, after)
        else:
            late, final = tops, got
            tops = None
        step, stage = 2 * step, stage + 1
        if tops is None:
            if step < n:
                tops = joined(late, final, late)
    out, slab, sea, line, own = pl.pallas_call(
        border,
        out_shape=(
            shape((rows, width, hidden), BF),
            shape((2 * width, hidden), F32),
            shape((2 * width, hidden), F32),
            shape((16, hidden), F32),
            shape((24, WIDE), F32),
        ),
        in_specs=[smem] + [vmem] * 13,
        out_specs=(hbm,) + (vmem,) * 4,
        scratch_shapes=[
            scratch((4, rows, WIDE), BF),
            scratch((4, rows, hidden), BF),
            scratch((hidden // LANES, rows * width, LANES), F32),
            scratch((rows, width, hidden), BF),
            dma((PIECES,)),
        ],
        compiler_params=limit(16),
        name="border",
    )(place, cols, top, outer, inner, part, last_a, last_b, outp, wt, w_first, bias, w_second, late)
    tops = joined(late, final, line)
    return pl.pallas_call(
        fold,
        out_shape=shape((rows, width, hidden), BF),
        in_specs=[smem] + [vmem] * 9 + [hbm],
        out_specs=hbm,
        scratch_shapes=[scratch((n * 2 * width, WIDE), F32)]
        + [scratch((24, WIDE), F32)] * 4
        + [scratch((24, hidden), F32)] * 2
        + [scratch((2, width, hidden), BF), dma],
        input_output_aliases={10: 0},
        compiler_params=limit(10),
        name="fold",
    )(at, tops, slab, sea, line, own, wt, w_first, bias, w_second, out)


def solution(mesh):
    return jax.shard_map(
        local,
        mesh=mesh,
        in_specs=(P(None, ("grp", "lon"), None), P(None, "lon"), P(), P(), P(), P(), P()),
        out_specs=P(None, ("grp", "lon"), None),
        check_vma=False,
    )
```

```python
import functools

import jax
import jax.numpy as jnp
from jax import lax
from jax.experimental import pallas as pl
from jax.experimental.pallas import tpu as pltpu
from jax.sharding import PartitionSpec as P

BF, F32 = jnp.bfloat16, jnp.float32
LANES, MAIN, SLOT, PIECES = 128, 256, 64, 4
WIDE = MAIN + 2 * SLOT


def gelu(value):
    return 0.5 * value * (1.0 + jnp.tanh(0.7978845608 * (value + 0.044715 * value * value * value)))


def turned(block):
    rows = block.shape[-1]
    tail = block[MAIN : MAIN + SLOT]
    tail = jnp.concatenate([tail, jnp.zeros((SLOT - tail.shape[0], rows), BF)], axis=0)
    full = jnp.concatenate([block[:MAIN], tail, tail], axis=0)
    eye = (
        lax.broadcasted_iota(jnp.int32, (rows, rows), 0) == lax.broadcasted_iota(jnp.int32, (rows, rows), 1)
    ).astype(F32).astype(BF)
    return lax.dot_general(eye, full, (((1,), (1,)), ((), ())), preferred_element_type=F32)


def prepare(
    me_ref, fold_hbm, x_hbm, mask_hbm, b1_hbm, b2_hbm, w1_hbm, w2_hbm,
    outer_ref, inner_ref, cols_ref, top_ref, bias_ref, at_ref, w1_ref, w2_ref,
    x_ref, mask_ref, fold_ref, field, sem,
):
    chans, width, rows = x_ref.shape
    held = outer_ref.shape[1]
    me = me_ref[0]
    cuts = [chans * i // PIECES for i in range(PIECES + 1)]
    pairs = [(mask_hbm, mask_ref)]
    pairs += [(x_hbm.at[lo:hi], x_ref.at[lo:hi]) for lo, hi in zip(cuts, cuts[1:])]
    pairs += [(b1_hbm, bias_ref.at[0:1]), (b2_hbm, bias_ref.at[1:2]), (fold_hbm, fold_ref)]
    pairs += [(w1_hbm, w1_ref), (w2_hbm, w2_ref)]
    copies = [pltpu.make_async_copy(src, dst, sem.at[i]) for i, (src, dst) in enumerate(pairs)]
    for copy in copies:
        copy.start()
    odd = lax.rem(me, 2) == 1
    copies[0].wait()
    mask = mask_ref[...].astype(F32)
    halves = [slice(i * LANES, (i + 1) * LANES) for i in range(rows // LANES)]
    for i, at in enumerate(halves):
        field[i, chans * width : (chans + 1) * width, :] = mask[:, at]
        field[i, (chans + 1) * width :, :] = jnp.zeros(((held - chans - 1) * width, LANES), F32)
    for lo, hi, copy in zip(cuts, cuts[1:], copies[1:]):
        copy.wait()
        for i, at in enumerate(halves):
            block = x_ref[lo:hi, :, at].astype(F32) * mask[None, :, at]
            field[i, lo * width : hi * width, :] = block.reshape((hi - lo) * width, LANES)

    def column(c):
        parts = [field[i, pl.ds(c, held, stride=width), :] for i in range(rows // LANES)]
        return jnp.concatenate(parts, axis=1).astype(BF)

    for c in range(2):
        low, high = column(c), column(width - 2 + c)
        outer_ref[c] = jnp.where(odd, high, low)
        inner_ref[c, :held] = jnp.where(odd, low, high)
    last = []
    for c in range(width):
        out = turned(column(c))
        cols_ref[c] = out.astype(BF)
        last.append(out[rows - 2 :])
    top = jnp.concatenate([v[i : i + 1] for i in range(2) for v in last], axis=0).astype(BF)
    top_ref[0] = top
    inner_ref[0, held:] = top[:, :rows]
    pad = jnp.zeros((2 * width, 2 * rows - WIDE), BF)
    inner_ref[1, held:] = jnp.concatenate([top[:, rows:], pad], axis=1)
    for copy in copies[1 + PIECES :]:
        copy.wait()
    total = fold_ref.shape[0]
    n = total // width
    start = lax.rem(fold_ref[0] - (width + 1) + total, total) // width
    for j in range(16):
        src = fold_ref[lax.rem(me * width + (j - 2) + total, total)]
        block = lax.rem(src // width - start + me + 2 * n, n)
        at_ref[j] = lax.rem(block, 3) * (2 * width) + lax.rem(src, width)
    peer = lax.bitwise_xor(me, n // 2)
    for j in range(3):
        theirs = lax.bitwise_xor(lax.rem(start - peer + j + n, n), me)
        mine = lax.bitwise_xor(lax.rem(start - me + j + n, n), me)
        at_ref[16 + j] = lax.rem(theirs, n // 2)
        at_ref[19 + j] = lax.rem(mine, n // 2)
        at_ref[22 + j] = mine // (n // 2)


def top_rows(block):
    return jnp.concatenate([block[0], block[1][:, : WIDE - MAIN]], axis=1)


def join_first(mine_ref, got_ref, after_ref, sent_ref, out_ref, pass_ref):
    out_ref[0] = mine_ref[0]
    out_ref[1] = top_rows(got_ref[:, got_ref.shape[1] - mine_ref.shape[1] :])


def join(mine_ref, got_ref, out_ref):
    count = mine_ref.shape[0]
    out_ref[:count] = mine_ref[...]
    out_ref[count:] = got_ref[...]


def choose(at_ref, mine_ref, got_ref, after_ref, send_ref, keep_ref, blocks):
    count = mine_ref.shape[0]
    blocks[:count] = mine_ref[...]
    blocks[count:] = got_ref[...]
    for j in range(3):
        send_ref[j] = blocks[at_ref[16 + j]]
        keep_ref[j] = blocks[at_ref[19 + j]]


def mm(a, b):
    return jnp.dot(a, b, preferred_element_type=F32)


def mask_of(column, chans):
    return column[:, MAIN:].astype(F32)[:, chans - MAIN : chans - MAIN + 1]


def tail_weights(w1_ref, wt):
    chans, hidden = w1_ref.shape[2:]
    for dy in range(3):
        for dx in range(3):
            rest = jnp.concatenate(
                [w1_ref[dy, dx, MAIN:, :], jnp.zeros((SLOT - chans + MAIN, hidden), BF)], axis=0
            )
            wt[dx * SLOT : (dx + 1) * SLOT, dy * hidden : (dy + 1) * hidden] = rest
    wt[3 * SLOT :, :] = jnp.zeros((SLOT, 3 * hidden), BF)


def first_taps(columns):
    some = next(c for c in columns if c is not None)
    lanes = lax.broadcasted_iota(jnp.int32, (some.shape[0], LANES), 1)
    zero = jnp.zeros((some.shape[0], LANES), BF)
    tail = [zero if c is None else c[:, MAIN:] for c in columns]
    parts = [c[:, :MAIN] for c in columns if c is not None]
    if columns[0] is not None or columns[1] is not None:
        parts.append(jnp.where(lanes < SLOT, tail[0], tail[1]))
    if columns[2] is not None:
        parts.append(tail[2])
    return jnp.concatenate(parts, axis=1)


def first_weights(w1_ref, wt, columns, dys=(0, 1, 2)):
    hidden = w1_ref.shape[3]
    out = []
    for dy in dys:
        at = slice(dy * hidden, (dy + 1) * hidden)
        parts = [w1_ref[dy, dx, :MAIN, :] for dx in range(3) if columns[dx] is not None]
        if columns[0] is not None or columns[1] is not None:
            parts.append(wt[: 2 * SLOT, at])
        if columns[2] is not None:
            parts.append(wt[2 * SLOT :, at])
        out.append(jnp.concatenate(parts, axis=0))
    return jnp.concatenate(out, axis=1)


def second_weights(w2_ref, columns, dys=(0, 1, 2)):
    return jnp.concatenate(
        [
            jnp.concatenate([w2_ref[dy, dx] for dx in range(3) if columns[dx] is not None], axis=0)
            for dy in dys
        ],
        axis=1,
    )


def summed(p):
    rows, hidden = p.shape[0], p.shape[1] // 3
    row = lax.broadcasted_iota(jnp.int32, (rows, hidden), 0)
    south = jnp.where(row == 0, 0.0, pltpu.roll(p[:, :hidden], 1, 0))
    north = jnp.where(row == rows - 1, 0.0, pltpu.roll(p[:, 2 * hidden :], rows - 1, 0))
    return p[:, hidden : 2 * hidden] + south + north


def edges(width):
    return (0, 1, width, width + 1)


def own_column(cols_ref, j):
    return cols_ref[j - 2] if 2 <= j < 2 + cols_ref.shape[0] else None


def hidden_columns(cols_ref, w1_ref, bias_ref, wt, hid_ref, last_ref, first):
    chans, hidden = w1_ref.shape[2:]
    rows = cols_ref.shape[1]
    row = lax.broadcasted_iota(jnp.int32, (rows, hidden), 0)
    last_ref[...] = jnp.zeros_like(last_ref)
    for i in range(hid_ref.shape[0]):
        columns = [own_column(cols_ref, first + i + dx) for dx in range(3)]
        value = summed(mm(first_taps(columns), first_weights(w1_ref, wt, columns)))
        last_ref[i : i + 1, :] = value[rows - 1 :]
        value = gelu(value + bias_ref[0:1]) * mask_of(columns[1], chans)
        hid_ref[i] = jnp.where(row == rows - 1, 0.0, value).astype(BF)


def inside_a(cols_ref, w1_ref, bias_ref, hid_ref, last_ref, wt_ref):
    tail_weights(w1_ref, wt_ref)
    hidden_columns(cols_ref, w1_ref, bias_ref, wt_ref, hid_ref, last_ref, 2)


def inside_b(before, cols_ref, w1_ref, bias_ref, wt_ref, after_ref, hid_ref, last_ref, part_ref):
    hidden_columns(cols_ref, w1_ref, bias_ref, wt_ref, hid_ref, last_ref, 2 + before)
    for i, h in enumerate(edges(cols_ref.shape[0])):
        columns = [own_column(cols_ref, h + dx) for dx in range(3)]
        part_ref[i] = summed(mm(first_taps(columns), first_weights(w1_ref, wt_ref, columns)))


def inside_c(chans, hid_a, hid_b, cols_ref, w2_ref, bias_ref, after_ref, out_ref):
    width, rows, _ = cols_ref.shape
    hidden = w2_ref.shape[3]
    before = hid_a.shape[0]
    for o in range(width):
        columns = []
        for h in range(o, o + 3):
            inside = 2 <= h < width
            columns.append((hid_a[h - 2] if h - 2 < before else hid_b[h - 2 - before]) if inside else None)
        have = [c for c in columns if c is not None]
        if have:
            value = summed(mm(jnp.concatenate(have, axis=1), second_weights(w2_ref, columns)))
        else:
            value = jnp.zeros((rows, hidden), F32)
        value = value + bias_ref[1:2]
        if len(have) == 3:
            value = value * mask_of(cols_ref[o], chans)
        for i in range(hidden // LANES):
            out_ref[i, pl.ds(o, rows, stride=width), :] = value[:, i * LANES : (i + 1) * LANES]


def border(
    me_ref, cols_ref, top_ref, outer_ref, inner_ref, part_ref, last_a, last_b, outp_ref, wt, w1_ref, bias_ref, w2_ref,
    after_ref, out_hbm, slab_ref, sea_ref, line_ref, own_ref, hx, hid, outf, outb, sem,
):
    chans, hidden = w1_ref.shape[2:]
    width, rows, _ = cols_ref.shape
    held = outer_ref.shape[1]
    odd = lax.rem(me_ref[0], 2) == 1
    for c in range(2):
        hx[c] = turned(jnp.where(odd, inner_ref[c, :held], outer_ref[c])).astype(BF)
        hx[2 + c] = turned(jnp.where(odd, outer_ref[c], inner_ref[c, :held])).astype(BF)

    def column(j):
        return hx[j] if j < 2 else cols_ref[j - 2] if j < 2 + width else hx[j - width]

    own_ref[...] = jnp.zeros_like(own_ref)
    for j in range(width + 4):
        own_ref[j : j + 1, :] = column(j)[rows - 16 :].astype(F32)[15:16]
    bias1 = bias_ref[0:1]
    row = lax.broadcasted_iota(jnp.int32, (rows, hidden), 0)
    line_ref[...] = jnp.zeros_like(line_ref)
    line_ref[2:6] = last_a[:4]
    line_ref[6:width] = last_b[: width - 6]
    for i, h in enumerate(edges(width)):
        columns = [column(h + dx) if not 2 <= h + dx < 2 + width else None for dx in range(3)]
        value = part_ref[i] + summed(mm(first_taps(columns), first_weights(w1_ref, wt, columns)))
        line_ref[h : h + 1, :] = value[rows - 1 :]
        value = gelu(value + bias1) * mask_of(column(h + 1), chans)
        hid[i] = jnp.where(row == rows - 1, 0.0, value).astype(BF)
    for o in (0, 1, width - 2, width - 1):
        columns = [hid[edges(width).index(o + dx)] if o + dx in edges(width) else None for dx in range(3)]
        have = [c for c in columns if c is not None]
        value = summed(mm(jnp.concatenate(have, axis=1), second_weights(w2_ref, columns)))
        mask = mask_of(cols_ref[o], chans)
        for i in range(hidden // LANES):
            at = (i, pl.ds(o, rows, stride=width), slice(None))
            outf[at] = (outp_ref[at] + value[:, i * LANES : (i + 1) * LANES]) * mask
    step = rows // PIECES
    place = lax.rem(lax.broadcasted_iota(jnp.int32, (step * width, LANES), 0), width)
    edge = (place < 2) | (place >= width - 2)
    copies = []
    for p in range(PIECES):
        at = slice(p * step * width, (p + 1) * step * width)
        for i in range(hidden // LANES):
            lanes = slice(i * LANES, (i + 1) * LANES)
            value = jnp.where(edge, outf[i, at], outp_ref[i, at])
            outb[p * step : (p + 1) * step, :, lanes] = value.reshape(step, width, LANES).astype(BF)
            if p == PIECES - 1:
                slab_ref[:, lanes] = value[(step - 2) * width :]
        here = slice(p * step, (p + 1) * step)
        copies.append(pltpu.make_async_copy(outb.at[here], out_hbm.at[here], sem.at[p]))
        copies[-1].start()
    sea = mask_of(top_ref[0], chans)
    sea_ref[...] = jnp.broadcast_to(sea, sea_ref.shape)
    for copy in copies:
        copy.wait()


def fold(
    at_ref, keep_ref, got_ref, slab_ref, sea_ref, line_ref, own_ref, wt, w1_ref, bias_ref, w2_ref, old_hbm,
    out_hbm, gf, m0, m1, r2, gs, hg, hz, outb, sem,
):
    chans, hidden = w1_ref.shape[2:]
    rows, width, _ = out_hbm.shape
    bias1 = bias_ref[0:1]
    for j in range(3):
        block = jnp.where(at_ref[22 + j] == 0, keep_ref[j], got_ref[j])
        gf[j * 2 * width : (j + 1) * 2 * width] = block.astype(F32)
    for ref in (m0, m1, r2, gs):
        ref[...] = jnp.zeros_like(ref)
    lane = lax.broadcasted_iota(jnp.int32, (1, WIDE), 1)
    sign = jnp.where(lane < chans // 2, -1.0, 1.0).astype(F32)
    for j in range(width + 4):
        at = at_ref[j]
        m0[j : j + 1, :] = gf[pl.ds(at, 1), :]
        north = gf[pl.ds(at + width, 1), :]
        m1[j : j + 1, :] = north
        gs[j : j + 1, :] = north * sign
    r2[...] = own_ref[...] * sign

    def taps(ref, offsets):
        return first_taps([ref[o : o + 16, :].astype(BF) for o in offsets])

    every = (0, 0, 0)
    mixed = mm(
        jnp.concatenate([taps(gs, (0, 1, 2)), taps(r2, (2, 1, 0))], axis=0), first_weights(w1_ref, wt, every, (2,))
    )
    pre = mixed[16:]
    pre += mm(taps(m0, (2, 1, 0)), first_weights(w1_ref, wt, every, (0,)))
    pre += mm(taps(m1, (2, 1, 0)), first_weights(w1_ref, wt, every, (1,)))
    hg[...] = jnp.zeros_like(hg)
    hg[:16, :] = gelu(pre + bias1) * m1[1:17, chans : chans + 1]
    hz[...] = jnp.zeros_like(hz)
    hz[:16, :] = gelu(line_ref[...] + mixed[:16] + bias1) * own_ref[1:17, chans : chans + 1]
    wide = [jnp.concatenate([ref[o : o + 16, :].astype(BF) for o in range(3)], axis=1) for ref in (hz, hg)]
    more = mm(jnp.concatenate(wide, axis=0), second_weights(w2_ref, every, (1, 2)))
    below = more[:width, hidden:]
    level = more[:width, :hidden] + more[16 : 16 + width, hidden:]
    value = slab_ref[...] + jnp.concatenate([below, level], axis=0) * sea_ref[...]
    outb[...] = value.reshape(2, width, hidden).astype(BF)
    copy = pltpu.make_async_copy(outb, out_hbm.at[rows - 2 : rows], sem)
    copy.start()
    copy.wait()


def local(state, ocean_mask, fold_map, w_first, b_first, w_second, b_second):
    rows, width, chans = state.shape
    hidden = w_first.shape[-1]
    n = lax.axis_size("lon")
    me = lax.axis_index("lon")
    assert n >= 8 and n & (n - 1) == 0 and MAIN <= chans < MAIN + SLOT and chans // 2 <= MAIN and width == 8 and rows == MAIN
    held = -(-(chans + 1) // 16) * 16
    smem = pl.BlockSpec(memory_space=pltpu.SMEM)
    vmem = pl.BlockSpec(memory_space=pltpu.VMEM)
    hbm = pl.BlockSpec(memory_space=pltpu.MemorySpace.HBM)
    shape = jax.ShapeDtypeStruct
    scratch = pltpu.VMEM
    dma = pltpu.SemaphoreType.DMA
    place = jnp.full((1,), me, jnp.int32)

    def limit(mib):
        return pltpu.CompilerParams(vmem_limit_bytes=mib << 20)

    def far(value):
        return pltpu.with_memory_space_constraint(value, pltpu.MemorySpace.HBM)

    sent, inner, cols, top, bias, at, w_first, w_second = pl.pallas_call(
        prepare,
        out_shape=(
            shape((2, held, rows), BF),
            shape((2, held + 2 * width, rows), BF),
            shape((width, rows, WIDE), BF),
            shape((1, 2 * width, WIDE), BF),
            shape((2, hidden), F32),
            shape((32,), jnp.int32),
            shape(w_first.shape, BF),
            shape(w_second.shape, BF),
        ),
        in_specs=[smem] + [hbm] * 7,
        out_specs=(vmem,) * 5 + (smem, vmem, vmem),
        scratch_shapes=[
            scratch((chans, width, rows), BF),
            scratch((width, rows), jnp.int32),
            pltpu.SMEM(fold_map.shape, jnp.int32),
            scratch((rows // LANES, held * width, LANES), F32),
            dma((PIECES + 6,)),
        ],
        compiler_params=limit(14),
        name="prepare",
    )(
        place, far(fold_map), far(state.transpose(2, 1, 0)), far(ocean_mask.T),
        far(b_first[None]), far(b_second[None]), far(w_first), far(w_second),
    )
    inner = lax.ppermute(inner, "lon", [(i, i ^ 1) for i in range(n)])

    before = 4
    hid_a, last_a, wt = pl.pallas_call(
        inside_a,
        out_shape=(
            shape((before, rows, hidden), BF),
            shape((8, hidden), F32),
            shape((4 * SLOT, 3 * hidden), BF),
        ),
        in_specs=[vmem] * 3,
        out_specs=(vmem,) * 3,
        compiler_params=limit(12),
        name="inside_a",
    )(cols, w_first, bias)

    def stage_b(after):
        return pl.pallas_call(
            functools.partial(inside_b, before),
            out_shape=(
                shape((width - 2 - before, rows, hidden), BF),
                shape((8, hidden), F32),
                shape((4, rows, hidden), F32),
            ),
            in_specs=[vmem] * 5,
            out_specs=(vmem,) * 3,
            compiler_params=limit(12),
            name="inside_b",
        )(cols, w_first, bias, wt, after)

    def stage_c(hid_b, after):
        return pl.pallas_call(
            functools.partial(inside_c, chans),
            out_shape=shape((hidden // LANES, rows * width, LANES), F32),
            in_specs=[vmem] * 6,
            out_specs=vmem,
            compiler_params=limit(12),
            name="inside_c",
        )(hid_a, hid_b, cols, w_second, bias, after)

    pair = shape((2, 2 * width, WIDE), BF)
    tops, sent = pl.pallas_call(
        join_first,
        out_shape=(pair, shape(sent.shape, BF)),
        in_specs=[vmem] * 4,
        out_specs=(vmem,) * 2,
        input_output_aliases={3: 1},
        compiler_params=limit(4),
        name="join_first",
    )(top, inner, last_a, sent)
    step = 2
    while step < n // 2:
        got = lax.ppermute(tops, "lon", [(i, i ^ step) for i in range(n)])
        if step == 2:
            outer = lax.ppermute(sent, "lon", [(i, (i + 1 if i % 2 else i - 1) % n) for i in range(n)])
        if step == n // 4:
            hid_b, last_b, part = stage_b(tops)
            outp = stage_c(hid_b, last_b)
            break
        tops = pl.pallas_call(
            join,
            out_shape=shape((2 * tops.shape[0],) + tops.shape[1:], BF),
            in_specs=[vmem] * 2,
            out_specs=vmem,
            compiler_params=limit(4),
            name="join",
        )(tops, got)
        step *= 2
    three = shape((3,) + tops.shape[1:], BF)
    give, keep = pl.pallas_call(
        choose,
        out_shape=(three, three),
        in_specs=[smem] + [vmem] * 3,
        out_specs=(vmem,) * 2,
        scratch_shapes=[scratch((2 * tops.shape[0],) + tops.shape[1:], BF)],
        compiler_params=limit(4),
        name="choose",
    )(at, tops, got, outp)
    got = lax.ppermute(give, "lon", [(i, i ^ (n // 2)) for i in range(n)])
    out, slab, sea, line, own = pl.pallas_call(
        border,
        out_shape=(
            shape((rows, width, hidden), BF),
            shape((2 * width, hidden), F32),
            shape((2 * width, hidden), F32),
            shape((16, hidden), F32),
            shape((24, WIDE), F32),
        ),
        in_specs=[smem] + [vmem] * 13,
        out_specs=(hbm,) + (vmem,) * 4,
        scratch_shapes=[
            scratch((4, rows, WIDE), BF),
            scratch((4, rows, hidden), BF),
            scratch((hidden // LANES, rows * width, LANES), F32),
            scratch((rows, width, hidden), BF),
            dma((PIECES,)),
        ],
        compiler_params=limit(16),
        name="border",
    )(place, cols, top, outer, inner, part, last_a, last_b, outp, wt, w_first, bias, w_second, give)
    return pl.pallas_call(
        fold,
        out_shape=shape((rows, width, hidden), BF),
        in_specs=[smem] + [vmem] * 10 + [hbm],
        out_specs=hbm,
        scratch_shapes=[scratch((6 * width, WIDE), F32)]
        + [scratch((24, WIDE), F32)] * 4
        + [scratch((24, hidden), F32)] * 2
        + [scratch((2, width, hidden), BF), dma],
        input_output_aliases={11: 0},
        compiler_params=limit(10),
        name="fold",
    )(at, keep, got, slab, sea, line, own, wt, w_first, bias, w_second, out)


def solution(mesh):
    return jax.shard_map(
        local,
        mesh=mesh,
        in_specs=(P(None, ("grp", "lon"), None), P(None, "lon"), P(), P(), P(), P(), P()),
        out_specs=P(None, ("grp", "lon"), None),
        check_vma=False,
    )
```

```python
import functools

import jax
import jax.numpy as jnp
from jax import lax
from jax.experimental import pallas as pl
from jax.experimental.pallas import tpu as pltpu
from jax.sharding import PartitionSpec as P

BF, F32 = jnp.bfloat16, jnp.float32
LANES, MAIN, SLOT, PIECES = 128, 256, 64, 4
GROUP = 2
WIDE = MAIN + 2 * SLOT


def gelu(value):
    return half_gelu(value, 0.5)


def half_gelu(value, half):
    inner = value * (0.7978845608 + (0.7978845608 * 0.044715) * (value * value))
    scaled = value * half
    return scaled + scaled * jnp.tanh(inner)


def turned(block):
    rows = block.shape[-1]
    tail = block[MAIN : MAIN + SLOT]
    tail = jnp.concatenate([tail, jnp.zeros((SLOT - tail.shape[0], rows), BF)], axis=0)
    full = jnp.concatenate([block[:MAIN], tail, tail], axis=0)
    eye = (
        lax.broadcasted_iota(jnp.int32, (rows, rows), 0) == lax.broadcasted_iota(jnp.int32, (rows, rows), 1)
    ).astype(F32).astype(BF)
    return lax.dot_general(eye, full, (((1,), (1,)), ((), ())), preferred_element_type=F32)


def prepare(
    fold_hbm, x_hbm, mask_hbm, b1_hbm, b2_hbm, w1_hbm, w2_hbm,
    outer_ref, inner_ref, cols_ref, top_ref, bias_ref, pick_ref, w1_ref, w2_ref,
    x_ref, mask_ref, fold_ref, field, sem,
):
    chans, width, rows = x_ref.shape
    held = outer_ref.shape[1]
    me = lax.axis_index("lon")
    cuts = [chans * i // PIECES for i in range(PIECES + 1)]
    pairs = [(mask_hbm, mask_ref)]
    pairs += [(x_hbm.at[lo:hi], x_ref.at[lo:hi]) for lo, hi in zip(cuts, cuts[1:])]
    pairs += [(b1_hbm, bias_ref.at[0:1]), (b2_hbm, bias_ref.at[1:2]), (fold_hbm, fold_ref)]
    pairs += [(w1_hbm, w1_ref), (w2_hbm, w2_ref)]
    copies = [pltpu.make_async_copy(src, dst, sem.at[i]) for i, (src, dst) in enumerate(pairs)]
    for copy in copies:
        copy.start()
    odd = lax.rem(me, 2) == 1
    copies[0].wait()
    mask = mask_ref[...].astype(F32)
    halves = [slice(i * LANES, (i + 1) * LANES) for i in range(rows // LANES)]
    for i, at in enumerate(halves):
        field[i, chans * width : (chans + 1) * width, :] = mask[:, at]
        field[i, (chans + 1) * width :, :] = jnp.zeros(((held - chans - 1) * width, LANES), F32)
    for lo, hi, copy in zip(cuts, cuts[1:], copies[1:]):
        copy.wait()
        for i, at in enumerate(halves):
            block = x_ref[lo:hi, :, at].astype(F32) * mask[None, :, at]
            field[i, lo * width : hi * width, :] = block.reshape((hi - lo) * width, LANES)

    def column(c):
        parts = [field[i, pl.ds(c, held, stride=width), :] for i in range(rows // LANES)]
        return jnp.concatenate(parts, axis=1).astype(BF)

    for c in range(2):
        low, high = column(c), column(width - 2 + c)
        outer_ref[c] = jnp.where(odd, high, low)
        inner_ref[c, :held] = jnp.where(odd, low, high)
    last = []
    for c in range(width):
        out = turned(column(c))
        cols_ref[c] = out.astype(BF)
        last.append(out[rows - 2 :])
    top = jnp.concatenate([v[i : i + 1] for i in range(2) for v in last], axis=0).astype(BF)
    top_ref[0] = top
    inner_ref[0, held:] = top[:, :rows]
    pad = jnp.zeros((2 * width, 2 * rows - WIDE), BF)
    inner_ref[1, held:] = jnp.concatenate([top[:, rows:], pad], axis=1)
    for copy in copies[1 + PIECES :]:
        copy.wait()
    total = fold_ref.shape[0]
    n = total // width
    index = lax.broadcasted_iota(jnp.int32, pick_ref.shape, 0)
    j, line = index & 15, lax.shift_right_logical(index, 4) & 1
    dev = jnp.where(index < 32, lax.bitwise_xor(me, n // 2), me)
    col = fold_ref[0] - width * dev + 2 - j
    col = jnp.where(col < 0, col + total, col)
    col = jnp.where(col < 0, col + total, col)
    col = jnp.where(col >= total, col - total, col)
    block = lax.bitwise_xor(lax.shift_right_logical(col, width.bit_length() - 1), me)
    spot = block * (2 * width) + line * width + (col & (width - 1))
    pick_ref[...] = jnp.where((block < n // 2) & (j < width + 4), spot, -1)


def top_rows(block):
    return jnp.concatenate([block[0], block[1][:, : WIDE - MAIN]], axis=1)


def join_first(mine_ref, got_ref, after_ref, sent_ref, out_ref, pass_ref):
    out_ref[0] = mine_ref[0]
    out_ref[1] = top_rows(got_ref[:, got_ref.shape[1] - mine_ref.shape[1] :])


def join(mine_ref, got_ref, after_ref, out_ref):
    count = mine_ref.shape[0]
    out_ref[:count] = mine_ref[...]
    out_ref[count:] = got_ref[...]


def choose(pick_ref, mine_ref, got_ref, after_ref, give_ref, keep_ref):
    count, lines, wide = mine_ref.shape
    blocks = jnp.concatenate([ref[...].reshape(count * lines, wide) for ref in (mine_ref, got_ref)], axis=0)
    lane = lax.broadcasted_iota(jnp.int32, (pick_ref.shape[0], blocks.shape[0]), 1)
    out = mm((pick_ref[:, :1] == lane).astype(F32).astype(BF), blocks).astype(BF)
    give_ref[...] = out[:32]
    keep_ref[...] = out[32:]


def mm(a, b):
    return jnp.dot(a, b, preferred_element_type=F32)


def mask_of(column, chans):
    return column[:, MAIN:].astype(F32)[:, chans - MAIN : chans - MAIN + 1]


def tail_weights(w1_ref, wt):
    chans, hidden = w1_ref.shape[2:]
    for dy in range(3):
        for dx in range(3):
            rest = jnp.concatenate(
                [w1_ref[dy, dx, MAIN:, :], jnp.zeros((SLOT - chans + MAIN, hidden), BF)], axis=0
            )
            wt[dx * SLOT : (dx + 1) * SLOT, dy * hidden : (dy + 1) * hidden] = rest
    wt[3 * SLOT :, :] = jnp.zeros((SLOT, 3 * hidden), BF)


def first_taps(columns):
    some = next(c for c in columns if c is not None)
    lanes = lax.broadcasted_iota(jnp.int32, (some.shape[0], LANES), 1)
    zero = jnp.zeros((some.shape[0], LANES), BF)
    tail = [zero if c is None else c[:, MAIN:] for c in columns]
    parts = [c[:, :MAIN] for c in columns if c is not None]
    if columns[0] is not None or columns[1] is not None:
        parts.append(jnp.where(lanes < SLOT, tail[0], tail[1]))
    if columns[2] is not None:
        parts.append(tail[2])
    return jnp.concatenate(parts, axis=1)


def first_weights(w1_ref, wt, columns, dys=(0, 1, 2)):
    hidden = w1_ref.shape[3]
    out = []
    for dy in dys:
        at = slice(dy * hidden, (dy + 1) * hidden)
        parts = [w1_ref[dy, dx, :MAIN, :] for dx in range(3) if columns[dx] is not None]
        if columns[0] is not None or columns[1] is not None:
            parts.append(wt[: 2 * SLOT, at])
        if columns[2] is not None:
            parts.append(wt[2 * SLOT :, at])
        out.append(jnp.concatenate(parts, axis=0))
    return jnp.concatenate(out, axis=1)


def second_weights(w2_ref, columns, dys=(0, 1, 2)):
    return jnp.concatenate(
        [
            jnp.concatenate([w2_ref[dy, dx] for dx in range(3) if columns[dx] is not None], axis=0)
            for dy in dys
        ],
        axis=1,
    )


def last_out(value):
    row = lax.broadcasted_iota(jnp.int32, (8, value.shape[1]), 0)
    return jnp.concatenate([value[:-8], jnp.where(row == 7, 0.0, value[-8:])], axis=0)


def summed(p):
    rows, hidden = p.shape[0], p.shape[1] // 3
    row = lax.broadcasted_iota(jnp.int32, (8, hidden), 0)
    south = pltpu.roll(p[:, :hidden], 1, 0)
    south = jnp.concatenate([jnp.where(row == 0, 0.0, south[:8]), south[8:]], axis=0)
    return p[:, hidden : 2 * hidden] + south + last_out(pltpu.roll(p[:, 2 * hidden :], rows - 1, 0))


def edges(width):
    return (0, 1, width, width + 1)


def own_column(cols_ref, j):
    return cols_ref[j - 2] if 2 <= j < 2 + cols_ref.shape[0] else None


def hidden_columns(cols_ref, w1_ref, bias_ref, wt, hid_ref, last_ref, first, part_ref, more):
    chans, _ = w1_ref.shape[2:]
    rows = cols_ref.shape[1]
    last_ref[...] = jnp.zeros_like(last_ref)
    for i in range(0, hid_ref.shape[0], GROUP):
        sets = [[own_column(cols_ref, first + i + g + dx) for dx in range(3)] for g in range(GROUP)]
        lhs = jnp.concatenate([first_taps(columns) for columns in sets], axis=0)
        out = mm(lhs, first_weights(w1_ref, wt, sets[0]))
        for g in range(GROUP):
            value = summed(out[g * rows : (g + 1) * rows])
            last_ref[i + g : i + g + 1, :] = value[rows - 1 :]
            value = half_gelu(value + bias_ref[0:1], 0.5 * mask_of(sets[g][1], chans))
            hid_ref[i + g] = last_out(value).astype(BF)
    for i, h in enumerate(more):
        columns = [own_column(cols_ref, h + dx) for dx in range(3)]
        part_ref[i] = summed(mm(first_taps(columns), first_weights(w1_ref, wt, columns)))


def inside_a(cols_ref, w1_ref, bias_ref, hid_ref, last_ref, wt_ref, part_ref):
    tail_weights(w1_ref, wt_ref)
    width = cols_ref.shape[0]
    hidden_columns(cols_ref, w1_ref, bias_ref, wt_ref, hid_ref, last_ref, 2, part_ref, edges(width)[:1])


def inside_b(before, cols_ref, w1_ref, bias_ref, wt_ref, after_ref, hid_ref, last_ref, part_ref):
    width = cols_ref.shape[0]
    hidden_columns(cols_ref, w1_ref, bias_ref, wt_ref, hid_ref, last_ref, 2 + before, part_ref, edges(width)[1:])


def inside_c(chans, hid_a, hid_b, cols_ref, w2_ref, bias_ref, after_ref, out_ref):
    width, rows, _ = cols_ref.shape
    hidden = w2_ref.shape[3]
    before = hid_a.shape[0]

    def hid(h):
        if not 2 <= h < width:
            return None
        return hid_a[h - 2] if h - 2 < before else hid_b[h - 2 - before]

    def put(o, value):
        for i in range(hidden // LANES):
            out_ref[i, pl.ds(o, rows, stride=width), :] = value[:, i * LANES : (i + 1) * LANES]

    def lhs(columns):
        return jnp.concatenate([c for c in columns if c is not None], axis=1)

    for o in range(2, width - 2, GROUP):
        sets = [[hid(o + g + dx) for dx in range(3)] for g in range(GROUP)]
        out = mm(jnp.concatenate([lhs(c) for c in sets], axis=0), second_weights(w2_ref, sets[0]))
        for g in range(GROUP):
            value = summed(out[g * rows : (g + 1) * rows]) + bias_ref[1:2]
            put(o + g, value * mask_of(cols_ref[o + g], chans))
    for o in (0, 1, width - 2, width - 1):
        columns = [hid(o + dx) for dx in range(3)]
        put(o, summed(mm(lhs(columns), second_weights(w2_ref, columns))) + bias_ref[1:2])


def border(
    cols_ref, top_ref, outer_ref, inner_ref, part_a, part_b, last_a, last_b, outp_ref, wt, w1_ref, bias_ref, w2_ref,
    after_ref, out_hbm, slab_ref, sea_ref, line_ref, own_ref, hx, hid, outf, outb, sem,
):
    chans, hidden = w1_ref.shape[2:]
    width, rows, _ = cols_ref.shape
    held = outer_ref.shape[1]
    odd = lax.rem(lax.axis_index("lon"), 2) == 1
    for c in range(2):
        hx[c] = turned(jnp.where(odd, inner_ref[c, :held], outer_ref[c])).astype(BF)
        hx[2 + c] = turned(jnp.where(odd, outer_ref[c], inner_ref[c, :held])).astype(BF)

    def column(j):
        return hx[j] if j < 2 else cols_ref[j - 2] if j < 2 + width else hx[j - width]

    own_ref[...] = jnp.zeros_like(own_ref)
    for j in range(width + 4):
        own_ref[j : j + 1, :] = column(j)[rows - 16 :].astype(F32)[15:16]
    bias1 = bias_ref[0:1]
    line_ref[...] = jnp.zeros_like(line_ref)
    line_ref[2:6] = last_a[:4]
    line_ref[6:width] = last_b[: width - 6]
    for i, h in enumerate(edges(width)):
        columns = [column(h + dx) if not 2 <= h + dx < 2 + width else None for dx in range(3)]
        value = (part_a[0] if i == 0 else part_b[i - 1]) + summed(mm(first_taps(columns), first_weights(w1_ref, wt, columns)))
        line_ref[h : h + 1, :] = value[rows - 1 :]
        value = half_gelu(value + bias1, 0.5 * mask_of(column(h + 1), chans))
        hid[i] = last_out(value).astype(BF)
    for o in (0, 1, width - 2, width - 1):
        columns = [hid[edges(width).index(o + dx)] if o + dx in edges(width) else None for dx in range(3)]
        have = [c for c in columns if c is not None]
        value = summed(mm(jnp.concatenate(have, axis=1), second_weights(w2_ref, columns)))
        mask = mask_of(cols_ref[o], chans)
        for i in range(hidden // LANES):
            at = (i, pl.ds(o, rows, stride=width), slice(None))
            outf[at] = (outp_ref[at] + value[:, i * LANES : (i + 1) * LANES]) * mask
    step = rows // PIECES
    place = lax.rem(lax.broadcasted_iota(jnp.int32, (step * width, LANES), 0), width)
    edge = (place < 2) | (place >= width - 2)
    copies = []
    for p in range(PIECES):
        at = slice(p * step * width, (p + 1) * step * width)
        for i in range(hidden // LANES):
            lanes = slice(i * LANES, (i + 1) * LANES)
            value = jnp.where(edge, outf[i, at], outp_ref[i, at])
            outb[p * step : (p + 1) * step, :, lanes] = value.reshape(step, width, LANES).astype(BF)
            if p == PIECES - 1:
                slab_ref[:, lanes] = value[(step - 2) * width :]
        here = slice(p * step, (p + 1) * step)
        copies.append(pltpu.make_async_copy(outb.at[here], out_hbm.at[here], sem.at[p]))
        copies[-1].start()
    sea = mask_of(top_ref[0], chans)
    sea_ref[...] = jnp.broadcast_to(sea, sea_ref.shape)
    for copy in copies:
        copy.wait()


def fold(
    keep_ref, got_ref, slab_ref, sea_ref, line_ref, own_ref, wt, w1_ref, bias_ref, w2_ref, old_hbm,
    out_hbm, m0, m1, r2, gs, hg, hz, outb, sem,
):
    chans, hidden = w1_ref.shape[2:]
    rows, width, _ = out_hbm.shape
    bias1 = bias_ref[0:1]
    lane = lax.broadcasted_iota(jnp.int32, (1, WIDE), 1)
    sign = jnp.where(lane < chans // 2, -1.0, 1.0).astype(F32)
    both = keep_ref[...].astype(F32) + got_ref[...].astype(F32)
    for ref, value in ((m0, both[:16]), (m1, both[16:]), (gs, both[16:] * sign)):
        ref[:16] = value
        ref[16:] = jnp.zeros_like(ref[16:])
    r2[...] = own_ref[...] * sign

    def taps(ref, offsets):
        return first_taps([ref[o : o + 16, :].astype(BF) for o in offsets])

    every = (0, 0, 0)
    mixed = mm(
        jnp.concatenate([taps(gs, (0, 1, 2)), taps(r2, (2, 1, 0))], axis=0), first_weights(w1_ref, wt, every, (2,))
    )
    pre = mixed[16:]
    pre += mm(taps(m0, (2, 1, 0)), first_weights(w1_ref, wt, every, (0,)))
    pre += mm(taps(m1, (2, 1, 0)), first_weights(w1_ref, wt, every, (1,)))
    hg[...] = jnp.zeros_like(hg)
    hg[:16, :] = gelu(pre + bias1) * m1[1:17, chans : chans + 1]
    hz[...] = jnp.zeros_like(hz)
    hz[:16, :] = gelu(line_ref[...] + mixed[:16] + bias1) * own_ref[1:17, chans : chans + 1]
    wide = [jnp.concatenate([ref[o : o + 16, :].astype(BF) for o in range(3)], axis=1) for ref in (hz, hg)]
    more = mm(jnp.concatenate(wide, axis=0), second_weights(w2_ref, every, (1, 2)))
    below = more[:width, hidden:]
    level = more[:width, :hidden] + more[16 : 16 + width, hidden:]
    value = slab_ref[...] + jnp.concatenate([below, level], axis=0) * sea_ref[...]
    outb[...] = value.reshape(2, width, hidden).astype(BF)
    copy = pltpu.make_async_copy(outb, out_hbm.at[rows - 2 : rows], sem)
    copy.start()
    copy.wait()


def local(state, ocean_mask, fold_map, w_first, b_first, w_second, b_second):
    rows, width, chans = state.shape
    hidden = w_first.shape[-1]
    n = lax.axis_size("lon")
    assert n >= 8 and n & (n - 1) == 0 and MAIN <= chans < MAIN + SLOT and chans // 2 <= MAIN and width == 8 and rows == MAIN
    held = -(-(chans + 1) // 16) * 16
    vmem = pl.BlockSpec(memory_space=pltpu.VMEM)
    hbm = pl.BlockSpec(memory_space=pltpu.MemorySpace.HBM)
    shape = jax.ShapeDtypeStruct
    scratch = pltpu.VMEM
    dma = pltpu.SemaphoreType.DMA

    def limit(mib):
        return pltpu.CompilerParams(vmem_limit_bytes=mib << 20)

    def far(value):
        return pltpu.with_memory_space_constraint(value, pltpu.MemorySpace.HBM)

    sent, inner, cols, top, bias, pick, w_first, w_second = pl.pallas_call(
        prepare,
        out_shape=(
            shape((2, held, rows), BF),
            shape((2, held + 2 * width, rows), BF),
            shape((width, rows, WIDE), BF),
            shape((1, 2 * width, WIDE), BF),
            shape((2, hidden), F32),
            shape((64, LANES), jnp.int32),
            shape(w_first.shape, BF),
            shape(w_second.shape, BF),
        ),
        in_specs=[hbm] * 7,
        out_specs=(vmem,) * 8,
        scratch_shapes=[
            scratch((chans, width, rows), BF),
            scratch((width, rows), jnp.int32),
            pltpu.SMEM(fold_map.shape, jnp.int32),
            scratch((rows // LANES, held * width, LANES), F32),
            dma((PIECES + 6,)),
        ],
        compiler_params=limit(14),
        name="prepare",
    )(
        far(fold_map), far(state.transpose(2, 1, 0)), far(ocean_mask.T),
        far(b_first[None]), far(b_second[None]), far(w_first), far(w_second),
    )
    inner = lax.ppermute(inner, "lon", [(i, i ^ 1) for i in range(n)])

    before = 4
    hid_a, last_a, wt, part_a = pl.pallas_call(
        inside_a,
        out_shape=(
            shape((before, rows, hidden), BF),
            shape((8, hidden), F32),
            shape((4 * SLOT, 3 * hidden), BF),
            shape((1, rows, hidden), F32),
        ),
        in_specs=[vmem] * 3,
        out_specs=(vmem,) * 4,
        compiler_params=limit(12),
        name="inside_a",
    )(cols, w_first, bias)

    def stage_b(after):
        return pl.pallas_call(
            functools.partial(inside_b, before),
            out_shape=(
                shape((width - 2 - before, rows, hidden), BF),
                shape((8, hidden), F32),
                shape((3, rows, hidden), F32),
            ),
            in_specs=[vmem] * 5,
            out_specs=(vmem,) * 3,
            compiler_params=limit(12),
            name="inside_b",
        )(cols, w_first, bias, wt, after)

    def stage_c(hid_b, after):
        return pl.pallas_call(
            functools.partial(inside_c, chans),
            out_shape=shape((hidden // LANES, rows * width, LANES), F32),
            in_specs=[vmem] * 6,
            out_specs=vmem,
            compiler_params=limit(12),
            name="inside_c",
        )(hid_a, hid_b, cols, w_second, bias, after)

    pair = shape((2, 2 * width, WIDE), BF)
    tops, sent = pl.pallas_call(
        join_first,
        out_shape=(pair, shape(sent.shape, BF)),
        in_specs=[vmem] * 4,
        out_specs=(vmem,) * 2,
        input_output_aliases={3: 1},
        compiler_params=limit(4),
        name="join_first",
    )(top, inner, last_a, sent)
    step = 2
    while step < n // 2:
        got = lax.ppermute(tops, "lon", [(i, i ^ step) for i in range(n)])
        if step == 2:
            outer = lax.ppermute(sent, "lon", [(i, (i + 1 if i % 2 else i - 1) % n) for i in range(n)])
            hid_b, last_b, part_b = stage_b(tops)
        if step == n // 4:
            outp = stage_c(hid_b, tops)
            break
        tops = pl.pallas_call(
            join,
            out_shape=shape((2 * tops.shape[0],) + tops.shape[1:], BF),
            in_specs=[vmem] * 3,
            out_specs=vmem,
            compiler_params=limit(4),
            name="join",
        )(tops, got, last_b)
        step *= 2
    lines = shape((32, WIDE), BF)
    give, keep = pl.pallas_call(
        choose,
        out_shape=(lines, lines),
        in_specs=[vmem] * 4,
        out_specs=(vmem,) * 2,
        compiler_params=limit(4),
        name="choose",
    )(pick, tops, got, outp)
    got = lax.ppermute(give, "lon", [(i, i ^ (n // 2)) for i in range(n)])
    out, slab, sea, line, own = pl.pallas_call(
        border,
        out_shape=(
            shape((rows, width, hidden), BF),
            shape((2 * width, hidden), F32),
            shape((2 * width, hidden), F32),
            shape((16, hidden), F32),
            shape((24, WIDE), F32),
        ),
        in_specs=[vmem] * 14,
        out_specs=(hbm,) + (vmem,) * 4,
        scratch_shapes=[
            scratch((4, rows, WIDE), BF),
            scratch((4, rows, hidden), BF),
            scratch((hidden // LANES, rows * width, LANES), F32),
            scratch((rows, width, hidden), BF),
            dma((PIECES,)),
        ],
        compiler_params=limit(16),
        name="border",
    )(cols, top, outer, inner, part_a, part_b, last_a, last_b, outp, wt, w_first, bias, w_second, give)
    return pl.pallas_call(
        fold,
        out_shape=shape((rows, width, hidden), BF),
        in_specs=[vmem] * 10 + [hbm],
        out_specs=hbm,
        scratch_shapes=[scratch((24, WIDE), F32)] * 4
        + [scratch((24, hidden), F32)] * 2
        + [scratch((2, width, hidden), BF), dma],
        input_output_aliases={10: 0},
        compiler_params=limit(10),
        name="fold",
    )(keep, got, slab, sea, line, own, wt, w_first, bias, w_second, out)


def solution(mesh):
    return jax.shard_map(
        local,
        mesh=mesh,
        in_specs=(P(None, ("grp", "lon"), None), P(None, "lon"), P(), P(), P(), P(), P()),
        out_specs=P(None, ("grp", "lon"), None),
        check_vma=False,
    )
```

```python
import functools

import jax
import jax.numpy as jnp
from jax import lax
from jax.experimental import pallas as pl
from jax.experimental.pallas import tpu as pltpu
from jax.sharding import PartitionSpec as P

BF, F32 = jnp.bfloat16, jnp.float32
LANES, MAIN, SLOT, PIECES = 128, 256, 64, 4
GROUP = 2
WIDE = MAIN + 2 * SLOT


def gelu(value):
    return half_gelu(value, 0.5)


def half_gelu(value, half):
    inner = value * (0.7978845608 + (0.7978845608 * 0.044715) * (value * value))
    scaled = value * half
    return scaled + scaled * jnp.tanh(inner)


def turned(block):
    rows = block.shape[-1]
    tail = block[MAIN : MAIN + SLOT]
    tail = jnp.concatenate([tail, jnp.zeros((SLOT - tail.shape[0], rows), BF)], axis=0)
    full = jnp.concatenate([block[:MAIN], tail, tail], axis=0)
    eye = (
        lax.broadcasted_iota(jnp.int32, (rows, rows), 0) == lax.broadcasted_iota(jnp.int32, (rows, rows), 1)
    ).astype(F32).astype(BF)
    return lax.dot_general(eye, full, (((1,), (1,)), ((), ())), preferred_element_type=F32)


def prepare(
    fold_hbm, x_hbm, mask_hbm, b1_hbm, b2_hbm, w1_hbm, w2_hbm,
    outer_ref, inner_ref, cols_ref, top_ref, bias_ref, pick_ref, w1_ref, w2_ref,
    x_ref, mask_ref, fold_ref, field, sem,
):
    chans, width, rows = x_ref.shape
    held = field.shape[1] // width
    me = lax.axis_index("lon")
    cuts = [chans * i // PIECES for i in range(PIECES + 1)]
    pairs = [(mask_hbm, mask_ref)]
    pairs += [(x_hbm.at[lo:hi], x_ref.at[lo:hi]) for lo, hi in zip(cuts, cuts[1:])]
    pairs += [(b1_hbm, bias_ref.at[0:1]), (b2_hbm, bias_ref.at[1:2]), (fold_hbm, fold_ref)]
    pairs += [(w1_hbm, w1_ref), (w2_hbm, w2_ref)]
    copies = [pltpu.make_async_copy(src, dst, sem.at[i]) for i, (src, dst) in enumerate(pairs)]
    for copy in copies:
        copy.start()
    odd = lax.rem(me, 2) == 1
    copies[0].wait()
    mask = mask_ref[...].astype(F32)
    halves = [slice(i * LANES, (i + 1) * LANES) for i in range(rows // LANES)]
    for i, at in enumerate(halves):
        field[i, chans * width : (chans + 1) * width, :] = mask[:, at]
        field[i, (chans + 1) * width :, :] = jnp.zeros(((held - chans - 1) * width, LANES), F32)
    for lo, hi, copy in zip(cuts, cuts[1:], copies[1:]):
        copy.wait()
        for i, at in enumerate(halves):
            block = x_ref[lo:hi, :, at].astype(F32) * mask[None, :, at]
            field[i, lo * width : hi * width, :] = block.reshape((hi - lo) * width, LANES)

    def column(c):
        parts = [field[i, pl.ds(c, held, stride=width), :] for i in range(rows // LANES)]
        return jnp.concatenate(parts, axis=1).astype(BF)

    last = []
    for c in range(width):
        out = turned(column(c))
        cols_ref[c] = out.astype(BF)
        last.append(out[rows - 2 :])
    lanes = lax.broadcasted_iota(jnp.int32, (rows, LANES), 1)

    def message(c):
        first, second = cols_ref[c], cols_ref[c + 1]
        rest = jnp.where(lanes < SLOT, first[:, MAIN:][:, :LANES], second[:, MAIN:][:, :LANES])
        return jnp.concatenate([first[:, :MAIN], second[:, :MAIN], rest], axis=1)

    low, high = message(0), message(width - 2)
    outer_ref[...] = jnp.where(odd, high, low)
    inner_ref[:rows] = jnp.where(odd, low, high)
    top = jnp.concatenate([v[i : i + 1] for i in range(2) for v in last], axis=0).astype(BF)
    top_ref[0] = top
    inner_ref[rows:] = jnp.concatenate([top, jnp.zeros((2 * width, inner_ref.shape[1] - WIDE), BF)], axis=1)
    for copy in copies[1 + PIECES :]:
        copy.wait()
    total = fold_ref.shape[0]
    n = total // width
    index = lax.broadcasted_iota(jnp.int32, pick_ref.shape, 0)
    j, line = index & 15, lax.shift_right_logical(index, 4) & 1
    dev = jnp.where(index < 32, lax.bitwise_xor(me, n // 2), me)
    col = fold_ref[0] - width * dev + 2 - j
    col = jnp.where(col < 0, col + total, col)
    col = jnp.where(col < 0, col + total, col)
    col = jnp.where(col >= total, col - total, col)
    block = lax.bitwise_xor(lax.shift_right_logical(col, width.bit_length() - 1), me)
    spot = block * (2 * width) + line * width + (col & (width - 1))
    pick_ref[...] = jnp.where((block < n // 2) & (j < width + 4), spot, -1)


def join_first(mine_ref, got_ref, after_ref, sent_ref, out_ref, pass_ref):
    out_ref[0] = mine_ref[0]
    out_ref[1] = got_ref[got_ref.shape[0] - mine_ref.shape[1] :, :WIDE]


def join(mine_ref, got_ref, out_ref):
    count = mine_ref.shape[0]
    out_ref[:count] = mine_ref[...]
    out_ref[count:] = got_ref[...]


def choose(pick_ref, mine_ref, got_ref, after_ref, give_ref, keep_ref):
    count, lines, wide = mine_ref.shape
    blocks = jnp.concatenate([ref[...].reshape(count * lines, wide) for ref in (mine_ref, got_ref)], axis=0)
    lane = lax.broadcasted_iota(jnp.int32, (pick_ref.shape[0], blocks.shape[0]), 1)
    out = mm((pick_ref[:, :1] == lane).astype(F32).astype(BF), blocks).astype(BF)
    give_ref[...] = out[:32]
    keep_ref[...] = out[32:]


def mm(a, b):
    return jnp.dot(a, b, preferred_element_type=F32)


def mask_of(column, chans):
    return column[:, MAIN:].astype(F32)[:, chans - MAIN : chans - MAIN + 1]


def tail_weights(w1_ref, wt):
    chans, hidden = w1_ref.shape[2:]
    for dy in range(3):
        for dx in range(3):
            rest = jnp.concatenate(
                [w1_ref[dy, dx, MAIN:, :], jnp.zeros((SLOT - chans + MAIN, hidden), BF)], axis=0
            )
            wt[(dx + 1) * SLOT : (dx + 2) * SLOT, dy * hidden : (dy + 1) * hidden] = rest
    for at in (0, 4 * SLOT):
        wt[at : at + SLOT, :] = jnp.zeros((SLOT, 3 * hidden), BF)


def first_taps(columns):
    some = next(c for c in columns if c is not None)
    lanes = lax.broadcasted_iota(jnp.int32, (some.shape[0], LANES), 1)
    zero = jnp.zeros((some.shape[0], LANES), BF)
    tail = [zero if c is None else c[:, MAIN:] for c in columns]
    parts = [c[:, :MAIN] for c in columns if c is not None]
    if columns[0] is not None or columns[1] is not None:
        parts.append(jnp.where(lanes < SLOT, tail[0], tail[1]))
    if columns[2] is not None:
        parts.append(tail[2])
    return jnp.concatenate(parts, axis=1)


def first_weights(w1_ref, wt, columns, dys=(0, 1, 2)):
    hidden = w1_ref.shape[3]
    out = []
    for dy in dys:
        at = slice(dy * hidden, (dy + 1) * hidden)
        parts = [w1_ref[dy, dx, :MAIN, :] for dx in range(3) if columns[dx] is not None]
        if columns[0] is not None or columns[1] is not None:
            parts.append(wt[SLOT : 3 * SLOT, at])
        if columns[2] is not None:
            parts.append(wt[3 * SLOT :, at])
        out.append(jnp.concatenate(parts, axis=0))
    return jnp.concatenate(out, axis=1)


def second_weights(w2_ref, columns, dys=(0, 1, 2)):
    return jnp.concatenate(
        [
            jnp.concatenate([w2_ref[dy, dx] for dx in range(3) if columns[dx] is not None], axis=0)
            for dy in dys
        ],
        axis=1,
    )


def last_out(value):
    row = lax.broadcasted_iota(jnp.int32, (8, value.shape[1]), 0)
    return jnp.concatenate([value[:-8], jnp.where(row == 7, 0.0, value[-8:])], axis=0)


def summed(p):
    rows, hidden = p.shape[0], p.shape[1] // 3
    row = lax.broadcasted_iota(jnp.int32, (8, hidden), 0)
    south = pltpu.roll(p[:, :hidden], 1, 0)
    south = jnp.concatenate([jnp.where(row == 0, 0.0, south[:8]), south[8:]], axis=0)
    return p[:, hidden : 2 * hidden] + south + last_out(pltpu.roll(p[:, 2 * hidden :], rows - 1, 0))


def edges(width):
    return (0, 1, width, width + 1)


def own_column(cols_ref, j):
    return cols_ref[j - 2] if 2 <= j < 2 + cols_ref.shape[0] else None


def hidden_columns(cols_ref, w1_ref, bias_ref, wt, hid_ref, last_ref, first, part_ref, more):
    chans, _ = w1_ref.shape[2:]
    rows = cols_ref.shape[1]
    last_ref[...] = jnp.zeros_like(last_ref)
    for i in range(0, hid_ref.shape[0], GROUP):
        sets = [[own_column(cols_ref, first + i + g + dx) for dx in range(3)] for g in range(GROUP)]
        lhs = jnp.concatenate([first_taps(columns) for columns in sets], axis=0)
        out = mm(lhs, first_weights(w1_ref, wt, sets[0]))
        for g in range(GROUP):
            value = summed(out[g * rows : (g + 1) * rows])
            last_ref[i + g : i + g + 1, :] = value[rows - 1 :]
            value = half_gelu(value + bias_ref[0:1], 0.5 * mask_of(sets[g][1], chans))
            hid_ref[i + g] = last_out(value).astype(BF)
    for i, h in enumerate(more):
        columns = [own_column(cols_ref, h + dx) for dx in range(3)]
        part_ref[i] = summed(mm(first_taps(columns), first_weights(w1_ref, wt, columns)))


def inside_a(cols_ref, w1_ref, bias_ref, hid_ref, last_ref, wt_ref, part_ref):
    tail_weights(w1_ref, wt_ref)
    width = cols_ref.shape[0]
    hidden_columns(cols_ref, w1_ref, bias_ref, wt_ref, hid_ref, last_ref, 2, part_ref, edges(width)[:1])


def inside_b(before, cols_ref, w1_ref, bias_ref, wt_ref, after_ref, hid_ref, last_ref, part_ref):
    width = cols_ref.shape[0]
    hidden_columns(cols_ref, w1_ref, bias_ref, wt_ref, hid_ref, last_ref, 2 + before, part_ref, edges(width)[1:])


def second_columns(chans, todo, hid_a, hid_b, cols_ref, w2_ref, bias_ref, out_ref):
    width, rows, _ = cols_ref.shape
    hidden = w2_ref.shape[3]
    before = hid_a.shape[0]

    def hid(h):
        if not 2 <= h < width:
            return None
        return hid_a[h - 2] if h - 2 < before else hid_b[h - 2 - before]

    def put(o, value):
        for i in range(hidden // LANES):
            out_ref[i, pl.ds(o, rows, stride=width), :] = value[:, i * LANES : (i + 1) * LANES]

    def lhs(columns):
        return jnp.concatenate([c for c in columns if c is not None], axis=1)

    for group in todo:
        sets = [[hid(o + dx) for dx in range(3)] for o in group]
        out = mm(jnp.concatenate([lhs(c) for c in sets], axis=0), second_weights(w2_ref, sets[0]))
        for g, o in enumerate(group):
            value = summed(out[g * rows : (g + 1) * rows]) + bias_ref[1:2]
            if 2 <= o < width - 2:
                value = value * mask_of(cols_ref[o], chans)
            put(o, value)


def inside_c(chans, hid_a, hid_b, cols_ref, w2_ref, bias_ref, after_ref, out_ref):
    width = cols_ref.shape[0]
    todo = ((2, 3), (4, 5), (0,), (1,), (width - 2,), (width - 1,))
    second_columns(chans, todo, hid_a, hid_b, cols_ref, w2_ref, bias_ref, out_ref)


def border(
    cols_ref, outer_ref, inner_ref, part_a, part_b, last_a, last_b, outp_ref, wt, w1_ref, bias_ref, w2_ref, after_ref,
    outf, line, own, hx, hid,
):
    chans, hidden = w1_ref.shape[2:]
    width, rows, _ = cols_ref.shape
    rest = 2 * MAIN
    odd = lax.rem(lax.axis_index("lon"), 2) == 1
    bias1 = bias_ref[0:1]
    outer, inner = outer_ref[...], inner_ref[:rows]
    hx[0] = jnp.where(odd, inner, outer)
    hx[1] = jnp.where(odd, outer, inner)

    at = edges(width)
    taken = (
        (0, slice(0, rest), (0, 1), 1),
        (0, slice(MAIN, rest), (0,), 0),
        (1, slice(0, MAIN), (2,), 3),
        (1, slice(0, rest), (1, 2), 2),
    )
    line[...] = jnp.zeros_like(line)
    line[2 : 2 + 4] = last_a[:4]
    line[6:width] = last_b[: width - 6]
    for i, (side, main, dxs, slot) in enumerate(taken):
        lhs = jnp.concatenate([hx[side, :, main], hx[side, :, rest:]], axis=1)
        rhs = []
        for dy in range(3):
            block = wt[slot * SLOT : (slot + 2) * SLOT, dy * hidden : (dy + 1) * hidden]
            rhs.append(jnp.concatenate([w1_ref[dy, dx, :MAIN, :] for dx in dxs] + [block], axis=0))
        value = (part_a[0] if i == 0 else part_b[i - 1]) + summed(mm(lhs, jnp.concatenate(rhs, axis=1)))
        line[at[i] : at[i] + 1, :] = value[rows - 1 :]
        sea = chans - MAIN
        if i == 0:
            mask = hx[0, :, rest:].astype(F32)[:, SLOT + sea : SLOT + sea + 1]
        elif i == 3:
            mask = hx[1, :, rest:].astype(F32)[:, sea : sea + 1]
        else:
            mask = mask_of(cols_ref[at[i] - 1], chans)
        hid[i] = last_out(half_gelu(value + bias1, 0.5 * mask)).astype(BF)

    for o in (0, 1, width - 2, width - 1):
        columns = [hid[at.index(o + dx)] if o + dx in at else None for dx in range(3)]
        have = [c for c in columns if c is not None]
        value = summed(mm(jnp.concatenate(have, axis=1), second_weights(w2_ref, columns)))
        mask = mask_of(cols_ref[o], chans)
        for i in range(hidden // LANES):
            to = (i, pl.ds(o, rows, stride=width), slice(None))
            outf[to] = (outp_ref[to] + value[:, i * LANES : (i + 1) * LANES]) * mask
    own[...] = jnp.zeros_like(own)
    for j in range(width):
        own[2 + j : 3 + j, :] = cols_ref[j, rows - 16 :].astype(F32)[15:16]
    half = lax.broadcasted_iota(jnp.int32, (8, LANES), 1) < SLOT
    for side, first in ((0, 0), (1, 2 + width)):
        end = hx[side, rows - 16 :].astype(F32)[8:16]
        tail = end[:, rest:]
        turn = pltpu.roll(tail, SLOT, 1)
        for c, both_halves in enumerate((jnp.where(half, tail, turn), jnp.where(half, turn, tail))):
            full = jnp.concatenate([end[:, c * MAIN : (c + 1) * MAIN], both_halves], axis=1)
            own[first + c : first + c + 1, :] = full[7:8]


def finish(
    keep_ref, got_ref, top_ref, outp_ref, outf, line, own, wt, w1_ref, bias_ref, w2_ref,
    out_hbm, m0, m1, r2, gs, hg, hz, outb, sem,
):
    chans, hidden = w1_ref.shape[2:]
    rows, width, _ = out_hbm.shape
    bias1 = bias_ref[0:1]
    step = rows // PIECES
    place = lax.rem(lax.broadcasted_iota(jnp.int32, (step * width, LANES), 0), width)
    edge = (place < 2) | (place >= width - 2)
    copies = []

    def assemble(p, more):
        here = slice(p * step, (p + 1) * step)
        lines = slice(p * step * width, (p + 1) * step * width)
        for i in range(hidden // LANES):
            lanes = slice(i * LANES, (i + 1) * LANES)
            value = jnp.where(edge, outf[i, lines], outp_ref[i, lines])
            if more is not None:
                end = (step - 2) * width
                value = jnp.concatenate([value[:end], value[end:] + more[:, lanes]], axis=0)
            outb[here, :, lanes] = value.reshape(step, width, LANES).astype(BF)
        copies.append(pltpu.make_async_copy(outb.at[here], out_hbm.at[here], sem.at[p]))
        copies[-1].start()

    for p in range(PIECES - 1):
        assemble(p, None)
    lane = lax.broadcasted_iota(jnp.int32, (1, WIDE), 1)
    sign = jnp.where(lane < chans // 2, -1.0, 1.0).astype(F32)
    both = keep_ref[...].astype(F32) + got_ref[...].astype(F32)
    for ref, value in ((m0, both[:16]), (m1, both[16:]), (gs, both[16:] * sign)):
        ref[:16] = value
        ref[16:] = jnp.zeros_like(ref[16:])
    r2[...] = own[...] * sign

    def taps(ref, offsets):
        return first_taps([ref[o : o + 16, :].astype(BF) for o in offsets])

    every = (0, 0, 0)
    mixed = mm(
        jnp.concatenate([taps(gs, (0, 1, 2)), taps(r2, (2, 1, 0))], axis=0), first_weights(w1_ref, wt, every, (2,))
    )
    pre = mixed[16:]
    pre += mm(taps(m0, (2, 1, 0)), first_weights(w1_ref, wt, every, (0,)))
    pre += mm(taps(m1, (2, 1, 0)), first_weights(w1_ref, wt, every, (1,)))
    hg[16:] = jnp.zeros_like(hg[16:])
    hg[:16] = gelu(pre + bias1) * m1[1:17, chans : chans + 1]
    hz[16:] = jnp.zeros_like(hz[16:])
    hz[:16] = gelu(line[...] + mixed[:16] + bias1) * own[1:17, chans : chans + 1]
    wide = [jnp.concatenate([ref[o : o + 16, :].astype(BF) for o in range(3)], axis=1) for ref in (hz, hg)]
    more = mm(jnp.concatenate(wide, axis=0), second_weights(w2_ref, every, (1, 2)))
    below = more[:width, hidden:]
    level = more[:width, :hidden] + more[16 : 16 + width, hidden:]
    fixed = jnp.concatenate([below, level], axis=0) * mask_of(top_ref[0], chans)

    assemble(PIECES - 1, fixed)
    for copy in copies:
        copy.wait()


def local(state, ocean_mask, fold_map, w_first, b_first, w_second, b_second):
    rows, width, chans = state.shape
    hidden = w_first.shape[-1]
    n = lax.axis_size("lon")
    assert n >= 8 and n & (n - 1) == 0 and MAIN <= chans < MAIN + SLOT and chans // 2 <= MAIN and width == 8 and rows == MAIN
    held = -(-(chans + 1) // 16) * 16
    vmem = pl.BlockSpec(memory_space=pltpu.VMEM)
    hbm = pl.BlockSpec(memory_space=pltpu.MemorySpace.HBM)
    shape = jax.ShapeDtypeStruct
    scratch = pltpu.VMEM
    dma = pltpu.SemaphoreType.DMA

    def limit(mib):
        return pltpu.CompilerParams(vmem_limit_bytes=mib << 20)

    def far(value):
        return pltpu.with_memory_space_constraint(value, pltpu.MemorySpace.HBM)

    sent, inner, cols, top, bias, pick, w_first, w_second = pl.pallas_call(
        prepare,
        out_shape=(
            shape((rows, 2 * MAIN + LANES), BF),
            shape((rows + 2 * width, 2 * MAIN + LANES), BF),
            shape((width, rows, WIDE), BF),
            shape((1, 2 * width, WIDE), BF),
            shape((2, hidden), F32),
            shape((64, LANES), jnp.int32),
            shape(w_first.shape, BF),
            shape(w_second.shape, BF),
        ),
        in_specs=[hbm] * 7,
        out_specs=(vmem,) * 8,
        scratch_shapes=[
            scratch((chans, width, rows), BF),
            scratch((width, rows), jnp.int32),
            pltpu.SMEM(fold_map.shape, jnp.int32),
            scratch((rows // LANES, held * width, LANES), F32),
            dma((PIECES + 6,)),
        ],
        compiler_params=limit(14),
        name="prepare",
    )(
        far(fold_map), far(state.transpose(2, 1, 0)), far(ocean_mask.T),
        far(b_first[None]), far(b_second[None]), far(w_first), far(w_second),
    )
    inner = lax.ppermute(inner, "lon", [(i, i ^ 1) for i in range(n)])

    before = 4
    hid_a, last_a, wt, part_a = pl.pallas_call(
        inside_a,
        out_shape=(
            shape((before, rows, hidden), BF),
            shape((8, hidden), F32),
            shape((5 * SLOT, 3 * hidden), BF),
            shape((1, rows, hidden), F32),
        ),
        in_specs=[vmem] * 3,
        out_specs=(vmem,) * 4,
        compiler_params=limit(12),
        name="inside_a",
    )(cols, w_first, bias)

    def stage_b(after):
        return pl.pallas_call(
            functools.partial(inside_b, before),
            out_shape=(
                shape((width - 2 - before, rows, hidden), BF),
                shape((8, hidden), F32),
                shape((3, rows, hidden), F32),
            ),
            in_specs=[vmem] * 5,
            out_specs=(vmem,) * 3,
            compiler_params=limit(12),
            name="inside_b",
        )(cols, w_first, bias, wt, after)

    field = shape((hidden // LANES, rows * width, LANES), F32)

    def stage_c(hid_b, after):
        return pl.pallas_call(
            functools.partial(inside_c, chans),
            out_shape=field,
            in_specs=[vmem] * 6,
            out_specs=vmem,
            compiler_params=limit(12),
            name="inside_c",
        )(hid_a, hid_b, cols, w_second, bias, after)

    pair = shape((2, 2 * width, WIDE), BF)
    tops, sent = pl.pallas_call(
        join_first,
        out_shape=(pair, shape(sent.shape, BF)),
        in_specs=[vmem] * 4,
        out_specs=(vmem,) * 2,
        input_output_aliases={3: 1},
        compiler_params=limit(4),
        name="join_first",
    )(top, inner, last_a, sent)
    step = 2
    while step < n // 2:
        got = lax.ppermute(tops, "lon", [(i, i ^ step) for i in range(n)])
        if step == 2:
            outer = lax.ppermute(sent, "lon", [(i, (i + 1 if i % 2 else i - 1) % n) for i in range(n)])
        if step == n // 4:
            hid_b, last_b, part_b = stage_b(tops)
            outp = stage_c(hid_b, tops)
            break
        tops = pl.pallas_call(
            join,
            out_shape=shape((2 * tops.shape[0],) + tops.shape[1:], BF),
            in_specs=[vmem] * 2,
            out_specs=vmem,
            compiler_params=limit(4),
            name="join",
        )(tops, got)
        step *= 2
    lines = shape((32, WIDE), BF)
    give, keep = pl.pallas_call(
        choose,
        out_shape=(lines, lines),
        in_specs=[vmem] * 4,
        out_specs=(vmem,) * 2,
        compiler_params=limit(4),
        name="choose",
    )(pick, tops, got, outp)
    got = lax.ppermute(give, "lon", [(i, i ^ (n // 2)) for i in range(n)])
    outf, line, own = pl.pallas_call(
        border,
        out_shape=(field, shape((16, hidden), F32), shape((24, WIDE), F32)),
        in_specs=[vmem] * 13,
        out_specs=(vmem,) * 3,
        scratch_shapes=[scratch((2, rows, 2 * MAIN + LANES), BF), scratch((4, rows, hidden), BF)],
        compiler_params=limit(14),
        name="border",
    )(cols, outer, inner, part_a, part_b, last_a, last_b, outp, wt, w_first, bias, w_second, give)
    return pl.pallas_call(
        finish,
        out_shape=shape((rows, width, hidden), BF),
        in_specs=[vmem] * 11,
        out_specs=hbm,
        scratch_shapes=[scratch((24, WIDE), F32)] * 4
        + [scratch((24, hidden), F32)] * 2
        + [scratch((rows, width, hidden), BF), dma((PIECES,))],
        compiler_params=limit(14),
        name="finish",
    )(keep, got, top, outp, outf, line, own, wt, w_first, bias, w_second)


def solution(mesh):
    return jax.shard_map(
        local,
        mesh=mesh,
        in_specs=(P(None, ("grp", "lon"), None), P(None, "lon"), P(), P(), P(), P(), P()),
        out_specs=P(None, ("grp", "lon"), None),
        check_vma=False,
    )
```

```python
import functools

import jax
import jax.numpy as jnp
from jax import lax
from jax.experimental import pallas as pl
from jax.experimental.pallas import tpu as pltpu
from jax.sharding import PartitionSpec as P

BF, F32 = jnp.bfloat16, jnp.float32
LANES, MAIN, SLOT, PIECES, CUTS = 128, 256, 64, 4, 4
GROUP, BEFORE = 2, 3
WIDE = MAIN + 2 * SLOT


def gelu(value):
    return half_gelu(value, 0.5)


def half_gelu(value, half):
    inner = value * (0.7978845608 + (0.7978845608 * 0.044715) * (value * value))
    scaled = value * half
    return scaled + scaled * jnp.tanh(inner)


def turned(block):
    rows = block.shape[-1]
    tail = block[MAIN : MAIN + SLOT]
    tail = jnp.concatenate([tail, jnp.zeros((SLOT - tail.shape[0], rows), BF)], axis=0)
    full = jnp.concatenate([block[:MAIN], tail, tail], axis=0)
    eye = (
        lax.broadcasted_iota(jnp.int32, (rows, rows), 0) == lax.broadcasted_iota(jnp.int32, (rows, rows), 1)
    ).astype(F32).astype(BF)
    return lax.dot_general(eye, full, (((1,), (1,)), ((), ())), preferred_element_type=F32)


def prepare(
    fold_hbm, x_hbm, mask_hbm, b1_hbm, b2_hbm, w1_hbm,
    outer_ref, inner_ref, cols_ref, top_ref, bias_ref, pick_ref, w1_ref,
    x_ref, mask_ref, fold_ref, field, sem,
):
    chans, width, rows = x_ref.shape
    held = field.shape[1] // width
    me = lax.axis_index("lon")
    halves = [slice(i * LANES, (i + 1) * LANES) for i in range(rows // LANES)]
    parts = CUTS // len(halves)
    cuts = [chans * i // parts for i in range(parts + 1)]
    spans = [(i, at, lo, hi) for i, at in enumerate(halves) for lo, hi in zip(cuts, cuts[1:])]
    pairs = [(mask_hbm, mask_ref)]
    pairs += [(x_hbm.at[lo:hi, :, at], x_ref.at[lo:hi, :, at]) for _, at, lo, hi in spans]
    pairs += [(b1_hbm, bias_ref.at[0:1]), (b2_hbm, bias_ref.at[1:2]), (fold_hbm, fold_ref)]
    pairs += [(w1_hbm, w1_ref)]
    copies = [pltpu.make_async_copy(src, dst, sem.at[i]) for i, (src, dst) in enumerate(pairs)]
    for copy in copies:
        copy.start()
    odd = lax.rem(me, 2) == 1
    copies[0].wait()
    mask = mask_ref[...].astype(F32)
    last = []
    for (i, at, lo, hi), copy in zip(spans, copies[1:]):
        copy.wait()
        block = x_ref[lo:hi, :, at].astype(F32) * mask[None, :, at]
        field[i, lo * width : hi * width, :] = block.reshape((hi - lo) * width, LANES)
        if hi < chans:
            continue
        field[i, chans * width : (chans + 1) * width, :] = mask[:, at]
        field[i, (chans + 1) * width :, :] = jnp.zeros(((held - chans - 1) * width, LANES), F32)
        for c in range(width):
            out = turned(field[i, pl.ds(c, held, stride=width), :].astype(BF))
            cols_ref[c, at] = out.astype(BF)
            if at.stop == rows:
                last.append(out[LANES - 2 :])
    lanes = lax.broadcasted_iota(jnp.int32, (rows, LANES), 1)

    def message(c):
        first, second = cols_ref[c], cols_ref[c + 1]
        rest = jnp.where(lanes < SLOT, first[:, MAIN:][:, :LANES], second[:, MAIN:][:, :LANES])
        return jnp.concatenate([first[:, :MAIN], second[:, :MAIN], rest], axis=1)

    low, high = message(0), message(width - 2)
    outer_ref[...] = jnp.where(odd, high, low)
    inner_ref[:rows] = jnp.where(odd, low, high)
    top = jnp.concatenate([v[i : i + 1] for i in range(2) for v in last], axis=0).astype(BF)
    top_ref[0] = top
    inner_ref[rows:] = jnp.concatenate([top, jnp.zeros((2 * width, inner_ref.shape[1] - WIDE), BF)], axis=1)
    for copy in copies[1 + CUTS :]:
        copy.wait()
    total = fold_ref.shape[0]
    n = total // width
    index = lax.broadcasted_iota(jnp.int32, pick_ref.shape, 0)
    j, line = index & 15, lax.shift_right_logical(index, 4) & 1
    dev = jnp.where(index < 32, lax.bitwise_xor(me, n // 2), me)
    col = fold_ref[0] - width * dev + 2 - j
    col = jnp.where(col < 0, col + total, col)
    col = jnp.where(col < 0, col + total, col)
    col = jnp.where(col >= total, col - total, col)
    block = lax.bitwise_xor(lax.shift_right_logical(col, width.bit_length() - 1), me)
    spot = block * (2 * width) + line * width + (col & (width - 1))
    pick_ref[...] = jnp.where((block < n // 2) & (j < width + 4), spot, -1)


def join_first(mine_ref, got_ref, after_ref, sent_ref, out_ref, pass_ref):
    out_ref[0] = mine_ref[0]
    out_ref[1] = got_ref[got_ref.shape[0] - mine_ref.shape[1] :, :WIDE]


def join(mine_ref, got_ref, out_ref):
    count = mine_ref.shape[0]
    out_ref[:count] = mine_ref[...]
    out_ref[count:] = got_ref[...]


def choose(pick_ref, mine_ref, got_ref, after_ref, give_ref, keep_ref):
    count, lines, wide = mine_ref.shape
    blocks = jnp.concatenate([ref[...].reshape(count * lines, wide) for ref in (mine_ref, got_ref)], axis=0)
    lane = lax.broadcasted_iota(jnp.int32, (pick_ref.shape[0], blocks.shape[0]), 1)
    out = mm((pick_ref[:, :1] == lane).astype(F32).astype(BF), blocks).astype(BF)
    give_ref[...] = out[:32]
    keep_ref[...] = out[32:]


def mm(a, b):
    return jnp.dot(a, b, preferred_element_type=F32)


def mask_of(column, chans):
    return column[:, MAIN:].astype(F32)[:, chans - MAIN : chans - MAIN + 1]


def tail_weights(w1_ref, wt):
    chans, hidden = w1_ref.shape[2:]
    for dy in range(3):
        for dx in range(3):
            rest = jnp.concatenate(
                [w1_ref[dy, dx, MAIN:, :], jnp.zeros((SLOT - chans + MAIN, hidden), BF)], axis=0
            )
            wt[(dx + 1) * SLOT : (dx + 2) * SLOT, dy * hidden : (dy + 1) * hidden] = rest
    for at in (0, 4 * SLOT):
        wt[at : at + SLOT, :] = jnp.zeros((SLOT, 3 * hidden), BF)


def first_taps(columns):
    some = next(c for c in columns if c is not None)
    lanes = lax.broadcasted_iota(jnp.int32, (some.shape[0], LANES), 1)
    zero = jnp.zeros((some.shape[0], LANES), BF)
    tail = [zero if c is None else c[:, MAIN:] for c in columns]
    parts = [c[:, :MAIN] for c in columns if c is not None]
    if columns[0] is not None or columns[1] is not None:
        parts.append(jnp.where(lanes < SLOT, tail[0], tail[1]))
    if columns[2] is not None:
        parts.append(tail[2])
    return jnp.concatenate(parts, axis=1)


def first_weights(w1_ref, wt, columns, dys=(0, 1, 2)):
    hidden = w1_ref.shape[3]
    out = []
    for dy in dys:
        at = slice(dy * hidden, (dy + 1) * hidden)
        parts = [w1_ref[dy, dx, :MAIN, :] for dx in range(3) if columns[dx] is not None]
        if columns[0] is not None or columns[1] is not None:
            parts.append(wt[SLOT : 3 * SLOT, at])
        if columns[2] is not None:
            parts.append(wt[3 * SLOT :, at])
        out.append(jnp.concatenate(parts, axis=0))
    return jnp.concatenate(out, axis=1)


def second_weights(w2_ref, columns, dys=(0, 1, 2)):
    return jnp.concatenate(
        [
            jnp.concatenate([w2_ref[dy, dx] for dx in range(3) if columns[dx] is not None], axis=0)
            for dy in dys
        ],
        axis=1,
    )


def last_out(value):
    row = lax.broadcasted_iota(jnp.int32, (8, value.shape[1]), 0)
    return jnp.concatenate([value[:-8], jnp.where(row == 7, 0.0, value[-8:])], axis=0)


def summed(p):
    rows, hidden = p.shape[0], p.shape[1] // 3
    row = lax.broadcasted_iota(jnp.int32, (8, hidden), 0)
    south = pltpu.roll(p[:, :hidden], 1, 0)
    south = jnp.concatenate([jnp.where(row == 0, 0.0, south[:8]), south[8:]], axis=0)
    return p[:, hidden : 2 * hidden] + south + last_out(pltpu.roll(p[:, 2 * hidden :], rows - 1, 0))


def edges(width):
    return (0, 1, width, width + 1)


def own_column(cols_ref, j):
    return cols_ref[j - 2] if 2 <= j < 2 + cols_ref.shape[0] else None


def hidden_columns(cols_ref, w1_ref, bias_ref, wt, hid_ref, last_ref, first, part_ref, more):
    chans, _ = w1_ref.shape[2:]
    rows = cols_ref.shape[1]
    last_ref[...] = jnp.zeros_like(last_ref)
    for i in range(0, hid_ref.shape[0], GROUP):
        group = range(min(GROUP, hid_ref.shape[0] - i))
        sets = [[own_column(cols_ref, first + i + g + dx) for dx in range(3)] for g in group]
        lhs = jnp.concatenate([first_taps(columns) for columns in sets], axis=0)
        out = mm(lhs, first_weights(w1_ref, wt, sets[0]))
        for g in group:
            value = summed(out[g * rows : (g + 1) * rows])
            last_ref[i + g : i + g + 1, :] = value[rows - 1 :]
            value = half_gelu(value + bias_ref[0:1], 0.5 * mask_of(sets[g][1], chans))
            hid_ref[i + g] = last_out(value).astype(BF)
    for i, h in enumerate(more):
        columns = [own_column(cols_ref, h + dx) for dx in range(3)]
        part_ref[i] = summed(mm(first_taps(columns), first_weights(w1_ref, wt, columns)))


def inside_a(cols_ref, w1_ref, bias_ref, w2_hbm, hid_ref, last_ref, wt_ref, w2_ref, sem):
    copy = pltpu.make_async_copy(w2_hbm, w2_ref, sem)
    copy.start()
    tail_weights(w1_ref, wt_ref)
    hidden_columns(cols_ref, w1_ref, bias_ref, wt_ref, hid_ref, last_ref, 2, None, ())
    copy.wait()


def inside_b(before, cols_ref, w1_ref, bias_ref, wt_ref, after_ref, hid_ref, last_ref, part_ref):
    width = cols_ref.shape[0]
    hidden_columns(cols_ref, w1_ref, bias_ref, wt_ref, hid_ref, last_ref, 2 + before, part_ref, edges(width))


def second_columns(chans, todo, hid_a, hid_b, cols_ref, w2_ref, bias_ref, out_ref):
    width, rows, _ = cols_ref.shape
    hidden = w2_ref.shape[3]
    before = hid_a.shape[0]

    def hid(h):
        if not 2 <= h < width:
            return None
        return hid_a[h - 2] if h - 2 < before else hid_b[h - 2 - before]

    def put(o, value):
        for i in range(hidden // LANES):
            out_ref[i, pl.ds(o, rows, stride=width), :] = value[:, i * LANES : (i + 1) * LANES]

    def lhs(columns):
        return jnp.concatenate([c for c in columns if c is not None], axis=1)

    for group in todo:
        sets = [[hid(o + dx) for dx in range(3)] for o in group]
        out = mm(jnp.concatenate([lhs(c) for c in sets], axis=0), second_weights(w2_ref, sets[0]))
        for g, o in enumerate(group):
            value = summed(out[g * rows : (g + 1) * rows]) + bias_ref[1:2]
            if 2 <= o < width - 2:
                value = value * mask_of(cols_ref[o], chans)
            put(o, value)


def inside_c(chans, hid_a, hid_b, cols_ref, w2_ref, bias_ref, after_ref, out_ref):
    width = cols_ref.shape[0]
    todo = ((2, 3), (4, 5), (0,), (1,), (width - 2,), (width - 1,))
    second_columns(chans, todo, hid_a, hid_b, cols_ref, w2_ref, bias_ref, out_ref)


def border(
    cols_ref, outer_ref, inner_ref, part_ref, last_a, last_b, outp_ref, wt, w1_ref, bias_ref, w2_ref, after_ref,
    outf, line, own, hx, hid,
):
    chans, hidden = w1_ref.shape[2:]
    width, rows, _ = cols_ref.shape
    rest = 2 * MAIN
    odd = lax.rem(lax.axis_index("lon"), 2) == 1
    bias1 = bias_ref[0:1]
    outer, inner = outer_ref[...], inner_ref[:rows]
    hx[0] = jnp.where(odd, inner, outer)
    hx[1] = jnp.where(odd, outer, inner)

    at = edges(width)
    taken = (
        (0, slice(0, rest), (0, 1), 1),
        (0, slice(MAIN, rest), (0,), 0),
        (1, slice(0, MAIN), (2,), 3),
        (1, slice(0, rest), (1, 2), 2),
    )
    line[...] = jnp.zeros_like(line)
    line[2 : 2 + BEFORE] = last_a[:BEFORE]
    line[2 + BEFORE : width] = last_b[: width - 2 - BEFORE]
    for i, (side, main, dxs, slot) in enumerate(taken):
        lhs = jnp.concatenate([hx[side, :, main], hx[side, :, rest:]], axis=1)
        rhs = []
        for dy in range(3):
            block = wt[slot * SLOT : (slot + 2) * SLOT, dy * hidden : (dy + 1) * hidden]
            rhs.append(jnp.concatenate([w1_ref[dy, dx, :MAIN, :] for dx in dxs] + [block], axis=0))
        value = part_ref[i] + summed(mm(lhs, jnp.concatenate(rhs, axis=1)))
        line[at[i] : at[i] + 1, :] = value[rows - 1 :]
        sea = chans - MAIN
        if i == 0:
            mask = hx[0, :, rest:].astype(F32)[:, SLOT + sea : SLOT + sea + 1]
        elif i == 3:
            mask = hx[1, :, rest:].astype(F32)[:, sea : sea + 1]
        else:
            mask = mask_of(cols_ref[at[i] - 1], chans)
        hid[i] = last_out(half_gelu(value + bias1, 0.5 * mask)).astype(BF)

    for o in (0, 1, width - 2, width - 1):
        columns = [hid[at.index(o + dx)] if o + dx in at else None for dx in range(3)]
        have = [c for c in columns if c is not None]
        value = summed(mm(jnp.concatenate(have, axis=1), second_weights(w2_ref, columns)))
        mask = mask_of(cols_ref[o], chans)
        for i in range(hidden // LANES):
            to = (i, pl.ds(o, rows, stride=width), slice(None))
            outf[to] = (outp_ref[to] + value[:, i * LANES : (i + 1) * LANES]) * mask
    own[...] = jnp.zeros_like(own)
    for j in range(width):
        own[2 + j : 3 + j, :] = cols_ref[j, rows - 16 :].astype(F32)[15:16]
    half = lax.broadcasted_iota(jnp.int32, (8, LANES), 1) < SLOT
    for side, first in ((0, 0), (1, 2 + width)):
        end = hx[side, rows - 16 :].astype(F32)[8:16]
        tail = end[:, rest:]
        turn = pltpu.roll(tail, SLOT, 1)
        for c, both_halves in enumerate((jnp.where(half, tail, turn), jnp.where(half, turn, tail))):
            full = jnp.concatenate([end[:, c * MAIN : (c + 1) * MAIN], both_halves], axis=1)
            own[first + c : first + c + 1, :] = full[7:8]


def finish(
    keep_ref, got_ref, top_ref, outp_ref, outf, line, own, wt, w1_ref, bias_ref, w2_ref,
    out_hbm, m0, m1, r2, gs, hg, hz, outb, sem,
):
    chans, hidden = w1_ref.shape[2:]
    rows, width, _ = out_hbm.shape
    bias1 = bias_ref[0:1]
    ends = [rows * p // PIECES for p in range(PIECES)] + [rows - 8, rows]
    copies = []

    def assemble(p, more):
        lo, hi = ends[p], ends[p + 1]
        here, lines = slice(lo, hi), slice(lo * width, hi * width)
        place = lax.rem(lax.broadcasted_iota(jnp.int32, ((hi - lo) * width, LANES), 0), width)
        edge = (place < 2) | (place >= width - 2)
        for i in range(hidden // LANES):
            lanes = slice(i * LANES, (i + 1) * LANES)
            value = jnp.where(edge, outf[i, lines], outp_ref[i, lines])
            if more is not None:
                end = (hi - lo - 2) * width
                value = jnp.concatenate([value[:end], value[end:] + more[:, lanes]], axis=0)
            outb[here, :, lanes] = value.reshape(hi - lo, width, LANES).astype(BF)
        copies.append(pltpu.make_async_copy(outb.at[here], out_hbm.at[here], sem.at[p]))
        copies[-1].start()

    for p in range(PIECES):
        assemble(p, None)
    lane = lax.broadcasted_iota(jnp.int32, (1, WIDE), 1)
    sign = jnp.where(lane < chans // 2, -1.0, 1.0).astype(F32)
    both = keep_ref[...].astype(F32) + got_ref[...].astype(F32)
    for ref, value in ((m0, both[:16]), (m1, both[16:]), (gs, both[16:] * sign)):
        ref[:16] = value
        ref[16:] = jnp.zeros_like(ref[16:])
    r2[...] = own[...] * sign

    def taps(ref, offsets):
        return first_taps([ref[o : o + 16, :].astype(BF) for o in offsets])

    every = (0, 0, 0)
    mixed = mm(
        jnp.concatenate([taps(gs, (0, 1, 2)), taps(r2, (2, 1, 0))], axis=0), first_weights(w1_ref, wt, every, (2,))
    )
    pre = mixed[16:]
    pre += mm(taps(m0, (2, 1, 0)), first_weights(w1_ref, wt, every, (0,)))
    pre += mm(taps(m1, (2, 1, 0)), first_weights(w1_ref, wt, every, (1,)))
    hg[16:] = jnp.zeros_like(hg[16:])
    hg[:16] = gelu(pre + bias1) * m1[1:17, chans : chans + 1]
    hz[16:] = jnp.zeros_like(hz[16:])
    hz[:16] = gelu(line[...] + mixed[:16] + bias1) * own[1:17, chans : chans + 1]
    wide = [jnp.concatenate([ref[o : o + 16, :].astype(BF) for o in range(3)], axis=1) for ref in (hz, hg)]
    more = mm(jnp.concatenate(wide, axis=0), second_weights(w2_ref, every, (1, 2)))
    below = more[:width, hidden:]
    level = more[:width, :hidden] + more[16 : 16 + width, hidden:]
    fixed = jnp.concatenate([below, level], axis=0) * mask_of(top_ref[0], chans)

    assemble(PIECES, fixed)
    for copy in copies:
        copy.wait()


def local(state, ocean_mask, fold_map, w_first, b_first, w_second, b_second):
    rows, width, chans = state.shape
    hidden = w_first.shape[-1]
    n = lax.axis_size("lon")
    assert n >= 8 and n & (n - 1) == 0 and MAIN <= chans < MAIN + SLOT and chans // 2 <= MAIN and width == 8 and rows == MAIN
    held = -(-(chans + 1) // 16) * 16
    vmem = pl.BlockSpec(memory_space=pltpu.VMEM)
    hbm = pl.BlockSpec(memory_space=pltpu.MemorySpace.HBM)
    shape = jax.ShapeDtypeStruct
    scratch = pltpu.VMEM
    dma = pltpu.SemaphoreType.DMA

    def limit(mib):
        return pltpu.CompilerParams(vmem_limit_bytes=mib << 20)

    def far(value):
        return pltpu.with_memory_space_constraint(value, pltpu.MemorySpace.HBM)

    sent, inner, cols, top, bias, pick, w_first = pl.pallas_call(
        prepare,
        out_shape=(
            shape((rows, 2 * MAIN + LANES), BF),
            shape((rows + 2 * width, 2 * MAIN + LANES), BF),
            shape((width, rows, WIDE), BF),
            shape((1, 2 * width, WIDE), BF),
            shape((2, hidden), F32),
            shape((64, LANES), jnp.int32),
            shape(w_first.shape, BF),
        ),
        in_specs=[hbm] * 6,
        out_specs=(vmem,) * 7,
        scratch_shapes=[
            scratch((chans, width, rows), BF),
            scratch((width, rows), jnp.int32),
            pltpu.SMEM(fold_map.shape, jnp.int32),
            scratch((rows // LANES, held * width, LANES), F32),
            dma((CUTS + 5,)),
        ],
        compiler_params=limit(14),
        name="prepare",
    )(
        far(fold_map), far(state.transpose(2, 1, 0)), far(ocean_mask.T),
        far(b_first[None]), far(b_second[None]), far(w_first),
    )
    inner = lax.ppermute(inner, "lon", [(i, i ^ 1) for i in range(n)])

    before = BEFORE
    hid_a, last_a, wt, w_second = pl.pallas_call(
        inside_a,
        out_shape=(
            shape((before, rows, hidden), BF),
            shape((8, hidden), F32),
            shape((5 * SLOT, 3 * hidden), BF),
            shape(w_second.shape, BF),
        ),
        in_specs=[vmem] * 3 + [hbm],
        out_specs=(vmem,) * 4,
        scratch_shapes=[dma],
        compiler_params=limit(12),
        name="inside_a",
    )(cols, w_first, bias, far(w_second))

    def stage_b(after):
        return pl.pallas_call(
            functools.partial(inside_b, before),
            out_shape=(
                shape((width - 2 - before, rows, hidden), BF),
                shape((8, hidden), F32),
                shape((4, rows, hidden), F32),
            ),
            in_specs=[vmem] * 5,
            out_specs=(vmem,) * 3,
            compiler_params=limit(12),
            name="inside_b",
        )(cols, w_first, bias, wt, after)

    field = shape((hidden // LANES, rows * width, LANES), F32)

    def stage_c(hid_b, after):
        return pl.pallas_call(
            functools.partial(inside_c, chans),
            out_shape=field,
            in_specs=[vmem] * 6,
            out_specs=vmem,
            compiler_params=limit(12),
            name="inside_c",
        )(hid_a, hid_b, cols, w_second, bias, after)

    pair = shape((2, 2 * width, WIDE), BF)
    tops, sent = pl.pallas_call(
        join_first,
        out_shape=(pair, shape(sent.shape, BF)),
        in_specs=[vmem] * 4,
        out_specs=(vmem,) * 2,
        input_output_aliases={3: 1},
        compiler_params=limit(4),
        name="join_first",
    )(top, inner, last_a, sent)
    step = 2
    while step < n // 2:
        got = lax.ppermute(tops, "lon", [(i, i ^ step) for i in range(n)])
        if step == 2:
            outer = lax.ppermute(sent, "lon", [(i, (i + 1 if i % 2 else i - 1) % n) for i in range(n)])
        if step == n // 4:
            hid_b, last_b, part_b = stage_b(tops)
            outp = stage_c(hid_b, tops)
            break
        tops = pl.pallas_call(
            join,
            out_shape=shape((2 * tops.shape[0],) + tops.shape[1:], BF),
            in_specs=[vmem] * 2,
            out_specs=vmem,
            compiler_params=limit(4),
            name="join",
        )(tops, got)
        step *= 2
    lines = shape((32, WIDE), BF)
    give, keep = pl.pallas_call(
        choose,
        out_shape=(lines, lines),
        in_specs=[vmem] * 4,
        out_specs=(vmem,) * 2,
        compiler_params=limit(4),
        name="choose",
    )(pick, tops, got, outp)
    got = lax.ppermute(give, "lon", [(i, i ^ (n // 2)) for i in range(n)])
    outf, line, own = pl.pallas_call(
        border,
        out_shape=(field, shape((16, hidden), F32), shape((24, WIDE), F32)),
        in_specs=[vmem] * 12,
        out_specs=(vmem,) * 3,
        scratch_shapes=[scratch((2, rows, 2 * MAIN + LANES), BF), scratch((4, rows, hidden), BF)],
        compiler_params=limit(14),
        name="border",
    )(cols, outer, inner, part_b, last_a, last_b, outp, wt, w_first, bias, w_second, give)
    return pl.pallas_call(
        finish,
        out_shape=shape((rows, width, hidden), BF),
        in_specs=[vmem] * 11,
        out_specs=hbm,
        scratch_shapes=[scratch((24, WIDE), F32)] * 4
        + [scratch((24, hidden), F32)] * 2
        + [scratch((rows, width, hidden), BF), dma((PIECES + 1,))],
        compiler_params=limit(14),
        name="finish",
    )(keep, got, top, outp, outf, line, own, wt, w_first, bias, w_second)


def solution(mesh):
    return jax.shard_map(
        local,
        mesh=mesh,
        in_specs=(P(None, ("grp", "lon"), None), P(None, "lon"), P(), P(), P(), P(), P()),
        out_specs=P(None, ("grp", "lon"), None),
        check_vma=False,
    )
```

```python
import functools

import jax
import jax.numpy as jnp
from jax import lax
from jax.experimental import pallas as pl
from jax.experimental.pallas import tpu as pltpu
from jax.sharding import PartitionSpec as P

BF, F32 = jnp.bfloat16, jnp.float32
LANES, MAIN, SLOT, PIECES, CUTS = 128, 256, 64, 4, 4
GROUP, BEFORE = 2, 3
WIDE = MAIN + 2 * SLOT


def gelu(value):
    return half_gelu(value, 0.5)


def half_gelu(value, half):
    inner = value * (0.7978845608 + (0.7978845608 * 0.044715) * (value * value))
    scaled = value * half
    return scaled + scaled * jnp.tanh(inner)


def turned(block):
    rows = block.shape[-1]
    tail = block[MAIN : MAIN + SLOT]
    tail = jnp.concatenate([tail, jnp.zeros((SLOT - tail.shape[0], rows), BF)], axis=0)
    full = jnp.concatenate([block[:MAIN], tail, tail], axis=0)
    eye = (
        lax.broadcasted_iota(jnp.int32, (rows, rows), 0) == lax.broadcasted_iota(jnp.int32, (rows, rows), 1)
    ).astype(F32).astype(BF)
    return lax.dot_general(eye, full, (((1,), (1,)), ((), ())), preferred_element_type=F32)


def prepare(
    fold_hbm, x_hbm, mask_hbm, b1_hbm, b2_hbm, w1_hbm,
    outer_ref, inner_ref, cols_ref, top_ref, bias_ref, pick_ref, w1_ref,
    x_ref, mask_ref, fold_ref, field, sem,
):
    chans, width, rows = x_ref.shape
    held = field.shape[1] // width
    me = lax.axis_index("lon")
    halves = [slice(i * LANES, (i + 1) * LANES) for i in range(rows // LANES)]
    parts = CUTS // len(halves)
    cuts = [chans * i // parts for i in range(parts + 1)]
    spans = [(i, at, lo, hi) for i, at in enumerate(halves) for lo, hi in zip(cuts, cuts[1:])]
    pairs = [(mask_hbm, mask_ref)]
    pairs += [(x_hbm.at[lo:hi, :, at], x_ref.at[lo:hi, :, at]) for _, at, lo, hi in spans]
    pairs += [(b1_hbm, bias_ref.at[0:1]), (b2_hbm, bias_ref.at[1:2]), (fold_hbm, fold_ref)]
    pairs += [(w1_hbm, w1_ref)]
    copies = [pltpu.make_async_copy(src, dst, sem.at[i]) for i, (src, dst) in enumerate(pairs)]
    for copy in copies:
        copy.start()
    odd = lax.rem(me, 2) == 1
    copies[3 + CUTS].wait()
    total = fold_ref.shape[0]
    n = total // width
    index = lax.broadcasted_iota(jnp.int32, pick_ref.shape, 0)
    j, line = index & 15, lax.shift_right_logical(index, 4) & 1
    dev = jnp.where(index < 32, lax.bitwise_xor(me, n // 2), me)
    col = fold_ref[0] - width * dev + 2 - j
    col = jnp.where(col < 0, col + total, col)
    col = jnp.where(col < 0, col + total, col)
    col = jnp.where(col >= total, col - total, col)
    block = lax.bitwise_xor(lax.shift_right_logical(col, width.bit_length() - 1), me)
    spot = block * (2 * width) + line * width + (col & (width - 1))
    pick_ref[...] = jnp.where((block < n // 2) & (j < width + 4), spot, -1)
    copies[0].wait()
    mask = mask_ref[...].astype(F32)
    last = []
    for (i, at, lo, hi), copy in zip(spans, copies[1:]):
        copy.wait()
        block = x_ref[lo:hi, :, at].astype(F32) * mask[None, :, at]
        field[i, lo * width : hi * width, :] = block.reshape((hi - lo) * width, LANES)
        if hi < chans:
            continue
        field[i, chans * width : (chans + 1) * width, :] = mask[:, at]
        field[i, (chans + 1) * width :, :] = jnp.zeros(((held - chans - 1) * width, LANES), F32)
    for i, at in enumerate(halves):
        for c in range(width):
            out = turned(field[i, pl.ds(c, held, stride=width), :].astype(BF))
            cols_ref[c, at] = out.astype(BF)
            if at.stop == rows:
                last.append(out[LANES - 2 :])
    lanes = lax.broadcasted_iota(jnp.int32, (rows, LANES), 1)

    def message(c):
        first, second = cols_ref[c], cols_ref[c + 1]
        rest = jnp.where(lanes < SLOT, first[:, MAIN:][:, :LANES], second[:, MAIN:][:, :LANES])
        return jnp.concatenate([first[:, :MAIN], second[:, :MAIN], rest], axis=1)

    low, high = message(0), message(width - 2)
    outer_ref[...] = jnp.where(odd, high, low)
    inner_ref[:rows] = jnp.where(odd, low, high)
    top = jnp.concatenate([v[i : i + 1] for i in range(2) for v in last], axis=0).astype(BF)
    top_ref[0] = top
    inner_ref[rows:] = jnp.concatenate([top, jnp.zeros((2 * width, inner_ref.shape[1] - WIDE), BF)], axis=1)
    for k, copy in enumerate(copies[1 + CUTS :]):
        if k != 2:
            copy.wait()


def join_first(mine_ref, got_ref, after_ref, sent_ref, out_ref, pass_ref):
    out_ref[0] = mine_ref[0]
    out_ref[1] = got_ref[got_ref.shape[0] - mine_ref.shape[1] :, :WIDE]


def join(mine_ref, got_ref, out_ref):
    count = mine_ref.shape[0]
    out_ref[:count] = mine_ref[...]
    out_ref[count:] = got_ref[...]


def choose(pick_ref, mine_ref, got_ref, after_ref, give_ref, keep_ref):
    count, lines, wide = mine_ref.shape
    blocks = jnp.concatenate([ref[...].reshape(count * lines, wide) for ref in (mine_ref, got_ref)], axis=0)
    lane = lax.broadcasted_iota(jnp.int32, (pick_ref.shape[0], blocks.shape[0]), 1)
    out = mm((pick_ref[:, :1] == lane).astype(F32).astype(BF), blocks).astype(BF)
    give_ref[...] = out[:32]
    keep_ref[...] = out[32:]


def mm(a, b):
    return jnp.dot(a, b, preferred_element_type=F32)


def mask_of(column, chans):
    return column[:, MAIN:].astype(F32)[:, chans - MAIN : chans - MAIN + 1]


def tail_weights(w1_ref, wt):
    chans, hidden = w1_ref.shape[2:]
    for dy in range(3):
        for dx in range(3):
            rest = jnp.concatenate(
                [w1_ref[dy, dx, MAIN:, :], jnp.zeros((SLOT - chans + MAIN, hidden), BF)], axis=0
            )
            wt[(dx + 1) * SLOT : (dx + 2) * SLOT, dy * hidden : (dy + 1) * hidden] = rest
    for at in (0, 4 * SLOT):
        wt[at : at + SLOT, :] = jnp.zeros((SLOT, 3 * hidden), BF)


def first_taps(columns):
    some = next(c for c in columns if c is not None)
    lanes = lax.broadcasted_iota(jnp.int32, (some.shape[0], LANES), 1)
    zero = jnp.zeros((some.shape[0], LANES), BF)
    tail = [zero if c is None else c[:, MAIN:] for c in columns]
    parts = [c[:, :MAIN] for c in columns if c is not None]
    if columns[0] is not None or columns[1] is not None:
        parts.append(jnp.where(lanes < SLOT, tail[0], tail[1]))
    if columns[2] is not None:
        parts.append(tail[2])
    return jnp.concatenate(parts, axis=1)


def first_weights(w1_ref, wt, columns, dys=(0, 1, 2)):
    hidden = w1_ref.shape[3]
    out = []
    for dy in dys:
        at = slice(dy * hidden, (dy + 1) * hidden)
        parts = [w1_ref[dy, dx, :MAIN, :] for dx in range(3) if columns[dx] is not None]
        if columns[0] is not None or columns[1] is not None:
            parts.append(wt[SLOT : 3 * SLOT, at])
        if columns[2] is not None:
            parts.append(wt[3 * SLOT :, at])
        out.append(jnp.concatenate(parts, axis=0))
    return jnp.concatenate(out, axis=1)


def second_weights(w2_ref, columns, dys=(0, 1, 2)):
    return jnp.concatenate(
        [
            jnp.concatenate([w2_ref[dy, dx] for dx in range(3) if columns[dx] is not None], axis=0)
            for dy in dys
        ],
        axis=1,
    )


def last_out(value):
    row = lax.broadcasted_iota(jnp.int32, (8, value.shape[1]), 0)
    return jnp.concatenate([value[:-8], jnp.where(row == 7, 0.0, value[-8:])], axis=0)


def summed(p):
    rows, hidden = p.shape[0], p.shape[1] // 3
    row = lax.broadcasted_iota(jnp.int32, (8, hidden), 0)
    south = pltpu.roll(p[:, :hidden], 1, 0)
    south = jnp.concatenate([jnp.where(row == 0, 0.0, south[:8]), south[8:]], axis=0)
    return p[:, hidden : 2 * hidden] + south + last_out(pltpu.roll(p[:, 2 * hidden :], rows - 1, 0))


def edges(width):
    return (0, 1, width, width + 1)


def own_column(cols_ref, j):
    return cols_ref[j - 2] if 2 <= j < 2 + cols_ref.shape[0] else None


def hidden_columns(cols_ref, w1_ref, bias_ref, wt, hid_ref, last_ref, first, part_ref, more):
    chans, _ = w1_ref.shape[2:]
    rows = cols_ref.shape[1]
    last_ref[...] = jnp.zeros_like(last_ref)
    for i in range(0, hid_ref.shape[0], GROUP):
        group = range(min(GROUP, hid_ref.shape[0] - i))
        sets = [[own_column(cols_ref, first + i + g + dx) for dx in range(3)] for g in group]
        lhs = jnp.concatenate([first_taps(columns) for columns in sets], axis=0)
        out = mm(lhs, first_weights(w1_ref, wt, sets[0]))
        for g in group:
            value = summed(out[g * rows : (g + 1) * rows])
            last_ref[i + g : i + g + 1, :] = value[rows - 1 :]
            value = half_gelu(value + bias_ref[0:1], 0.5 * mask_of(sets[g][1], chans))
            hid_ref[i + g] = last_out(value).astype(BF)
    for i, h in enumerate(more):
        columns = [own_column(cols_ref, h + dx) for dx in range(3)]
        part_ref[i] = summed(mm(first_taps(columns), first_weights(w1_ref, wt, columns)))


def inside_a(cols_ref, w1_ref, bias_ref, w2_hbm, hid_ref, last_ref, wt_ref, w2_ref, sem):
    copy = pltpu.make_async_copy(w2_hbm, w2_ref, sem)
    copy.start()
    tail_weights(w1_ref, wt_ref)
    hidden_columns(cols_ref, w1_ref, bias_ref, wt_ref, hid_ref, last_ref, 2, None, ())
    copy.wait()


def inside_b(before, cols_ref, w1_ref, bias_ref, wt_ref, after_ref, hid_ref, last_ref, part_ref):
    width = cols_ref.shape[0]
    hidden_columns(cols_ref, w1_ref, bias_ref, wt_ref, hid_ref, last_ref, 2 + before, part_ref, edges(width))


def second_columns(chans, todo, hid_a, hid_b, cols_ref, w2_ref, bias_ref, out_ref):
    width, rows, _ = cols_ref.shape
    hidden = w2_ref.shape[3]
    before = hid_a.shape[0]

    def hid(h):
        if not 2 <= h < width:
            return None
        return hid_a[h - 2] if h - 2 < before else hid_b[h - 2 - before]

    def put(o, value):
        for i in range(hidden // LANES):
            out_ref[i, pl.ds(o, rows, stride=width), :] = value[:, i * LANES : (i + 1) * LANES]

    def lhs(columns):
        return jnp.concatenate([c for c in columns if c is not None], axis=1)

    for group in todo:
        sets = [[hid(o + dx) for dx in range(3)] for o in group]
        out = mm(jnp.concatenate([lhs(c) for c in sets], axis=0), second_weights(w2_ref, sets[0]))
        for g, o in enumerate(group):
            value = summed(out[g * rows : (g + 1) * rows]) + bias_ref[1:2]
            if 2 <= o < width - 2:
                value = value * mask_of(cols_ref[o], chans)
            put(o, value)


def inside_c(chans, hid_a, hid_b, cols_ref, w2_ref, bias_ref, after_ref, out_ref):
    width = cols_ref.shape[0]
    todo = ((2, 3), (4, 5), (0,), (1,), (width - 2,), (width - 1,))
    second_columns(chans, todo, hid_a, hid_b, cols_ref, w2_ref, bias_ref, out_ref)


def border(
    cols_ref, outer_ref, inner_ref, part_ref, last_a, last_b, outp_ref, wt, w1_ref, bias_ref, w2_ref, after_ref,
    outf, line, own, hx, hid,
):
    chans, hidden = w1_ref.shape[2:]
    width, rows, _ = cols_ref.shape
    rest = 2 * MAIN
    odd = lax.rem(lax.axis_index("lon"), 2) == 1
    bias1 = bias_ref[0:1]
    outer, inner = outer_ref[...], inner_ref[:rows]
    hx[0] = jnp.where(odd, inner, outer)
    hx[1] = jnp.where(odd, outer, inner)

    at = edges(width)
    taken = (
        (0, slice(0, rest), (0, 1), 1),
        (0, slice(MAIN, rest), (0,), 0),
        (1, slice(0, MAIN), (2,), 3),
        (1, slice(0, rest), (1, 2), 2),
    )
    line[...] = jnp.zeros_like(line)
    line[2 : 2 + BEFORE] = last_a[:BEFORE]
    line[2 + BEFORE : width] = last_b[: width - 2 - BEFORE]
    for i, (side, main, dxs, slot) in enumerate(taken):
        lhs = jnp.concatenate([hx[side, :, main], hx[side, :, rest:]], axis=1)
        rhs = []
        for dy in range(3):
            block = wt[slot * SLOT : (slot + 2) * SLOT, dy * hidden : (dy + 1) * hidden]
            rhs.append(jnp.concatenate([w1_ref[dy, dx, :MAIN, :] for dx in dxs] + [block], axis=0))
        value = part_ref[i] + summed(mm(lhs, jnp.concatenate(rhs, axis=1)))
        line[at[i] : at[i] + 1, :] = value[rows - 1 :]
        sea = chans - MAIN
        if i == 0:
            mask = hx[0, :, rest:].astype(F32)[:, SLOT + sea : SLOT + sea + 1]
        elif i == 3:
            mask = hx[1, :, rest:].astype(F32)[:, sea : sea + 1]
        else:
            mask = mask_of(cols_ref[at[i] - 1], chans)
        hid[i] = last_out(half_gelu(value + bias1, 0.5 * mask)).astype(BF)

    for o in (0, 1, width - 2, width - 1):
        columns = [hid[at.index(o + dx)] if o + dx in at else None for dx in range(3)]
        have = [c for c in columns if c is not None]
        value = summed(mm(jnp.concatenate(have, axis=1), second_weights(w2_ref, columns)))
        mask = mask_of(cols_ref[o], chans)
        for i in range(hidden // LANES):
            to = (i, pl.ds(o, rows, stride=width), slice(None))
            outf[to] = (outp_ref[to] + value[:, i * LANES : (i + 1) * LANES]) * mask
    own[...] = jnp.zeros_like(own)
    for j in range(width):
        own[2 + j : 3 + j, :] = cols_ref[j, rows - 16 :].astype(F32)[15:16]
    half = lax.broadcasted_iota(jnp.int32, (8, LANES), 1) < SLOT
    for side, first in ((0, 0), (1, 2 + width)):
        end = hx[side, rows - 16 :].astype(F32)[8:16]
        tail = end[:, rest:]
        turn = pltpu.roll(tail, SLOT, 1)
        for c, both_halves in enumerate((jnp.where(half, tail, turn), jnp.where(half, turn, tail))):
            full = jnp.concatenate([end[:, c * MAIN : (c + 1) * MAIN], both_halves], axis=1)
            own[first + c : first + c + 1, :] = full[7:8]


def finish(
    keep_ref, got_ref, top_ref, outp_ref, outf, line, own, wt, w1_ref, bias_ref, w2_ref,
    out_hbm, m0, m1, r2, gs, hg, hz, outb, sem,
):
    chans, hidden = w1_ref.shape[2:]
    rows, width, _ = out_hbm.shape
    bias1 = bias_ref[0:1]
    ends = [rows * p // PIECES for p in range(PIECES)] + [rows - 8, rows]
    copies = []

    def assemble(p, more):
        lo, hi = ends[p], ends[p + 1]
        here, lines = slice(lo, hi), slice(lo * width, hi * width)
        place = lax.rem(lax.broadcasted_iota(jnp.int32, ((hi - lo) * width, LANES), 0), width)
        edge = (place < 2) | (place >= width - 2)
        for i in range(hidden // LANES):
            lanes = slice(i * LANES, (i + 1) * LANES)
            value = jnp.where(edge, outf[i, lines], outp_ref[i, lines])
            if more is not None:
                end = (hi - lo - 2) * width
                value = jnp.concatenate([value[:end], value[end:] + more[:, lanes]], axis=0)
            outb[here, :, lanes] = value.reshape(hi - lo, width, LANES).astype(BF)
        copies.append(pltpu.make_async_copy(outb.at[here], out_hbm.at[here], sem.at[p]))
        copies[-1].start()

    for p in range(PIECES):
        assemble(p, None)
    lane = lax.broadcasted_iota(jnp.int32, (1, WIDE), 1)
    sign = jnp.where(lane < chans // 2, -1.0, 1.0).astype(F32)
    both = keep_ref[...].astype(F32) + got_ref[...].astype(F32)
    for ref, value in ((m0, both[:16]), (m1, both[16:]), (gs, both[16:] * sign)):
        ref[:16] = value
        ref[16:] = jnp.zeros_like(ref[16:])
    r2[...] = own[...] * sign

    def taps(ref, offsets):
        return first_taps([ref[o : o + 16, :].astype(BF) for o in offsets])

    every = (0, 0, 0)
    mixed = mm(
        jnp.concatenate([taps(gs, (0, 1, 2)), taps(r2, (2, 1, 0))], axis=0), first_weights(w1_ref, wt, every, (2,))
    )
    pre = mixed[16:]
    pre += mm(taps(m0, (2, 1, 0)), first_weights(w1_ref, wt, every, (0,)))
    pre += mm(taps(m1, (2, 1, 0)), first_weights(w1_ref, wt, every, (1,)))
    hg[16:] = jnp.zeros_like(hg[16:])
    hg[:16] = gelu(pre + bias1) * m1[1:17, chans : chans + 1]
    hz[16:] = jnp.zeros_like(hz[16:])
    hz[:16] = gelu(line[...] + mixed[:16] + bias1) * own[1:17, chans : chans + 1]
    wide = [jnp.concatenate([ref[o : o + 16, :].astype(BF) for o in range(3)], axis=1) for ref in (hz, hg)]
    more = mm(jnp.concatenate(wide, axis=0), second_weights(w2_ref, every, (1, 2)))
    below = more[:width, hidden:]
    level = more[:width, :hidden] + more[16 : 16 + width, hidden:]
    fixed = jnp.concatenate([below, level], axis=0) * mask_of(top_ref[0], chans)

    assemble(PIECES, fixed)
    for copy in copies:
        copy.wait()


def local(state, ocean_mask, fold_map, w_first, b_first, w_second, b_second):
    rows, width, chans = state.shape
    hidden = w_first.shape[-1]
    n = lax.axis_size("lon")
    assert n >= 8 and n & (n - 1) == 0 and MAIN <= chans < MAIN + SLOT and chans // 2 <= MAIN and width == 8 and rows == MAIN
    held = -(-(chans + 1) // 16) * 16
    vmem = pl.BlockSpec(memory_space=pltpu.VMEM)
    hbm = pl.BlockSpec(memory_space=pltpu.MemorySpace.HBM)
    shape = jax.ShapeDtypeStruct
    scratch = pltpu.VMEM
    dma = pltpu.SemaphoreType.DMA

    def limit(mib):
        return pltpu.CompilerParams(vmem_limit_bytes=mib << 20)

    def far(value):
        return pltpu.with_memory_space_constraint(value, pltpu.MemorySpace.HBM)

    sent, inner, cols, top, bias, pick, w_first = pl.pallas_call(
        prepare,
        out_shape=(
            shape((rows, 2 * MAIN + LANES), BF),
            shape((rows + 2 * width, 2 * MAIN + LANES), BF),
            shape((width, rows, WIDE), BF),
            shape((1, 2 * width, WIDE), BF),
            shape((2, hidden), F32),
            shape((64, LANES), jnp.int32),
            shape(w_first.shape, BF),
        ),
        in_specs=[hbm] * 6,
        out_specs=(vmem,) * 7,
        scratch_shapes=[
            scratch((chans, width, rows), BF),
            scratch((width, rows), jnp.int32),
            pltpu.SMEM(fold_map.shape, jnp.int32),
            scratch((rows // LANES, held * width, LANES), F32),
            dma((CUTS + 5,)),
        ],
        compiler_params=limit(14),
        name="prepare",
    )(
        far(fold_map), far(state.transpose(2, 1, 0)), far(ocean_mask.T),
        far(b_first[None]), far(b_second[None]), far(w_first),
    )
    inner = lax.ppermute(inner, "lon", [(i, i ^ 1) for i in range(n)])

    before = BEFORE
    hid_a, last_a, wt, w_second = pl.pallas_call(
        inside_a,
        out_shape=(
            shape((before, rows, hidden), BF),
            shape((8, hidden), F32),
            shape((5 * SLOT, 3 * hidden), BF),
            shape(w_second.shape, BF),
        ),
        in_specs=[vmem] * 3 + [hbm],
        out_specs=(vmem,) * 4,
        scratch_shapes=[dma],
        compiler_params=limit(12),
        name="inside_a",
    )(cols, w_first, bias, far(w_second))

    def stage_b(after):
        return pl.pallas_call(
            functools.partial(inside_b, before),
            out_shape=(
                shape((width - 2 - before, rows, hidden), BF),
                shape((8, hidden), F32),
                shape((4, rows, hidden), F32),
            ),
            in_specs=[vmem] * 5,
            out_specs=(vmem,) * 3,
            compiler_params=limit(12),
            name="inside_b",
        )(cols, w_first, bias, wt, after)

    field = shape((hidden // LANES, rows * width, LANES), F32)

    def stage_c(hid_b, after):
        return pl.pallas_call(
            functools.partial(inside_c, chans),
            out_shape=field,
            in_specs=[vmem] * 6,
            out_specs=vmem,
            compiler_params=limit(12),
            name="inside_c",
        )(hid_a, hid_b, cols, w_second, bias, after)

    pair = shape((2, 2 * width, WIDE), BF)
    tops, sent = pl.pallas_call(
        join_first,
        out_shape=(pair, shape(sent.shape, BF)),
        in_specs=[vmem] * 4,
        out_specs=(vmem,) * 2,
        input_output_aliases={3: 1},
        compiler_params=limit(4),
        name="join_first",
    )(top, inner, last_a, sent)
    step = 2
    while step < n // 2:
        got = lax.ppermute(tops, "lon", [(i, i ^ step) for i in range(n)])
        if step == 2:
            outer = lax.ppermute(sent, "lon", [(i, (i + 1 if i % 2 else i - 1) % n) for i in range(n)])
        if step == n // 4:
            hid_b, last_b, part_b = stage_b(tops)
            outp = stage_c(hid_b, tops)
            break
        tops = pl.pallas_call(
            join,
            out_shape=shape((2 * tops.shape[0],) + tops.shape[1:], BF),
            in_specs=[vmem] * 2,
            out_specs=vmem,
            compiler_params=limit(4),
            name="join",
        )(tops, got)
        step *= 2
    lines = shape((32, WIDE), BF)
    give, keep = pl.pallas_call(
        choose,
        out_shape=(lines, lines),
        in_specs=[vmem] * 4,
        out_specs=(vmem,) * 2,
        compiler_params=limit(4),
        name="choose",
    )(pick, tops, got, outp)
    got = lax.ppermute(give, "lon", [(i, i ^ (n // 2)) for i in range(n)])
    outf, line, own = pl.pallas_call(
        border,
        out_shape=(field, shape((16, hidden), F32), shape((24, WIDE), F32)),
        in_specs=[vmem] * 12,
        out_specs=(vmem,) * 3,
        scratch_shapes=[scratch((2, rows, 2 * MAIN + LANES), BF), scratch((4, rows, hidden), BF)],
        compiler_params=limit(14),
        name="border",
    )(cols, outer, inner, part_b, last_a, last_b, outp, wt, w_first, bias, w_second, give)
    return pl.pallas_call(
        finish,
        out_shape=shape((rows, width, hidden), BF),
        in_specs=[vmem] * 11,
        out_specs=hbm,
        scratch_shapes=[scratch((24, WIDE), F32)] * 4
        + [scratch((24, hidden), F32)] * 2
        + [scratch((rows, width, hidden), BF), dma((PIECES + 1,))],
        compiler_params=limit(14),
        name="finish",
    )(keep, got, top, outp, outf, line, own, wt, w_first, bias, w_second)


def solution(mesh):
    return jax.shard_map(
        local,
        mesh=mesh,
        in_specs=(P(None, ("grp", "lon"), None), P(None, "lon"), P(), P(), P(), P(), P()),
        out_specs=P(None, ("grp", "lon"), None),
        check_vma=False,
    )
```

```python
import functools

import jax
import jax.numpy as jnp
from jax import lax
from jax.experimental import pallas as pl
from jax.experimental.pallas import tpu as pltpu
from jax.sharding import PartitionSpec as P

BF, F32 = jnp.bfloat16, jnp.float32
LANES, MAIN, SLOT, PIECES, CUTS = 128, 256, 64, 4, 4
GROUP, BEFORE = 2, 3
WIDE = MAIN + 2 * SLOT


def gelu(value):
    return half_gelu(value, 0.5)


def half_gelu(value, half):
    inner = value * (0.7978845608 + (0.7978845608 * 0.044715) * (value * value))
    scaled = value * half
    return scaled + scaled * jnp.tanh(inner)


def turned(block):
    rows = block.shape[-1]
    tail = block[MAIN : MAIN + SLOT]
    tail = jnp.concatenate([tail, jnp.zeros((SLOT - tail.shape[0], rows), BF)], axis=0)
    full = jnp.concatenate([block[:MAIN], tail, tail], axis=0)
    eye = (
        lax.broadcasted_iota(jnp.int32, (rows, rows), 0) == lax.broadcasted_iota(jnp.int32, (rows, rows), 1)
    ).astype(F32).astype(BF)
    return lax.dot_general(eye, full, (((1,), (1,)), ((), ())), preferred_element_type=F32)


def prepare(
    fold_hbm, x_hbm, mask_hbm, b1_hbm, b2_hbm, w1_hbm,
    outer_ref, inner_ref, cols_ref, top_ref, bias_ref, pick_ref, w1_ref,
    x_ref, mask_ref, fold_ref, field, sem,
):
    chans, width, rows = x_ref.shape
    held = field.shape[1] // width
    me = lax.axis_index("lon")
    halves = [slice(i * LANES, (i + 1) * LANES) for i in range(rows // LANES)]
    parts = CUTS // len(halves)
    cuts = [chans * i // parts for i in range(parts + 1)]
    spans = [(i, at, lo, hi) for i, at in enumerate(halves) for lo, hi in zip(cuts, cuts[1:])]
    pairs = [(mask_hbm, mask_ref)]
    pairs += [(x_hbm.at[lo:hi, :, at], x_ref.at[lo:hi, :, at]) for _, at, lo, hi in spans]
    pairs += [(b1_hbm, bias_ref.at[0:1]), (b2_hbm, bias_ref.at[1:2]), (fold_hbm, fold_ref)]
    pairs += [(w1_hbm, w1_ref)]
    copies = [pltpu.make_async_copy(src, dst, sem.at[i]) for i, (src, dst) in enumerate(pairs)]
    for copy in copies:
        copy.start()
    odd = lax.rem(me, 2) == 1
    copies[3 + CUTS].wait()
    total = fold_ref.shape[0]
    n = total // width
    index = lax.broadcasted_iota(jnp.int32, pick_ref.shape, 0)
    j, line = index & 15, lax.shift_right_logical(index, 4) & 1
    dev = jnp.where(index < 32, lax.bitwise_xor(me, n // 2), me)
    col = fold_ref[0] - width * dev + 2 - j
    col = jnp.where(col < 0, col + total, col)
    col = jnp.where(col < 0, col + total, col)
    col = jnp.where(col >= total, col - total, col)
    block = lax.bitwise_xor(lax.shift_right_logical(col, width.bit_length() - 1), me)
    spot = block * (2 * width) + line * width + (col & (width - 1))
    pick_ref[...] = jnp.where((block < n // 2) & (j < width + 4), spot, -1)
    copies[0].wait()
    mask = mask_ref[...].astype(F32)
    last = []
    for (i, at, lo, hi), copy in zip(spans, copies[1:]):
        copy.wait()
        block = x_ref[lo:hi, :, at].astype(F32) * mask[None, :, at]
        field[i, lo * width : hi * width, :] = block.reshape((hi - lo) * width, LANES)
        if hi < chans:
            continue
        field[i, chans * width : (chans + 1) * width, :] = mask[:, at]
        field[i, (chans + 1) * width :, :] = jnp.zeros(((held - chans - 1) * width, LANES), F32)
    for i, at in enumerate(halves):
        for c in range(width):
            out = turned(field[i, pl.ds(c, held, stride=width), :].astype(BF))
            cols_ref[c, at] = out.astype(BF)
            if at.stop == rows:
                last.append(out[LANES - 2 :])
    lanes = lax.broadcasted_iota(jnp.int32, (rows, LANES), 1)

    def message(c):
        first, second = cols_ref[c], cols_ref[c + 1]
        rest = jnp.where(lanes < SLOT, first[:, MAIN:][:, :LANES], second[:, MAIN:][:, :LANES])
        return jnp.concatenate([first[:, :MAIN], second[:, :MAIN], rest], axis=1)

    low, high = message(0), message(width - 2)
    outer_ref[...] = jnp.where(odd, high, low)
    inner_ref[:rows] = jnp.where(odd, low, high)
    top = jnp.concatenate([v[i : i + 1] for i in range(2) for v in last], axis=0).astype(BF)
    top_ref[0] = top
    inner_ref[rows:] = jnp.concatenate([top, jnp.zeros((2 * width, inner_ref.shape[1] - WIDE), BF)], axis=1)
    for k, copy in enumerate(copies[1 + CUTS :]):
        if k != 2:
            copy.wait()


def join_first(mine_ref, got_ref, after_ref, sent_ref, out_ref, pass_ref):
    out_ref[0] = mine_ref[0]
    out_ref[1] = got_ref[got_ref.shape[0] - mine_ref.shape[1] :, :WIDE]


def join(mine_ref, got_ref, out_ref):
    count = mine_ref.shape[0]
    out_ref[:count] = mine_ref[...]
    out_ref[count:] = got_ref[...]


def choose(pick_ref, mine_ref, got_ref, after_ref, give_ref, keep_ref):
    count, lines, wide = mine_ref.shape
    blocks = jnp.concatenate([ref[...].reshape(count * lines, wide) for ref in (mine_ref, got_ref)], axis=0)
    lane = lax.broadcasted_iota(jnp.int32, (pick_ref.shape[0], blocks.shape[0]), 1)
    out = mm((pick_ref[:, :1] == lane).astype(F32).astype(BF), blocks).astype(BF)
    give_ref[...] = out[:32]
    keep_ref[...] = out[32:]


def mm(a, b):
    return jnp.dot(a, b, preferred_element_type=F32)


def mask_of(column, chans):
    return column[:, MAIN:].astype(F32)[:, chans - MAIN : chans - MAIN + 1]


def tail_weights(w1_ref, wt):
    chans, hidden = w1_ref.shape[2:]
    for dy in range(3):
        for dx in range(3):
            rest = jnp.concatenate(
                [w1_ref[dy, dx, MAIN:, :], jnp.zeros((SLOT - chans + MAIN, hidden), BF)], axis=0
            )
            wt[(dx + 1) * SLOT : (dx + 2) * SLOT, dy * hidden : (dy + 1) * hidden] = rest
    for at in (0, 4 * SLOT):
        wt[at : at + SLOT, :] = jnp.zeros((SLOT, 3 * hidden), BF)


def first_taps(columns):
    some = next(c for c in columns if c is not None)
    lanes = lax.broadcasted_iota(jnp.int32, (some.shape[0], LANES), 1)
    zero = jnp.zeros((some.shape[0], LANES), BF)
    tail = [zero if c is None else c[:, MAIN:] for c in columns]
    parts = [c[:, :MAIN] for c in columns if c is not None]
    if columns[0] is not None or columns[1] is not None:
        parts.append(jnp.where(lanes < SLOT, tail[0], tail[1]))
    if columns[2] is not None:
        parts.append(tail[2])
    return jnp.concatenate(parts, axis=1)


def first_weights(w1_ref, wt, columns, dys=(0, 1, 2)):
    hidden = w1_ref.shape[3]
    out = []
    for dy in dys:
        at = slice(dy * hidden, (dy + 1) * hidden)
        parts = [w1_ref[dy, dx, :MAIN, :] for dx in range(3) if columns[dx] is not None]
        if columns[0] is not None or columns[1] is not None:
            parts.append(wt[SLOT : 3 * SLOT, at])
        if columns[2] is not None:
            parts.append(wt[3 * SLOT :, at])
        out.append(jnp.concatenate(parts, axis=0))
    return jnp.concatenate(out, axis=1)


def second_weights(w2_ref, columns, dys=(0, 1, 2)):
    return jnp.concatenate(
        [
            jnp.concatenate([w2_ref[dy, dx] for dx in range(3) if columns[dx] is not None], axis=0)
            for dy in dys
        ],
        axis=1,
    )


def last_out(value):
    row = lax.broadcasted_iota(jnp.int32, (8, value.shape[1]), 0)
    return jnp.concatenate([value[:-8], jnp.where(row == 7, 0.0, value[-8:])], axis=0)


def summed(p):
    rows, hidden = p.shape[0], p.shape[1] // 3
    row = lax.broadcasted_iota(jnp.int32, (8, hidden), 0)
    south = pltpu.roll(p[:, :hidden], 1, 0)
    south = jnp.concatenate([jnp.where(row == 0, 0.0, south[:8]), south[8:]], axis=0)
    return p[:, hidden : 2 * hidden] + south + last_out(pltpu.roll(p[:, 2 * hidden :], rows - 1, 0))


def edges(width):
    return (0, 1, width, width + 1)


def own_column(cols_ref, j):
    return cols_ref[j - 2] if 2 <= j < 2 + cols_ref.shape[0] else None


def hidden_columns(cols_ref, w1_ref, bias_ref, wt, hid_ref, last_ref, first, part_ref, more):
    chans, _ = w1_ref.shape[2:]
    rows = cols_ref.shape[1]
    last_ref[...] = jnp.zeros_like(last_ref)
    for i in range(0, hid_ref.shape[0], GROUP):
        group = range(min(GROUP, hid_ref.shape[0] - i))
        sets = [[own_column(cols_ref, first + i + g + dx) for dx in range(3)] for g in group]
        lhs = jnp.concatenate([first_taps(columns) for columns in sets], axis=0)
        out = mm(lhs, first_weights(w1_ref, wt, sets[0]))
        for g in group:
            value = summed(out[g * rows : (g + 1) * rows])
            last_ref[i + g : i + g + 1, :] = value[rows - 1 :]
            value = half_gelu(value + bias_ref[0:1], 0.5 * mask_of(sets[g][1], chans))
            hid_ref[i + g] = last_out(value).astype(BF)
    for i, h in enumerate(more):
        columns = [own_column(cols_ref, h + dx) for dx in range(3)]
        part_ref[i] = summed(mm(first_taps(columns), first_weights(w1_ref, wt, columns)))


def inside_a(cols_ref, w1_ref, bias_ref, w2_hbm, hid_ref, last_ref, wt_ref, w2_ref, sem):
    copy = pltpu.make_async_copy(w2_hbm, w2_ref, sem)
    copy.start()
    tail_weights(w1_ref, wt_ref)
    hidden_columns(cols_ref, w1_ref, bias_ref, wt_ref, hid_ref, last_ref, 2, None, ())
    copy.wait()


def inside_b(before, cols_ref, w1_ref, bias_ref, wt_ref, after_ref, hid_ref, last_ref, part_ref):
    width = cols_ref.shape[0]
    hidden_columns(cols_ref, w1_ref, bias_ref, wt_ref, hid_ref, last_ref, 2 + before, part_ref, edges(width))


def second_columns(chans, todo, hid_a, hid_b, cols_ref, w2_ref, bias_ref, out_ref):
    width, rows, _ = cols_ref.shape
    hidden = w2_ref.shape[3]
    before = hid_a.shape[0]

    def hid(h):
        if not 2 <= h < width:
            return None
        return hid_a[h - 2] if h - 2 < before else hid_b[h - 2 - before]

    def put(o, value):
        for i in range(hidden // LANES):
            out_ref[i, pl.ds(o, rows, stride=width), :] = value[:, i * LANES : (i + 1) * LANES]

    def lhs(columns):
        return jnp.concatenate([c for c in columns if c is not None], axis=1)

    for group in todo:
        sets = [[hid(o + dx) for dx in range(3)] for o in group]
        out = mm(jnp.concatenate([lhs(c) for c in sets], axis=0), second_weights(w2_ref, sets[0]))
        for g, o in enumerate(group):
            value = summed(out[g * rows : (g + 1) * rows]) + bias_ref[1:2]
            if 2 <= o < width - 2:
                value = value * mask_of(cols_ref[o], chans)
            put(o, value)


def inside_c(chans, hid_a, hid_b, cols_ref, w2_ref, bias_ref, after_ref, out_ref):
    width = cols_ref.shape[0]
    todo = ((2, 3), (4, 5), (0,), (1,), (width - 2,), (width - 1,))
    second_columns(chans, todo, hid_a, hid_b, cols_ref, w2_ref, bias_ref, out_ref)


def border(
    cols_ref, outer_ref, inner_ref, part_ref, last_a, last_b, outp_ref, wt, w1_ref, bias_ref, w2_ref, after_ref,
    outf, line, own, hx, hid,
):
    chans, hidden = w1_ref.shape[2:]
    width, rows, _ = cols_ref.shape
    rest = 2 * MAIN
    odd = lax.rem(lax.axis_index("lon"), 2) == 1
    bias1 = bias_ref[0:1]
    outer, inner = outer_ref[...], inner_ref[:rows]
    hx[0] = jnp.where(odd, inner, outer)
    hx[1] = jnp.where(odd, outer, inner)

    at = edges(width)
    taken = (
        (0, slice(0, rest), (0, 1), 1),
        (0, slice(MAIN, rest), (0,), 0),
        (1, slice(0, MAIN), (2,), 3),
        (1, slice(0, rest), (1, 2), 2),
    )
    line[...] = jnp.zeros_like(line)
    line[2 : 2 + BEFORE] = last_a[:BEFORE]
    line[2 + BEFORE : width] = last_b[: width - 2 - BEFORE]
    for i, (side, main, dxs, slot) in enumerate(taken):
        lhs = jnp.concatenate([hx[side, :, main], hx[side, :, rest:]], axis=1)
        rhs = []
        for dy in range(3):
            block = wt[slot * SLOT : (slot + 2) * SLOT, dy * hidden : (dy + 1) * hidden]
            rhs.append(jnp.concatenate([w1_ref[dy, dx, :MAIN, :] for dx in dxs] + [block], axis=0))
        value = part_ref[i] + summed(mm(lhs, jnp.concatenate(rhs, axis=1)))
        line[at[i] : at[i] + 1, :] = value[rows - 1 :]
        sea = chans - MAIN
        if i == 0:
            mask = hx[0, :, rest:].astype(F32)[:, SLOT + sea : SLOT + sea + 1]
        elif i == 3:
            mask = hx[1, :, rest:].astype(F32)[:, sea : sea + 1]
        else:
            mask = mask_of(cols_ref[at[i] - 1], chans)
        hid[i] = last_out(half_gelu(value + bias1, 0.5 * mask)).astype(BF)

    for o in (0, 1, width - 2, width - 1):
        columns = [hid[at.index(o + dx)] if o + dx in at else None for dx in range(3)]
        have = [c for c in columns if c is not None]
        value = summed(mm(jnp.concatenate(have, axis=1), second_weights(w2_ref, columns)))
        mask = mask_of(cols_ref[o], chans)
        for i in range(hidden // LANES):
            to = (i, pl.ds(o, rows, stride=width), slice(None))
            outf[to] = (outp_ref[to] + value[:, i * LANES : (i + 1) * LANES]) * mask
    own[...] = jnp.zeros_like(own)
    for j in range(width):
        own[2 + j : 3 + j, :] = cols_ref[j, rows - 16 :].astype(F32)[15:16]
    half = lax.broadcasted_iota(jnp.int32, (8, LANES), 1) < SLOT
    for side, first in ((0, 0), (1, 2 + width)):
        end = hx[side, rows - 16 :].astype(F32)[8:16]
        tail = end[:, rest:]
        turn = pltpu.roll(tail, SLOT, 1)
        for c, both_halves in enumerate((jnp.where(half, tail, turn), jnp.where(half, turn, tail))):
            full = jnp.concatenate([end[:, c * MAIN : (c + 1) * MAIN], both_halves], axis=1)
            own[first + c : first + c + 1, :] = full[7:8]


def finish(
    keep_ref, got_ref, top_ref, outp_ref, outf, line, own, wt, w1_ref, bias_ref, w2_ref,
    out_hbm, m0, m1, r2, gs, hg, hz, outb, sem,
):
    chans, hidden = w1_ref.shape[2:]
    rows, width, _ = out_hbm.shape
    bias1 = bias_ref[0:1]
    ends = [rows * p // PIECES for p in range(PIECES)] + [rows - 8, rows]
    copies = []

    def assemble(p, more):
        lo, hi = ends[p], ends[p + 1]
        here, lines = slice(lo, hi), slice(lo * width, hi * width)
        place = lax.rem(lax.broadcasted_iota(jnp.int32, ((hi - lo) * width, LANES), 0), width)
        edge = (place < 2) | (place >= width - 2)
        for i in range(hidden // LANES):
            lanes = slice(i * LANES, (i + 1) * LANES)
            value = jnp.where(edge, outf[i, lines], outp_ref[i, lines])
            if more is not None:
                end = (hi - lo - 2) * width
                value = jnp.concatenate([value[:end], value[end:] + more[:, lanes]], axis=0)
            outb[here, :, lanes] = value.reshape(hi - lo, width, LANES).astype(BF)

    def send(p):
        here = slice(ends[p], ends[p + 1])
        copies.append(pltpu.make_async_copy(outb.at[here], out_hbm.at[here], sem.at[p]))
        copies[-1].start()

    assemble(0, None)
    send(0)
    assemble(1, None)
    send(1)
    assemble(2, None)
    send(2)
    lane = lax.broadcasted_iota(jnp.int32, (1, WIDE), 1)
    sign = jnp.where(lane < chans // 2, -1.0, 1.0).astype(F32)
    both = keep_ref[...].astype(F32) + got_ref[...].astype(F32)
    for ref, value in ((m0, both[:16]), (m1, both[16:]), (gs, both[16:] * sign)):
        ref[:16] = value
        ref[16:] = jnp.zeros_like(ref[16:])
    r2[...] = own[...] * sign

    def taps(ref, offsets):
        return first_taps([ref[o : o + 16, :].astype(BF) for o in offsets])

    every = (0, 0, 0)
    mixed = mm(
        jnp.concatenate([taps(gs, (0, 1, 2)), taps(r2, (2, 1, 0))], axis=0), first_weights(w1_ref, wt, every, (2,))
    )
    pre = mixed[16:]
    pre += mm(taps(m0, (2, 1, 0)), first_weights(w1_ref, wt, every, (0,)))
    pre += mm(taps(m1, (2, 1, 0)), first_weights(w1_ref, wt, every, (1,)))
    hg[16:] = jnp.zeros_like(hg[16:])
    hg[:16] = gelu(pre + bias1) * m1[1:17, chans : chans + 1]
    hz[16:] = jnp.zeros_like(hz[16:])
    hz[:16] = gelu(line[...] + mixed[:16] + bias1) * own[1:17, chans : chans + 1]
    assemble(3, None)
    send(3)
    wide = [jnp.concatenate([ref[o : o + 16, :].astype(BF) for o in range(3)], axis=1) for ref in (hz, hg)]
    more = mm(jnp.concatenate(wide, axis=0), second_weights(w2_ref, every, (1, 2)))
    below = more[:width, hidden:]
    level = more[:width, :hidden] + more[16 : 16 + width, hidden:]
    fixed = jnp.concatenate([below, level], axis=0) * mask_of(top_ref[0], chans)

    assemble(PIECES, fixed)
    send(PIECES)
    for copy in copies:
        copy.wait()


def local(state, ocean_mask, fold_map, w_first, b_first, w_second, b_second):
    rows, width, chans = state.shape
    hidden = w_first.shape[-1]
    n = lax.axis_size("lon")
    assert n >= 8 and n & (n - 1) == 0 and MAIN <= chans < MAIN + SLOT and chans // 2 <= MAIN and width == 8 and rows == MAIN
    held = -(-(chans + 1) // 16) * 16
    vmem = pl.BlockSpec(memory_space=pltpu.VMEM)
    hbm = pl.BlockSpec(memory_space=pltpu.MemorySpace.HBM)
    shape = jax.ShapeDtypeStruct
    scratch = pltpu.VMEM
    dma = pltpu.SemaphoreType.DMA

    def limit(mib):
        return pltpu.CompilerParams(vmem_limit_bytes=mib << 20)

    def far(value):
        return pltpu.with_memory_space_constraint(value, pltpu.MemorySpace.HBM)

    sent, inner, cols, top, bias, pick, w_first = pl.pallas_call(
        prepare,
        out_shape=(
            shape((rows, 2 * MAIN + LANES), BF),
            shape((rows + 2 * width, 2 * MAIN + LANES), BF),
            shape((width, rows, WIDE), BF),
            shape((1, 2 * width, WIDE), BF),
            shape((2, hidden), F32),
            shape((64, LANES), jnp.int32),
            shape(w_first.shape, BF),
        ),
        in_specs=[hbm] * 6,
        out_specs=(vmem,) * 7,
        scratch_shapes=[
            scratch((chans, width, rows), BF),
            scratch((width, rows), jnp.int32),
            pltpu.SMEM(fold_map.shape, jnp.int32),
            scratch((rows // LANES, held * width, LANES), F32),
            dma((CUTS + 5,)),
        ],
        compiler_params=limit(14),
        name="prepare",
    )(
        far(fold_map), far(state.transpose(2, 1, 0)), far(ocean_mask.T),
        far(b_first[None]), far(b_second[None]), far(w_first),
    )
    inner = lax.ppermute(inner, "lon", [(i, i ^ 1) for i in range(n)])

    before = BEFORE
    hid_a, last_a, wt, w_second = pl.pallas_call(
        inside_a,
        out_shape=(
            shape((before, rows, hidden), BF),
            shape((8, hidden), F32),
            shape((5 * SLOT, 3 * hidden), BF),
            shape(w_second.shape, BF),
        ),
        in_specs=[vmem] * 3 + [hbm],
        out_specs=(vmem,) * 4,
        scratch_shapes=[dma],
        compiler_params=limit(12),
        name="inside_a",
    )(cols, w_first, bias, far(w_second))

    def stage_b(after):
        return pl.pallas_call(
            functools.partial(inside_b, before),
            out_shape=(
                shape((width - 2 - before, rows, hidden), BF),
                shape((8, hidden), F32),
                shape((4, rows, hidden), F32),
            ),
            in_specs=[vmem] * 5,
            out_specs=(vmem,) * 3,
            compiler_params=limit(12),
            name="inside_b",
        )(cols, w_first, bias, wt, after)

    field = shape((hidden // LANES, rows * width, LANES), F32)

    def stage_c(hid_b, after):
        return pl.pallas_call(
            functools.partial(inside_c, chans),
            out_shape=field,
            in_specs=[vmem] * 6,
            out_specs=vmem,
            compiler_params=limit(12),
            name="inside_c",
        )(hid_a, hid_b, cols, w_second, bias, after)

    pair = shape((2, 2 * width, WIDE), BF)
    tops, sent = pl.pallas_call(
        join_first,
        out_shape=(pair, shape(sent.shape, BF)),
        in_specs=[vmem] * 4,
        out_specs=(vmem,) * 2,
        input_output_aliases={3: 1},
        compiler_params=limit(4),
        name="join_first",
    )(top, inner, last_a, sent)
    step = 2
    while step < n // 2:
        got = lax.ppermute(tops, "lon", [(i, i ^ step) for i in range(n)])
        if step == 2:
            outer = lax.ppermute(sent, "lon", [(i, (i + 1 if i % 2 else i - 1) % n) for i in range(n)])
        if step == n // 4:
            hid_b, last_b, part_b = stage_b(tops)
            outp = stage_c(hid_b, tops)
            break
        tops = pl.pallas_call(
            join,
            out_shape=shape((2 * tops.shape[0],) + tops.shape[1:], BF),
            in_specs=[vmem] * 2,
            out_specs=vmem,
            compiler_params=limit(4),
            name="join",
        )(tops, got)
        step *= 2
    lines = shape((32, WIDE), BF)
    give, keep = pl.pallas_call(
        choose,
        out_shape=(lines, lines),
        in_specs=[vmem] * 4,
        out_specs=(vmem,) * 2,
        compiler_params=limit(4),
        name="choose",
    )(pick, tops, got, outp)
    got = lax.ppermute(give, "lon", [(i, i ^ (n // 2)) for i in range(n)])
    outf, line, own = pl.pallas_call(
        border,
        out_shape=(field, shape((16, hidden), F32), shape((24, WIDE), F32)),
        in_specs=[vmem] * 12,
        out_specs=(vmem,) * 3,
        scratch_shapes=[scratch((2, rows, 2 * MAIN + LANES), BF), scratch((4, rows, hidden), BF)],
        compiler_params=limit(14),
        name="border",
    )(cols, outer, inner, part_b, last_a, last_b, outp, wt, w_first, bias, w_second, give)
    return pl.pallas_call(
        finish,
        out_shape=shape((rows, width, hidden), BF),
        in_specs=[vmem] * 11,
        out_specs=hbm,
        scratch_shapes=[scratch((24, WIDE), F32)] * 4
        + [scratch((24, hidden), F32)] * 2
        + [scratch((rows, width, hidden), BF), dma((PIECES + 1,))],
        compiler_params=limit(14),
        name="finish",
    )(keep, got, top, outp, outf, line, own, wt, w_first, bias, w_second)


def solution(mesh):
    return jax.shard_map(
        local,
        mesh=mesh,
        in_specs=(P(None, ("grp", "lon"), None), P(None, "lon"), P(), P(), P(), P(), P()),
        out_specs=P(None, ("grp", "lon"), None),
        check_vma=False,
    )
```

```python
import functools

import jax
import jax.numpy as jnp
from jax import lax
from jax.experimental import pallas as pl
from jax.experimental.pallas import tpu as pltpu
from jax.sharding import PartitionSpec as P

BF, F32 = jnp.bfloat16, jnp.float32
LANES, MAIN, SLOT, PIECES, CUTS = 128, 256, 64, 4, 4
GROUP, BEFORE = 2, 3
WIDE = MAIN + 2 * SLOT


def gelu(value):
    return half_gelu(value, 0.5)


def half_gelu(value, half):
    inner = value * (0.7978845608 + (0.7978845608 * 0.044715) * (value * value))
    scaled = value * half
    return scaled + scaled * jnp.tanh(inner)


def turned(block):
    rows = block.shape[-1]
    tail = block[MAIN : MAIN + SLOT]
    tail = jnp.concatenate([tail, jnp.zeros((SLOT - tail.shape[0], rows), BF)], axis=0)
    full = jnp.concatenate([block[:MAIN], tail, tail], axis=0)
    eye = (
        lax.broadcasted_iota(jnp.int32, (rows, rows), 0) == lax.broadcasted_iota(jnp.int32, (rows, rows), 1)
    ).astype(F32).astype(BF)
    return lax.dot_general(eye, full, (((1,), (1,)), ((), ())), preferred_element_type=F32)


def prepare(
    fold_hbm, x_hbm, mask_hbm, b1_hbm, b2_hbm, w1_hbm,
    outer_ref, inner_ref, cols_ref, top_ref, bias_ref, pick_ref, w1_ref,
    x_ref, mask_ref, fold_ref, field, sem,
):
    chans, width, rows = x_ref.shape
    held = field.shape[1] // width
    me = lax.axis_index("lon")
    halves = [slice(i * LANES, (i + 1) * LANES) for i in range(rows // LANES)]
    parts = CUTS // len(halves)
    cuts = [chans * i // parts for i in range(parts + 1)]
    spans = [(i, at, lo, hi) for i, at in enumerate(halves) for lo, hi in zip(cuts, cuts[1:])]
    pairs = [(mask_hbm, mask_ref)]
    pairs += [(x_hbm.at[lo:hi, :, at], x_ref.at[lo:hi, :, at]) for _, at, lo, hi in spans]
    pairs += [(b1_hbm, bias_ref.at[0:1]), (b2_hbm, bias_ref.at[1:2]), (fold_hbm, fold_ref)]
    pairs += [(w1_hbm, w1_ref)]
    copies = [pltpu.make_async_copy(src, dst, sem.at[i]) for i, (src, dst) in enumerate(pairs)]
    for copy in copies:
        copy.start()
    odd = lax.rem(me, 2) == 1
    copies[3 + CUTS].wait()
    total = fold_ref.shape[0]
    n = total // width
    index = lax.broadcasted_iota(jnp.int32, pick_ref.shape, 0)
    j, line = index & 15, lax.shift_right_logical(index, 4) & 1
    dev = jnp.where(index < 32, lax.bitwise_xor(me, n // 2), me)
    col = fold_ref[0] - width * dev + 2 - j
    col = jnp.where(col < 0, col + total, col)
    col = jnp.where(col < 0, col + total, col)
    col = jnp.where(col >= total, col - total, col)
    block = lax.bitwise_xor(lax.shift_right_logical(col, width.bit_length() - 1), me)
    spot = block * (2 * width) + line * width + (col & (width - 1))
    pick_ref[...] = jnp.where((block < n // 2) & (j < width + 4), spot, -1)
    copies[0].wait()
    mask = mask_ref[...].astype(F32)
    last = []
    for (i, at, lo, hi), copy in zip(spans, copies[1:]):
        copy.wait()
        block = x_ref[lo:hi, :, at].astype(F32) * mask[None, :, at]
        field[i, lo * width : hi * width, :] = block.reshape((hi - lo) * width, LANES)
        if hi < chans:
            continue
        field[i, chans * width : (chans + 1) * width, :] = mask[:, at]
        field[i, (chans + 1) * width :, :] = jnp.zeros(((held - chans - 1) * width, LANES), F32)
    for i, at in enumerate(halves):
        for c in range(width):
            out = turned(field[i, pl.ds(c, held, stride=width), :].astype(BF))
            cols_ref[c, at] = out.astype(BF)
            if at.stop == rows:
                last.append(out[LANES - 2 :])
    lanes = lax.broadcasted_iota(jnp.int32, (rows, LANES), 1)

    def message(c):
        first, second = cols_ref[c], cols_ref[c + 1]
        rest = jnp.where(lanes < SLOT, first[:, MAIN:][:, :LANES], second[:, MAIN:][:, :LANES])
        return jnp.concatenate([first[:, :MAIN], second[:, :MAIN], rest], axis=1)

    low, high = message(0), message(width - 2)
    outer_ref[...] = jnp.where(odd, high, low)
    inner_ref[:rows] = jnp.where(odd, low, high)
    top = jnp.concatenate([v[i : i + 1] for i in range(2) for v in last], axis=0).astype(BF)
    top_ref[0] = top
    inner_ref[rows:] = jnp.concatenate([top, jnp.zeros((2 * width, inner_ref.shape[1] - WIDE), BF)], axis=1)
    for k, copy in enumerate(copies[1 + CUTS :]):
        if k != 2:
            copy.wait()


def join_first(mine_ref, got_ref, after_ref, sent_ref, out_ref, pass_ref):
    out_ref[0] = mine_ref[0]
    out_ref[1] = got_ref[got_ref.shape[0] - mine_ref.shape[1] :, :WIDE]


def join(mine_ref, got_ref, out_ref):
    count = mine_ref.shape[0]
    out_ref[:count] = mine_ref[...]
    out_ref[count:] = got_ref[...]


def choose(pick_ref, mine_ref, got_ref, after_ref, give_ref, keep_ref):
    count, lines, wide = mine_ref.shape
    blocks = jnp.concatenate([ref[...].reshape(count * lines, wide) for ref in (mine_ref, got_ref)], axis=0)
    lane = lax.broadcasted_iota(jnp.int32, (pick_ref.shape[0], blocks.shape[0]), 1)
    out = mm((pick_ref[:, :1] == lane).astype(F32).astype(BF), blocks).astype(BF)
    give_ref[...] = out[:32]
    keep_ref[...] = out[32:]


def mm(a, b):
    return jnp.dot(a, b, preferred_element_type=F32)


def mask_of(column, chans):
    return column[:, MAIN:].astype(F32)[:, chans - MAIN : chans - MAIN + 1]


def tail_weights(w1_ref, wt):
    chans, hidden = w1_ref.shape[2:]
    for dy in range(3):
        for dx in range(3):
            rest = jnp.concatenate(
                [w1_ref[dy, dx, MAIN:, :], jnp.zeros((SLOT - chans + MAIN, hidden), BF)], axis=0
            )
            wt[(dx + 1) * SLOT : (dx + 2) * SLOT, dy * hidden : (dy + 1) * hidden] = rest
    wt[5 * SLOT : 6 * SLOT, :] = wt[2 * SLOT : 3 * SLOT, :]
    wt[6 * SLOT :, :] = wt[SLOT : 2 * SLOT, :]
    for at in (0, 4 * SLOT):
        wt[at : at + SLOT, :] = jnp.zeros((SLOT, 3 * hidden), BF)


def first_taps(columns):
    some = next(c for c in columns if c is not None)
    lanes = lax.broadcasted_iota(jnp.int32, (some.shape[0], LANES), 1)
    zero = jnp.zeros((some.shape[0], LANES), BF)
    tail = [zero if c is None else c[:, MAIN:] for c in columns]
    parts = [c[:, :MAIN] for c in columns if c is not None]
    if columns[0] is not None or columns[1] is not None:
        parts.append(jnp.where(lanes < SLOT, tail[0], tail[1]))
    if columns[2] is not None:
        parts.append(tail[2])
    return jnp.concatenate(parts, axis=1)


def first_weights(w1_ref, wt, columns, dys=(0, 1, 2)):
    hidden = w1_ref.shape[3]
    out = []
    for dy in dys:
        at = slice(dy * hidden, (dy + 1) * hidden)
        parts = [w1_ref[dy, dx, :MAIN, :] for dx in range(3) if columns[dx] is not None]
        if columns[0] is not None or columns[1] is not None:
            parts.append(wt[SLOT : 3 * SLOT, at])
        if columns[2] is not None:
            parts.append(wt[3 * SLOT : 5 * SLOT, at])
        out.append(jnp.concatenate(parts, axis=0))
    return jnp.concatenate(out, axis=1)


def second_weights(w2_ref, columns, dys=(0, 1, 2)):
    return jnp.concatenate(
        [
            jnp.concatenate([w2_ref[dy, dx] for dx in range(3) if columns[dx] is not None], axis=0)
            for dy in dys
        ],
        axis=1,
    )


def last_out(value):
    row = lax.broadcasted_iota(jnp.int32, (8, value.shape[1]), 0)
    return jnp.concatenate([value[:-8], jnp.where(row == 7, 0.0, value[-8:])], axis=0)


def summed(p):
    rows, hidden = p.shape[0], p.shape[1] // 3
    row = lax.broadcasted_iota(jnp.int32, (8, hidden), 0)
    south = pltpu.roll(p[:, :hidden], 1, 0)
    south = jnp.concatenate([jnp.where(row == 0, 0.0, south[:8]), south[8:]], axis=0)
    return p[:, hidden : 2 * hidden] + south + last_out(pltpu.roll(p[:, 2 * hidden :], rows - 1, 0))


def edges(width):
    return (0, 1, width, width + 1)


def own_column(cols_ref, j):
    return cols_ref[j - 2] if 2 <= j < 2 + cols_ref.shape[0] else None


def hidden_columns(cols_ref, w1_ref, bias_ref, wt, hid_ref, last_ref, first, part_ref, more):
    chans, _ = w1_ref.shape[2:]
    rows = cols_ref.shape[1]
    last_ref[...] = jnp.zeros_like(last_ref)
    for i in range(0, hid_ref.shape[0], GROUP):
        group = range(min(GROUP, hid_ref.shape[0] - i))
        sets = [[own_column(cols_ref, first + i + g + dx) for dx in range(3)] for g in group]
        lhs = jnp.concatenate([first_taps(columns) for columns in sets], axis=0)
        out = mm(lhs, first_weights(w1_ref, wt, sets[0]))
        for g in group:
            value = summed(out[g * rows : (g + 1) * rows])
            last_ref[i + g : i + g + 1, :] = value[rows - 1 :]
            value = half_gelu(value + bias_ref[0:1], 0.5 * mask_of(sets[g][1], chans))
            hid_ref[i + g] = last_out(value).astype(BF)
    for i, h in enumerate(more):
        columns = [own_column(cols_ref, h + dx) for dx in range(3)]
        lhs, rhs = first_taps(columns), first_weights(w1_ref, wt, columns)
        if h == 1:
            lhs = jnp.concatenate([lhs[:, : 2 * MAIN], lhs[:, 2 * MAIN + LANES :]], axis=1)
            rhs = jnp.concatenate([rhs[: 2 * MAIN], rhs[2 * MAIN + LANES :]], axis=0)
        part_ref[i] = summed(mm(lhs, rhs))


def inside_a(cols_ref, w1_ref, bias_ref, w2_hbm, hid_ref, last_ref, wt_ref, w2_ref, sem):
    copy = pltpu.make_async_copy(w2_hbm, w2_ref, sem)
    copy.start()
    tail_weights(w1_ref, wt_ref)
    hidden_columns(cols_ref, w1_ref, bias_ref, wt_ref, hid_ref, last_ref, 2, None, ())
    copy.wait()


def inside_b(before, cols_ref, w1_ref, bias_ref, wt_ref, after_ref, hid_ref, last_ref, part_ref):
    width = cols_ref.shape[0]
    hidden_columns(cols_ref, w1_ref, bias_ref, wt_ref, hid_ref, last_ref, 2 + before, part_ref, edges(width))


def second_columns(chans, todo, hid_a, hid_b, cols_ref, w2_ref, bias_ref, out_ref):
    width, rows, _ = cols_ref.shape
    hidden = w2_ref.shape[3]
    before = hid_a.shape[0]

    def hid(h):
        if not 2 <= h < width:
            return None
        return hid_a[h - 2] if h - 2 < before else hid_b[h - 2 - before]

    def put(o, value):
        for i in range(hidden // LANES):
            out_ref[i, pl.ds(o, rows, stride=width), :] = value[:, i * LANES : (i + 1) * LANES]

    def lhs(columns):
        return jnp.concatenate([c for c in columns if c is not None], axis=1)

    for group in todo:
        sets = [[hid(o + dx) for dx in range(3)] for o in group]
        out = mm(jnp.concatenate([lhs(c) for c in sets], axis=0), second_weights(w2_ref, sets[0]))
        for g, o in enumerate(group):
            value = summed(out[g * rows : (g + 1) * rows]) + bias_ref[1:2]
            if 2 <= o < width - 2:
                value = value * mask_of(cols_ref[o], chans)
            put(o, value)


def inside_c(chans, hid_a, hid_b, cols_ref, w2_ref, bias_ref, after_ref, out_ref):
    width = cols_ref.shape[0]
    todo = ((2, 3), (4, 5), (0,), (1,), (width - 2,), (width - 1,))
    second_columns(chans, todo, hid_a, hid_b, cols_ref, w2_ref, bias_ref, out_ref)


def border(
    cols_ref, outer_ref, inner_ref, part_ref, last_a, last_b, outp_ref, wt, w1_ref, bias_ref, w2_ref, after_ref,
    outf, line, own, hx, hid,
):
    chans, hidden = w1_ref.shape[2:]
    width, rows, _ = cols_ref.shape
    rest = 2 * MAIN
    odd = lax.rem(lax.axis_index("lon"), 2) == 1
    bias1 = bias_ref[0:1]
    outer, inner = outer_ref[...], inner_ref[:rows]
    hx[0] = jnp.where(odd, inner, outer)
    hx[1] = jnp.where(odd, outer, inner)

    at = edges(width)
    taken = (
        (0, slice(0, rest), (0, 1), 1),
        (0, slice(MAIN, rest), (0,), 5),
        (1, slice(0, MAIN), (2,), 3),
        (1, slice(0, rest), (1, 2), 2),
    )
    line[...] = jnp.zeros_like(line)
    line[2 : 2 + BEFORE] = last_a[:BEFORE]
    line[2 + BEFORE : width] = last_b[: width - 2 - BEFORE]
    for i, (side, main, dxs, slot) in enumerate(taken):
        tail = hx[side, :, rest:]
        if i == 1:
            lanes = lax.broadcasted_iota(jnp.int32, tail.shape, 1)
            tail = jnp.where(lanes < SLOT, cols_ref[0, :, MAIN:], tail)
        lhs = jnp.concatenate([hx[side, :, main], tail], axis=1)
        rhs = []
        for dy in range(3):
            block = wt[slot * SLOT : (slot + 2) * SLOT, dy * hidden : (dy + 1) * hidden]
            rhs.append(jnp.concatenate([w1_ref[dy, dx, :MAIN, :] for dx in dxs] + [block], axis=0))
        value = part_ref[i] + summed(mm(lhs, jnp.concatenate(rhs, axis=1)))
        line[at[i] : at[i] + 1, :] = value[rows - 1 :]
        sea = chans - MAIN
        if i == 0:
            mask = hx[0, :, rest:].astype(F32)[:, SLOT + sea : SLOT + sea + 1]
        elif i == 3:
            mask = hx[1, :, rest:].astype(F32)[:, sea : sea + 1]
        else:
            mask = mask_of(cols_ref[at[i] - 1], chans)
        hid[i] = last_out(half_gelu(value + bias1, 0.5 * mask)).astype(BF)

    for o in (0, 1, width - 2, width - 1):
        columns = [hid[at.index(o + dx)] if o + dx in at else None for dx in range(3)]
        have = [c for c in columns if c is not None]
        value = summed(mm(jnp.concatenate(have, axis=1), second_weights(w2_ref, columns)))
        mask = mask_of(cols_ref[o], chans)
        for i in range(hidden // LANES):
            to = (i, pl.ds(o, rows, stride=width), slice(None))
            outf[to] = (outp_ref[to] + value[:, i * LANES : (i + 1) * LANES]) * mask
    own[...] = jnp.zeros_like(own)
    for j in range(width):
        own[2 + j : 3 + j, :] = cols_ref[j, rows - 16 :].astype(F32)[15:16]
    half = lax.broadcasted_iota(jnp.int32, (8, LANES), 1) < SLOT
    for side, first in ((0, 0), (1, 2 + width)):
        end = hx[side, rows - 16 :].astype(F32)[8:16]
        tail = end[:, rest:]
        turn = pltpu.roll(tail, SLOT, 1)
        for c, both_halves in enumerate((jnp.where(half, tail, turn), jnp.where(half, turn, tail))):
            full = jnp.concatenate([end[:, c * MAIN : (c + 1) * MAIN], both_halves], axis=1)
            own[first + c : first + c + 1, :] = full[7:8]


def finish(
    keep_ref, got_ref, top_ref, outp_ref, outf, line, own, wt, w1_ref, bias_ref, w2_ref,
    out_hbm, m0, m1, r2, gs, hg, hz, outb, sem,
):
    chans, hidden = w1_ref.shape[2:]
    rows, width, _ = out_hbm.shape
    bias1 = bias_ref[0:1]
    ends = [rows * p // PIECES for p in range(PIECES)] + [rows - 8, rows]
    copies = []

    def assemble(p, more):
        lo, hi = ends[p], ends[p + 1]
        here, lines = slice(lo, hi), slice(lo * width, hi * width)
        place = lax.rem(lax.broadcasted_iota(jnp.int32, ((hi - lo) * width, LANES), 0), width)
        edge = (place < 2) | (place >= width - 2)
        for i in range(hidden // LANES):
            lanes = slice(i * LANES, (i + 1) * LANES)
            value = jnp.where(edge, outf[i, lines], outp_ref[i, lines])
            if more is not None:
                end = (hi - lo - 2) * width
                value = jnp.concatenate([value[:end], value[end:] + more[:, lanes]], axis=0)
            outb[here, :, lanes] = value.reshape(hi - lo, width, LANES).astype(BF)
        copies.append(pltpu.make_async_copy(outb.at[here], out_hbm.at[here], sem.at[p]))
        copies[-1].start()

    for p in range(PIECES):
        assemble(p, None)
    lane = lax.broadcasted_iota(jnp.int32, (1, WIDE), 1)
    sign = jnp.where(lane < chans // 2, -1.0, 1.0).astype(F32)
    both = keep_ref[...].astype(F32) + got_ref[...].astype(F32)
    for ref, value in ((m0, both[:16]), (m1, both[16:]), (gs, both[16:] * sign)):
        ref[:16] = value
        ref[16:] = jnp.zeros_like(ref[16:])
    r2[...] = own[...] * sign

    def taps(ref, offsets):
        return first_taps([ref[o : o + 16, :].astype(BF) for o in offsets])

    every = (0, 0, 0)
    mixed = mm(
        jnp.concatenate([taps(gs, (0, 1, 2)), taps(r2, (2, 1, 0))], axis=0), first_weights(w1_ref, wt, every, (2,))
    )
    pre = mixed[16:]
    pre += mm(taps(m0, (2, 1, 0)), first_weights(w1_ref, wt, every, (0,)))
    pre += mm(taps(m1, (2, 1, 0)), first_weights(w1_ref, wt, every, (1,)))
    hg[16:] = jnp.zeros_like(hg[16:])
    hg[:16] = gelu(pre + bias1) * m1[1:17, chans : chans + 1]
    hz[16:] = jnp.zeros_like(hz[16:])
    hz[:16] = gelu(line[...] + mixed[:16] + bias1) * own[1:17, chans : chans + 1]
    wide = [jnp.concatenate([ref[o : o + 16, :].astype(BF) for o in range(3)], axis=1) for ref in (hz, hg)]
    more = mm(jnp.concatenate(wide, axis=0), second_weights(w2_ref, every, (1, 2)))
    below = more[:width, hidden:]
    level = more[:width, :hidden] + more[16 : 16 + width, hidden:]
    fixed = jnp.concatenate([below, level], axis=0) * mask_of(top_ref[0], chans)

    assemble(PIECES, fixed)
    for copy in copies:
        copy.wait()


def local(state, ocean_mask, fold_map, w_first, b_first, w_second, b_second):
    rows, width, chans = state.shape
    hidden = w_first.shape[-1]
    n = lax.axis_size("lon")
    assert n >= 8 and n & (n - 1) == 0 and MAIN <= chans < MAIN + SLOT and chans // 2 <= MAIN and width == 8 and rows == MAIN
    held = -(-(chans + 1) // 16) * 16
    vmem = pl.BlockSpec(memory_space=pltpu.VMEM)
    hbm = pl.BlockSpec(memory_space=pltpu.MemorySpace.HBM)
    shape = jax.ShapeDtypeStruct
    scratch = pltpu.VMEM
    dma = pltpu.SemaphoreType.DMA

    def limit(mib):
        return pltpu.CompilerParams(vmem_limit_bytes=mib << 20)

    def far(value):
        return pltpu.with_memory_space_constraint(value, pltpu.MemorySpace.HBM)

    sent, inner, cols, top, bias, pick, w_first = pl.pallas_call(
        prepare,
        out_shape=(
            shape((rows, 2 * MAIN + LANES), BF),
            shape((rows + 2 * width, 2 * MAIN + LANES), BF),
            shape((width, rows, WIDE), BF),
            shape((1, 2 * width, WIDE), BF),
            shape((2, hidden), F32),
            shape((64, LANES), jnp.int32),
            shape(w_first.shape, BF),
        ),
        in_specs=[hbm] * 6,
        out_specs=(vmem,) * 7,
        scratch_shapes=[
            scratch((chans, width, rows), BF),
            scratch((width, rows), jnp.int32),
            pltpu.SMEM(fold_map.shape, jnp.int32),
            scratch((rows // LANES, held * width, LANES), F32),
            dma((CUTS + 5,)),
        ],
        compiler_params=limit(14),
        name="prepare",
    )(
        far(fold_map), far(state.transpose(2, 1, 0)), far(ocean_mask.T),
        far(b_first[None]), far(b_second[None]), far(w_first),
    )
    inner = lax.ppermute(inner, "lon", [(i, i ^ 1) for i in range(n)])

    before = BEFORE
    hid_a, last_a, wt, w_second = pl.pallas_call(
        inside_a,
        out_shape=(
            shape((before, rows, hidden), BF),
            shape((8, hidden), F32),
            shape((7 * SLOT, 3 * hidden), BF),
            shape(w_second.shape, BF),
        ),
        in_specs=[vmem] * 3 + [hbm],
        out_specs=(vmem,) * 4,
        scratch_shapes=[dma],
        compiler_params=limit(12),
        name="inside_a",
    )(cols, w_first, bias, far(w_second))

    def stage_b(after):
        return pl.pallas_call(
            functools.partial(inside_b, before),
            out_shape=(
                shape((width - 2 - before, rows, hidden), BF),
                shape((8, hidden), F32),
                shape((4, rows, hidden), F32),
            ),
            in_specs=[vmem] * 5,
            out_specs=(vmem,) * 3,
            compiler_params=limit(12),
            name="inside_b",
        )(cols, w_first, bias, wt, after)

    field = shape((hidden // LANES, rows * width, LANES), F32)

    def stage_c(hid_b, after):
        return pl.pallas_call(
            functools.partial(inside_c, chans),
            out_shape=field,
            in_specs=[vmem] * 6,
            out_specs=vmem,
            compiler_params=limit(12),
            name="inside_c",
        )(hid_a, hid_b, cols, w_second, bias, after)

    pair = shape((2, 2 * width, WIDE), BF)
    tops, sent = pl.pallas_call(
        join_first,
        out_shape=(pair, shape(sent.shape, BF)),
        in_specs=[vmem] * 4,
        out_specs=(vmem,) * 2,
        input_output_aliases={3: 1},
        compiler_params=limit(4),
        name="join_first",
    )(top, inner, last_a, sent)
    step = 2
    while step < n // 2:
        got = lax.ppermute(tops, "lon", [(i, i ^ step) for i in range(n)])
        if step == 2:
            outer = lax.ppermute(sent, "lon", [(i, (i + 1 if i % 2 else i - 1) % n) for i in range(n)])
        if step == n // 4:
            hid_b, last_b, part_b = stage_b(tops)
            outp = stage_c(hid_b, tops)
            break
        tops = pl.pallas_call(
            join,
            out_shape=shape((2 * tops.shape[0],) + tops.shape[1:], BF),
            in_specs=[vmem] * 2,
            out_specs=vmem,
            compiler_params=limit(4),
            name="join",
        )(tops, got)
        step *= 2
    lines = shape((32, WIDE), BF)
    give, keep = pl.pallas_call(
        choose,
        out_shape=(lines, lines),
        in_specs=[vmem] * 4,
        out_specs=(vmem,) * 2,
        compiler_params=limit(4),
        name="choose",
    )(pick, tops, got, outp)
    got = lax.ppermute(give, "lon", [(i, i ^ (n // 2)) for i in range(n)])
    outf, line, own = pl.pallas_call(
        border,
        out_shape=(field, shape((16, hidden), F32), shape((24, WIDE), F32)),
        in_specs=[vmem] * 12,
        out_specs=(vmem,) * 3,
        scratch_shapes=[scratch((2, rows, 2 * MAIN + LANES), BF), scratch((4, rows, hidden), BF)],
        compiler_params=limit(14),
        name="border",
    )(cols, outer, inner, part_b, last_a, last_b, outp, wt, w_first, bias, w_second, give)
    return pl.pallas_call(
        finish,
        out_shape=shape((rows, width, hidden), BF),
        in_specs=[vmem] * 11,
        out_specs=hbm,
        scratch_shapes=[scratch((24, WIDE), F32)] * 4
        + [scratch((24, hidden), F32)] * 2
        + [scratch((rows, width, hidden), BF), dma((PIECES + 1,))],
        compiler_params=limit(14),
        name="finish",
    )(keep, got, top, outp, outf, line, own, wt, w_first, bias, w_second)


def solution(mesh):
    return jax.shard_map(
        local,
        mesh=mesh,
        in_specs=(P(None, ("grp", "lon"), None), P(None, "lon"), P(), P(), P(), P(), P()),
        out_specs=P(None, ("grp", "lon"), None),
        check_vma=False,
    )
```
